32 devices in a mesh: gx: 2 (over x), gy: 4 (over y, core), gz: 4 (over z).
Axes of the slice: x: 2, y: 2, z: 4, core: 2. Of those that a mesh axis runs over, the one named last changes fastest.
Arguments:
- solid_state: float32 [9, 32, 16, 512], P(None, 'gz', 'gx', 'gy'), may hold values from -6 to 6
- material: float32 [4, 32, 16, 512], P(None, 'gz', 'gx', 'gy'), may hold values from 0.5 to 2
- ocean_state: float32 [4, 16, 32, 1024], P(None, None, 'gx', ('gy', 'gz')), may hold values from -6 to 6
- ocean_medium: float32 [2, 16], replicated, may hold values from 0.5 to 2
- offset_x: int32 [32], P('gx'), may hold values from -1 to 1
- offset_y: int32 [1024], P(('gy', 'gz')), may hold values from -1 to 1
Outputs:
- solid_next: float32 [9, 32, 16, 512], P(None, 'gz', 'gx', 'gy')
- solid_rate: float32 [9, 32, 16, 512], P(None, 'gz', 'gx', 'gy')
- ocean_next: float32 [4, 16, 32, 1024], P(None, None, 'gx', ('gy', 'gz'))
- ocean_rate: float32 [4, 16, 32, 1024], P(None, None, 'gx', ('gy', 'gz'))
The draws below stay inside these ranges and needn't reach their ends.
All inputs are finite; a program needn't handle non-finite values.
Results may differ from the reference program's by a relative error of at most 0.000059.
Values sent between devices are 32-bit elements; how exact they have to be, the bound alone decides.
No kernel may reach another device: no remote copies, remote signals or barrier semaphores. Data moves between devices by JAX's collectives and lax.ppermute only.
A program may use at most 64 MiB of HBM per device.

```python
import math
import jax
import jax.numpy as jnp
from jax import lax

OZ = 16
NX = 16
NY = 512
NZ = 32
FX = 32
FY = 1024


def plant(array, rng, least, top_value):
    place = [jax.random.randint(jax.random.fold_in(rng, axis), (), 0, length) for axis, length in enumerate(array.shape)]
    widest = array.shape.index(max(array.shape))
    beside = place[:widest] + [(place[widest] + 1) % array.shape[widest]] + place[widest + 1:]
    return array.at[tuple(place)].set(least).at[tuple(beside)].set(top_value)


def shard_levels(own_key, shape, shards, smallest, top_value):
    def one(axis_at, parts):
        draws = jax.random.uniform(jax.random.fold_in(jax.random.fold_in(own_key, 6), axis_at), (parts,), jnp.float32, smallest / len(shards), top_value / len(shards))
        return jnp.repeat(jnp.exp(draws), shape[axis_at] // parts).reshape((-1,) + (1,) * (len(shape) - axis_at - 1))

    loudness = one(*shards[0])
    for cut in shards[1:]:
        loudness = loudness * one(*cut)
    return loudness


def bell_draw(rng, dims, width, limit, cuts=(), held_as=jnp.bfloat16):
    drawn = jax.random.normal(rng, dims, jnp.float32) * width
    if len(cuts) > 0:
        drawn = shard_levels(rng, dims, cuts, -0.22, 0.18) * drawn
    return jnp.clip(drawn, min=-limit, max=limit).astype(held_as)


def setup_inputs(seed: int = 0) -> dict:
    keys = jax.random.split(jax.random.key(seed), 7)
    solid_state = bell_draw(keys[0], (9, NZ, NX, NY), 1.0, 6.0, ((1, 4), (2, 2), (3, 4)), jnp.float32)
    material = jnp.clip(jnp.exp(math.log(2.0) - 1.3862944 * jax.random.uniform(keys[1], (4, NZ, NX, NY), jnp.float32) ** shard_levels(keys[1], (4, NZ, NX, NY), ((1, 4), (2, 2), (3, 4)), -0.2, 0.2)), 0.5, 2.0)
    ocean_state = bell_draw(keys[2], (4, OZ, FX, FY), 1.0, 6.0, ((2, 2), (3, 16)), jnp.float32)
    ocean_medium = jnp.clip(jnp.exp(jax.random.uniform(keys[3], (2, OZ), jnp.float32, math.log(0.5), math.log(2.0))), 0.5, 2.0)
    offset_x = plant(jax.random.randint(keys[4], (FX,), -1, 2), jax.random.fold_in(keys[4], 1), -1, 1).astype(jnp.int32)
    offset_y = plant(jax.random.randint(keys[5], (FY,), -1, 2), jax.random.fold_in(keys[5], 1), -1, 1).astype(jnp.int32)
    return dict(solid_state=solid_state, material=material, ocean_state=ocean_state, ocean_medium=ocean_medium, offset_x=offset_x, offset_y=offset_y)


closure_rows = ((-24.0 / 17.0, 59.0 / 34.0, -4.0 / 17.0, -3.0 / 34.0, 0.0, 0.0),
                (-0.5, 0.0, 0.5, 0.0, 0.0, 0.0),
                (4.0 / 43.0, -59.0 / 86.0, 0.0, 59.0 / 86.0, -4.0 / 43.0, 0.0),
                (3.0 / 98.0, 0.0, -59.0 / 98.0, 0.0, 32.0 / 49.0, -4.0 / 49.0))
inv_norm = 48.0 / 17.0
step_size = 0.25
section_weight = 0.1496590219993
gravity = 0.4


def take_slab(field, first_index, length, dimension):
    return lax.slice_in_dim(field, first_index, first_index + length, axis=dimension)


def closure(field, dimension, at_end):
    extent = field.shape[dimension]
    pieces = []
    for row_index in range(4):
        running = jnp.zeros_like(take_slab(field, 0, 1, dimension))
        for col_index in range(6):
            weight = closure_rows[row_index][col_index]
            if weight != 0.0:
                if at_end:
                    running = running - weight * take_slab(field, extent - 1 - col_index, 1, dimension)
                else:
                    running = running + weight * take_slab(field, col_index, 1, dimension)
        pieces.append(running)
    if at_end:
        pieces = pieces[::-1]
    return jnp.concatenate(pieces, axis=dimension)


def interior(padded, dimension, extent):
    return (take_slab(padded, 0, extent, dimension) - 8.0 * take_slab(padded, 1, extent, dimension)
            + 8.0 * take_slab(padded, 3, extent, dimension) - take_slab(padded, 4, extent, dimension)) / 12.0


def derivative(field, dimension):
    extent = field.shape[dimension]
    widths = [(0, 0)] * field.ndim
    widths[dimension] = (2, 2)
    middle = interior(jnp.pad(field, widths), dimension, extent)
    return jnp.concatenate([closure(field, dimension, False), take_slab(middle, 4, extent - 8, dimension),
                            closure(field, dimension, True)], axis=dimension)


def blend_matrix(offsets, fine_first, coarse_first, columns, coarse_total):
    fine_index = fine_first + jnp.arange(offsets.shape[0], dtype=jnp.int32)
    coarse = fine_index // 2
    target = jnp.clip(coarse + offsets, 0, coarse_total - 1)
    column = jnp.arange(columns, dtype=jnp.int32)[None, :]
    nearest = (column == (coarse - coarse_first)[:, None]).astype(jnp.float32)
    farther = (column == (target - coarse_first)[:, None]).astype(jnp.float32)
    return 0.75 * nearest + 0.25 * farther


def restrict(bottom):
    fine_rows, fine_cols = bottom.shape
    return bottom.reshape(fine_rows // 2, 2, fine_cols // 2, 2).mean(axis=(1, 3))


def solid_rates(material, diff_x, diff_y, diff_z):
    buoyancy = material[0]
    lame_one = material[1]
    lame_two = material[2]
    metric = material[3]

    def vertical(member):
        return metric * diff_z(member)

    strain_xx = diff_x(0)
    strain_yy = diff_y(1)
    strain_zz = vertical(2)
    dilation = strain_xx + strain_yy + strain_zz
    return [buoyancy * (diff_x(3) + diff_y(8) + vertical(7)),
            buoyancy * (diff_x(8) + diff_y(4) + vertical(6)),
            buoyancy * (diff_x(7) + diff_y(6) + vertical(5)),
            lame_one * dilation + 2.0 * lame_two * strain_xx,
            lame_one * dilation + 2.0 * lame_two * strain_yy,
            lame_one * dilation + 2.0 * lame_two * strain_zz,
            lame_two * (vertical(1) + diff_y(2)),
            lame_two * (vertical(0) + diff_x(2)),
            lame_two * (diff_y(0) + diff_x(1))]


def seafloor_terms(state, material, bed_pressure):
    factor = inv_norm * material[0, 0] * material[3, 0]
    return factor * state[7, 0], factor * state[6, 0], factor * (state[5, 0] + bed_pressure)


def ocean_rates(state, medium, diff_x, diff_y, bed_speed):
    bulk = medium[0][:, None, None]
    light = medium[1][:, None, None]
    pressure = state[0]
    flow_z = state[3]
    rate_p = -bulk * (2.0 * diff_x(1) + 2.0 * diff_y(2) + derivative(flow_z, 0)) + gravity * flow_z / light
    rate_p = rate_p.at[-1].add(inv_norm * bulk[-1] * (flow_z[-1] - bed_speed))
    rate_u = -2.0 * light * diff_x(0)
    rate_v = -2.0 * light * diff_y(0)
    rate_w = -light * derivative(pressure, 0)
    rate_w = rate_w.at[0].add(-inv_norm * light[0] * pressure[0])
    return jnp.stack([rate_p, rate_u, rate_v, rate_w])


def reference(solid_state, material, ocean_state, ocean_medium, offset_x, offset_y):
    highest = lax.Precision.HIGHEST
    plane = solid_state[2, 0]
    blend_x = blend_matrix(offset_x, 0, 0, NX, NX)
    blend_y = blend_matrix(offset_y, 0, 0, NY, NY)
    bed_speed = jnp.dot(jnp.dot(blend_x, plane, precision=highest), blend_y.T, precision=highest)
    bed_pressure = restrict(ocean_state[0, -1])
    rates = solid_rates(material,
                        lambda member: derivative(solid_state[member], 1),
                        lambda member: derivative(solid_state[member], 2),
                        lambda member: derivative(solid_state[member], 0))
    term_x, term_y, term_z = seafloor_terms(solid_state, material, bed_pressure)
    rates[0] = rates[0].at[0].add(term_x)
    rates[1] = rates[1].at[0].add(term_y)
    rates[2] = rates[2].at[0].add(term_z)
    solid_rate = step_size * jnp.stack(rates)
    solid_next = solid_state + section_weight * solid_rate
    ocean_rate = step_size * ocean_rates(ocean_state, ocean_medium,
                                         lambda member: derivative(ocean_state[member], 1),
                                         lambda member: derivative(ocean_state[member], 2),
                                         bed_speed)
    ocean_next = ocean_state + section_weight * ocean_rate
    return solid_next, solid_rate, ocean_next, ocean_rate
```

```python
import functools

import jax
import jax.numpy as jnp
from jax import lax
from jax.experimental import pallas as pl
from jax.experimental.pallas import tpu as pltpu
from jax.sharding import PartitionSpec as P

closure_rows = (
    (-24.0 / 17.0, 59.0 / 34.0, -4.0 / 17.0, -3.0 / 34.0, 0.0, 0.0),
    (-0.5, 0.0, 0.5, 0.0, 0.0, 0.0),
    (4.0 / 43.0, -59.0 / 86.0, 0.0, 59.0 / 86.0, -4.0 / 43.0, 0.0),
    (3.0 / 98.0, 0.0, -59.0 / 98.0, 0.0, 32.0 / 49.0, -4.0 / 49.0),
)
inv_norm = 48.0 / 17.0
step_size = 0.25
section_weight = 0.1496590219993
gravity = 0.4
interior_weights = {-2: 1.0 / 12.0, -1: -8.0 / 12.0, 1: 8.0 / 12.0, 2: -1.0 / 12.0}

x_fields = (0, 1, 2, 3, 8, 7)
y_fields = (0, 1, 2, 4, 8, 6)
z_fields = (0, 1, 2, 5, 6, 7)
ocean_x_fields = (1, 0)
ocean_y_fields = (2, 0)
rows, lanes, half = 8, 128, 64
far = 1 << 20


def turn(x, shift, axis):
    shift = shift % x.shape[axis]
    return x if shift == 0 else pltpu.roll(x, shift, axis)


def flag(value, shape=(rows, lanes)):
    return jnp.broadcast_to(value.astype(jnp.int32), shape) == 1


def lane_of(shape=(rows, lanes)):
    return lax.broadcasted_iota(jnp.int32, shape, 1)


def row_of(shape=(rows, lanes)):
    return lax.broadcasted_iota(jnp.int32, shape, 0)


def stencil(position, extent, first, last):
    low = position + far * (1 - first)
    high = extent - 1 - position + far * (1 - last)
    plain = jnp.logical_and(low >= 4, high >= 4)
    weights = {}
    for s in range(-3, 4):
        inside = jnp.logical_and(position + s >= 0, position + s < extent)
        w = jnp.where(jnp.logical_and(inside, plain), interior_weights.get(s, 0.0), 0.0)
        for r in range(4):
            if 0 <= r + s < 6 and closure_rows[r][r + s] != 0.0:
                w = jnp.where(low == r, closure_rows[r][r + s], w)
            if 0 <= r - s < 6 and closure_rows[r][r - s] != 0.0:
                w = jnp.where(high == r, -closure_rows[r][r - s], w)
        weights[s] = w
    return weights


def slope(x, weights, axis):
    total = weights[0] * x
    for s in (-3, -2, -1, 1, 2, 3):
        total = total + weights[s] * turn(x, -s, axis)
    return total


def pack_edges(tiles):
    group = lax.shift_right_logical(lane_of(), 2)
    out = []
    for start in range(0, len(tiles), 32):
        acc = jnp.zeros((rows, lanes), jnp.float32)
        for q, tile in enumerate(tiles[start : start + 32]):
            acc = jnp.where(group == q, turn(tile, 4 * q + 2, 1), acc)
        out.append(acc)
    return out


def edge_terms(left, right, has_left, has_right):
    place = jnp.bitwise_and(lane_of(), 3)
    low = jnp.where(
        place == 2, turn(left, 2, 1) - 8.0 * turn(left, 1, 1), turn(left, 2, 1)
    )
    high = jnp.where(
        place == 0, -turn(right, -2, 1), 8.0 * turn(right, -1, 1) - turn(right, -2, 1)
    )
    low = jnp.where(has_left, low, 0.0)
    high = jnp.where(has_right, high, 0.0)
    return jnp.where(place >= 2, low, high) * (1.0 / 12.0)


def row_terms(pack, from_low):
    even = jnp.bitwise_and(row_of(), 1) == 0
    low = jnp.where(even, pack - 8.0 * turn(pack, -1, 0), pack)
    high = jnp.where(even, -pack, 8.0 * turn(pack, 1, 0) - pack)
    return jnp.where(from_low, low, turn(high, 6, 0)) * (1.0 / 12.0)


def pair_rounds(size):
    first = [(i, i ^ 1) for i in range(size)]
    if size == 2:
        return (first,)
    second = [(i, (i + 1) % size if i % 2 else (i - 1) % size) for i in range(size)]
    return (first, second)


def where_am_i():
    return lax.axis_index("gx"), lax.axis_index("gy"), lax.axis_index("gz")


def paired_level(ocean, field, k, levels):
    a = ocean[field, k]
    b = ocean[field, k + levels // 2]
    return jnp.concatenate([a, b], axis=1)


def pack_x_kernel(solid, ocean, *outs):
    levels = ocean.shape[1]
    fine = ocean.shape[2]
    depth = solid.shape[1]
    odd = flag(lax.rem(lax.axis_index("gx"), 2))
    pair = lax.shift_right_logical(row_of(), 1)
    heads = []
    for field in x_fields:
        for z in range(depth):
            tile = solid[field, z]
            heads.append((tile, turn(tile, 2, 0)))
    for field in ocean_x_fields:
        for k in range(levels // 2):
            tile = paired_level(ocean, field, k, levels)
            heads.append((tile[:rows], turn(tile[fine - rows :], 2, 0)))
    for number, out in enumerate(outs):
        acc = None
        for t, (head, tail) in enumerate(heads):
            q = t % 4
            edge = jnp.where(odd, head, tail) if number == 0 else jnp.where(odd, tail, head)
            edge = turn(edge, 2 * q, 0)
            acc = edge if q == 0 else jnp.where(pair == q, edge, acc)
            if q == 3:
                out[t // 4] = acc


def row_rims(plane_packs, odd, single):
    if single:
        pack = plane_packs[0]
        return jnp.where(row_of() == 0, turn(pack, -1, 0), turn(pack, 1, 0))
    low = jnp.where(odd, plane_packs[0], plane_packs[1])
    high = jnp.where(odd, plane_packs[1], plane_packs[0])
    return jnp.where(row_of() == 0, turn(low, -1, 0), turn(high, 1, 0))


def pack_rest_kernel(count_x, solid, ocean, *refs):
    packs, (out_y, out_even, out_odd, out_bed, out_own) = refs[:count_x], refs[count_x:]
    levels, fine, width = ocean.shape[1:]
    depth = solid.shape[1]
    x, y, z = where_am_i()
    odd_x = flag(lax.rem(x, 2))
    odd_z = lax.rem(z, 2)
    plane_tile = (x_fields.index(2) * depth) // 4
    rim = row_rims([pack[plane_tile] for pack in packs], odd_x, count_x == 1)
    rim = jnp.where(row_of() < 2, rim, 0.0)
    tiles = [solid[field, k] for field in y_fields for k in range(depth)]
    packed = pack_edges(tiles)
    for i, tile in enumerate(packed):
        out_y[i] = tile
    out_y[len(packed)] = rim

    start_even = (1 - odd_z) * (depth - 2)
    start_odd = odd_z * (depth - 2)
    count = 0
    for field in z_fields:
        for k in range(2):
            out_even[count] = solid[field, start_even + k]
            out_odd[count] = solid[field, start_odd + k]
            count += 1
    outer, inner = [], []
    for field in ocean_y_fields:
        for k in range(levels // 2):
            tile = paired_level(ocean, field, k, levels)
            for r in range(0, fine, rows):
                outer.append(tile[r : r + rows])
                inner.append(turn(tile[r : r + rows], half, 1))
    for tile in pack_edges(outer) + pack_edges(inner):
        out_even[count] = tile
        out_odd[count] = tile
        count += 1

    deepest = ocean[0, levels - 1]
    pick_row = (
        lax.shift_right_logical(lax.broadcasted_iota(jnp.int32, (rows, fine), 1), 1)
        == lax.broadcasted_iota(jnp.int32, (rows, fine), 0)
    ).astype(jnp.float32)
    fine_col = lax.broadcasted_iota(jnp.int32, (width, lanes), 0)
    coarse_col = lax.broadcasted_iota(jnp.int32, (width, lanes), 1)
    pick_col = jnp.where(
        lax.shift_right_logical(fine_col, 1) + z * (width // 2) == coarse_col, 0.25, 0.0
    )
    dot = functools.partial(
        jnp.dot, precision=lax.Precision.HIGHEST, preferred_element_type=jnp.float32
    )
    pressure = dot(dot(pick_row, deepest), pick_col)
    bed = jnp.where(flag((z == 0)), solid[2, 0], pressure)
    for out in (out_even, out_odd):
        out[count] = bed
        out[count + 1] = rim
    out_bed[0] = bed
    out_bed[1] = rim
    out_own[0] = pressure
    out_own[1] = rim


def section_kernel(sizes, solid, material, ocean, medium, offset_x, offset_y, *refs):
    span_x, span_y, span_z = sizes
    count_x = len(pair_rounds(span_x))
    packs = refs[:count_x]
    got_y = refs[count_x : count_x + 2]
    got_ring = refs[count_x + 2 : count_x + 4]
    got_bed = refs[count_x + 4 : count_x + 4 + span_z - 2]
    solid_next, solid_rate, ocean_next, ocean_rate = refs[-5:-1]
    own_bed = refs[count_x + 4 + span_z - 2]
    row_scratch = refs[-1]
    levels, fine, width = ocean.shape[1:]
    depth = solid.shape[1]
    x, y, z = where_am_i()
    one = lambda condition: condition.astype(jnp.int32)
    x_first, x_last = one(x == 0), one(x == span_x - 1)
    y_first, y_last = one(y == 0), one(y == span_y - 1)
    z_first, z_last = one(z == 0), one(z == span_z - 1)
    odd_x, odd_y, odd_z = (flag(lax.rem(i, 2)) for i in (x, y, z))
    lane, row = lane_of(), row_of()

    def sides(got, odd, i):
        if len(got) == 1:
            return got[0][i], got[0][i]
        a, b = got[0][i], got[1][i]
        return jnp.where(odd, a, b), jnp.where(odd, b, a)

    has_low = flag(1 - x_first)
    has_high = flag(1 - x_last)
    pack_tiles = packs[0].shape[0]
    for i in range(pack_tiles):
        low, high = sides(packs, odd_x, i)
        if count_x == 1:
            row_scratch[0, i] = row_terms(low, odd_x)
        else:
            yes = jnp.full((rows, lanes), True)
            row_scratch[0, i] = row_terms(low, yes)
            row_scratch[1, i] = row_terms(high, jnp.logical_not(yes))
    low_rows = jnp.logical_and(row < 2, has_low)
    high_rows = jnp.logical_and(row >= rows - 2, has_high)
    end_rows = jnp.logical_or(low_rows, high_rows)

    def x_terms(t, mask_low, mask_high):
        q = t % 4
        if count_x == 1:
            tile = turn(row_scratch[0, t // 4], -2 * q, 0)
            return jnp.where(jnp.logical_or(mask_low, mask_high), tile, 0.0)
        low = turn(row_scratch[0, t // 4], -2 * q, 0)
        high = turn(row_scratch[1, t // 4], -2 * q, 0)
        return jnp.where(mask_low, low, jnp.where(mask_high, high, 0.0))

    edge_tiles = got_y[0].shape[0] - 1
    y_edges = []
    for i in range(edge_tiles):
        low, high = sides(got_y, odd_y, i)
        y_edges.append(edge_terms(low, high, flag(1 - y_first), flag(1 - y_last)))
    end_lanes = jnp.logical_or(lane < 2, lane >= lanes - 2)

    def y_terms(t):
        return jnp.where(end_lanes, turn(y_edges[t // 32], -(4 * (t % 32) + 2), 1), 0.0)

    weights_x = stencil(row, rows, x_first, x_last)
    weights_y = stencil(lane, lanes, y_first, y_last)
    at_first, at_last = flag(z_first), flag(z_last)
    ring_layers = 2 * len(z_fields)
    span_bed = ring_layers + 4

    def layer(i, k):
        if 0 <= k < depth:
            return solid[z_fields[i], k]
        low, high = sides(got_ring, odd_z, 2 * i + (k + 2 if k < 0 else k - depth))
        return low if k < 0 else high

    def slope_z(i, k):
        total = (
            layer(i, k - 2) - layer(i, k + 2) + 8.0 * (layer(i, k + 1) - layer(i, k - 1))
        ) * (1.0 / 12.0)
        if k < 4:
            near = sum(
                w * layer(i, c) for c, w in enumerate(closure_rows[k]) if w != 0.0
            )
            total = jnp.where(at_first, near, total)
        if depth - 1 - k < 4:
            near = sum(
                -w * layer(i, depth - 1 - c)
                for c, w in enumerate(closure_rows[depth - 1 - k])
                if w != 0.0
            )
            total = jnp.where(at_last, near, total)
        return total

    pressure = own_bed[0] + got_ring[0][span_bed - 2]
    for got in got_bed:
        pressure = pressure + got[0]

    for k in range(depth):
        dx = {
            m: slope(solid[m, k], weights_x, 0) + x_terms(i * depth + k, low_rows, high_rows)
            for i, m in enumerate(x_fields)
        }
        dy = {
            m: slope(solid[m, k], weights_y, 1) + y_terms(i * depth + k)
            for i, m in enumerate(y_fields)
        }
        metric = material[3, k]
        dz = {m: metric * slope_z(i, k) for i, m in enumerate(z_fields)}
        buoyancy, lame_one, lame_two = material[0, k], material[1, k], material[2, k]
        dilation = lame_one * (dx[0] + dy[1] + dz[2])
        twice = 2.0 * lame_two
        rates = [
            buoyancy * (dx[3] + dy[8] + dz[7]),
            buoyancy * (dx[8] + dy[4] + dz[6]),
            buoyancy * (dx[7] + dy[6] + dz[5]),
            dilation + twice * dx[0],
            dilation + twice * dy[1],
            dilation + twice * dz[2],
            lame_two * (dz[1] + dy[2]),
            lame_two * (dz[0] + dx[2]),
            lame_two * (dy[0] + dx[1]),
        ]
        if k == 0:
            factor = jnp.where(at_first, inv_norm * buoyancy * metric, 0.0)
            rates[0] = rates[0] + factor * solid[7, 0]
            rates[1] = rates[1] + factor * solid[6, 0]
            rates[2] = rates[2] + factor * (solid[5, 0] + pressure)
        for m, rate in enumerate(rates):
            rate = step_size * rate
            solid_rate[m, k] = rate
            solid_next[m, k] = solid[m, k] + section_weight * rate

    plane = solid[2, 0]
    rim_tile = own_bed[1]
    for d in range(1, span_z):
        got = got_ring[0] if d == 1 else got_bed[d - 2]
        offset = span_bed - 2 if d == 1 else 0
        here = flag(z == d)
        plane = jnp.where(here, got[offset], plane)
        rim_tile = jnp.where(here, got[offset + 1], rim_tile)
    t = y_fields.index(2) * depth
    left_edge, _ = sides(got_y, odd_y, t // 32)
    left_plane = turn(left_edge, lanes - 1 - (4 * (t % 32) + 1), 1)
    left_rim, _ = sides(got_y, odd_y, edge_tiles)
    _, right_plane = sides(got_ring, odd_z, span_bed - 2)
    _, right_rim = sides(got_ring, odd_z, span_bed - 1)
    beside_plane = jnp.where(lane == 0, right_plane, left_plane)
    beside_rim = jnp.where(lane == 0, right_rim, left_rim)
    dot = functools.partial(
        lax.dot_general,
        precision=lax.Precision.HIGHEST,
        preferred_element_type=jnp.float32,
    )
    fine_row = lax.broadcasted_iota(jnp.int32, (2 * rows, fine), 1)
    source_row = lax.broadcasted_iota(jnp.int32, (2 * rows, fine), 0)
    coarse = lax.shift_right_logical(fine_row, 1)
    low_end = -(x * rows)
    high_end = (span_x - x) * rows - 1
    target = jnp.clip(coarse + offset_x[...], low_end, high_end)
    target = jnp.where(target < 0, rows, jnp.where(target >= rows, rows + 1, target))
    blend_x = 0.75 * (source_row == coarse).astype(jnp.float32) + 0.25 * (
        source_row == target
    ).astype(jnp.float32)
    fine_col = lax.broadcasted_iota(jnp.int32, (lanes, lanes), 1)
    source_col = lax.broadcasted_iota(jnp.int32, (lanes, lanes), 0)
    coarse = lax.shift_right_logical(fine_col - half, 1) + z * (width // 2)
    shift_y = jnp.concatenate([offset_y[...], offset_y[...]], axis=1)
    target = jnp.clip(coarse + shift_y, -(y * lanes), (span_y - y) * lanes - 1)
    upper = fine_col >= half
    weight_near = jnp.where(upper, 0.75, 0.0)
    weight_far = jnp.where(upper, 0.25, 0.0)
    blend_y = jnp.where(source_col == coarse, weight_near, 0.0) + jnp.where(
        source_col == target, weight_far, 0.0
    )
    outside = jnp.logical_or(
        jnp.logical_and(source_col == lanes - 1, target == -1),
        jnp.logical_and(source_col == 0, target == lanes),
    )
    blend_beside = jnp.where(outside, weight_far, 0.0)
    contract_rows = (((0,), (0,)), ((), ()))
    plain = (((1,), (0,)), ((), ()))
    inside_rows = dot(blend_x, jnp.concatenate([plane, rim_tile], axis=0), contract_rows)
    beside_rows = dot(
        blend_x, jnp.concatenate([beside_plane, beside_rim], axis=0), contract_rows
    )
    bed_speed = dot(inside_rows, blend_y, plain) + dot(beside_rows, blend_beside, plain)

    pairs = levels // 2
    wide = (fine, lanes)
    lane2, row2 = lane_of(wide), row_of(wide)
    lower = lane2 < half
    joint_first, joint_last = y_first * z_first, y_last * z_last
    ocean_x = stencil(row2, fine, x_first, x_last)
    ocean_y = stencil(jnp.bitwise_and(lane2, half - 1), half, joint_first, joint_last)
    low_outer, high_outer = sides(got_ring, odd_z, ring_layers)
    low_inner, high_inner = sides(got_ring, odd_z, ring_layers + 1)
    has_left, has_right = flag(1 - joint_first), flag(1 - joint_last)
    outer = edge_terms(low_inner, high_inner, has_left, has_right)
    inner = edge_terms(low_outer, high_outer, has_left, has_right)
    mid_lanes = jnp.logical_and(lane >= half - 2, lane < half + 2)
    never = jnp.full((rows, lanes), False)

    def ocean_x_terms(t):
        low = x_terms(t, low_rows, never)
        high = x_terms(t, never, high_rows)
        middle = [jnp.zeros((fine - 2 * rows, lanes), jnp.float32)] if fine > 2 * rows else []
        return jnp.concatenate([low] + middle + [high], axis=0)

    def ocean_y_terms(t):
        parts = []
        for r in range(fine // rows):
            q = t * (fine // rows) + r
            end = turn(outer, -(4 * q + 2), 1)
            mid = turn(inner, half - (4 * q + 2), 1)
            parts.append(jnp.where(end_lanes, end, jnp.where(mid_lanes, mid, 0.0)))
        return jnp.concatenate(parts, axis=0)

    states = [[paired_level(ocean, m, k, levels) for k in range(pairs)] for m in range(4)]

    def ocean_z(m, k):
        def at(i):
            if 0 <= i < pairs:
                return states[m][i]
            return turn(states[m][i % pairs], half, 1)

        total = (at(k - 2) - at(k + 2) + 8.0 * (at(k + 1) - at(k - 1))) * (1.0 / 12.0)
        if k < 4:
            near = sum(w * at(c) for c, w in enumerate(closure_rows[k]) if w != 0.0)
            total = jnp.where(lower, near, total)
        if pairs - 1 - k < 4:
            near = sum(
                -w * at(pairs - 1 - c)
                for c, w in enumerate(closure_rows[pairs - 1 - k])
                if w != 0.0
            )
            total = jnp.where(lower, total, near)
        return total

    solid_packs = (len(x_fields) * depth) // 4 * 4
    for k in range(pairs):
        bulk = jnp.where(lower, medium[0, k], medium[0, k + pairs])
        light = jnp.where(lower, medium[1, k], medium[1, k + pairs])
        p, u, v, w = (states[m][k] for m in range(4))
        dxu = slope(u, ocean_x, 0) + ocean_x_terms(solid_packs + k)
        dxp = slope(p, ocean_x, 0) + ocean_x_terms(solid_packs + pairs + k)
        dyv = slope(v, ocean_y, 1) + ocean_y_terms(k)
        dyp = slope(p, ocean_y, 1) + ocean_y_terms(pairs + k)
        rate_p = -bulk * (2.0 * (dxu + dyv) + ocean_z(3, k)) + gravity * w / light
        rate_w = -light * ocean_z(0, k)
        if k == pairs - 1:
            rate_p = rate_p + jnp.where(lower, 0.0, inv_norm * bulk * (w - bed_speed))
        if k == 0:
            rate_w = rate_w - jnp.where(lower, inv_norm * light * p, 0.0)
        rates = (rate_p, -2.0 * light * dxp, -2.0 * light * dyp, rate_w)
        for m, rate in enumerate(rates):
            rate = step_size * rate
            after = states[m][k] + section_weight * rate
            ocean_rate[m, k] = rate[:, :half]
            ocean_next[m, k] = after[:, :half]
            ocean_rate[m, k + pairs] = turn(rate, half, 1)[:, :half]
            ocean_next[m, k + pairs] = turn(after, half, 1)[:, :half]


def body(solid_state, material, ocean_state, ocean_medium, offset_x, offset_y):
    sizes = tuple(lax.axis_size(axis) for axis in ("gx", "gy", "gz"))
    span_x, span_y, span_z = sizes
    depth = solid_state.shape[1]
    levels, fine, width = ocean_state.shape[1:]
    if solid_state.shape[2:] != (rows, lanes) or (fine, width) != (2 * rows, half):
        raise ValueError("tile shape")
    if depth % 4 or levels % 2 or span_z & (span_z - 1) or span_x % 2 or span_y % 2:
        raise ValueError("sizes")
    vmem = pl.BlockSpec(memory_space=pltpu.VMEM)
    smem = pl.BlockSpec(memory_space=pltpu.SMEM)
    f32 = jnp.float32
    tiles = lambda n: jax.ShapeDtypeStruct((n, rows, lanes), f32)
    x_rounds = pair_rounds(span_x)
    pack_tiles = (len(x_fields) * depth + len(ocean_x_fields) * levels // 2) // 4
    sent_x = pl.pallas_call(
        pack_x_kernel,
        out_shape=[tiles(pack_tiles) for _ in x_rounds],
        in_specs=[vmem, vmem],
        out_specs=[vmem for _ in x_rounds],
        name="pack_x",
    )(solid_state, ocean_state)
    got_x = [lax.ppermute(m, "gx", pairs) for m, pairs in zip(sent_x, x_rounds)]
    edge_tiles = -(-len(y_fields) * depth // 32)
    ring_tiles = 2 * len(z_fields) + 4
    sent_y, sent_even, sent_odd, sent_bed, own_bed = pl.pallas_call(
        functools.partial(pack_rest_kernel, len(got_x)),
        out_shape=[tiles(edge_tiles + 1), tiles(ring_tiles), tiles(ring_tiles), tiles(2), tiles(2)],
        in_specs=[vmem] * (2 + len(got_x)),
        out_specs=[vmem] * 5,
        name="pack_rest",
    )(solid_state, ocean_state, *got_x)
    y_rounds = pair_rounds(span_y)
    ring = ("gy", "gz")
    ring_rounds = pair_rounds(span_y * span_z)
    got_bed = [
        lax.ppermute(sent_bed, "gz", [(i, i ^ d) for i in range(span_z)])
        for d in range(2, span_z)
    ]
    got_ring = [
        lax.ppermute(m, ring, pairs) for m, pairs in zip((sent_even, sent_odd), ring_rounds)
    ]
    got_y = [lax.ppermute(sent_y, "gy", pairs) for pairs in y_rounds]
    if len(got_y) == 1:
        got_y = got_y * 2
    return pl.pallas_call(
        functools.partial(section_kernel, sizes),
        out_shape=[
            jax.ShapeDtypeStruct(solid_state.shape, f32),
            jax.ShapeDtypeStruct(solid_state.shape, f32),
            jax.ShapeDtypeStruct(ocean_state.shape, f32),
            jax.ShapeDtypeStruct(ocean_state.shape, f32),
        ],
        in_specs=[vmem, vmem, vmem, smem, vmem, vmem]
        + [vmem] * (len(got_x) + 4 + len(got_bed) + 1),
        out_specs=[vmem] * 4,
        scratch_shapes=[pltpu.VMEM((len(got_x), pack_tiles, rows, lanes), f32)],
        name="section",
    )(
        solid_state,
        material,
        ocean_state,
        ocean_medium,
        offset_x.reshape(1, fine),
        offset_y.reshape(1, width),
        *got_x,
        *got_y,
        *got_ring,
        *got_bed,
        own_bed,
    )


def solution(mesh):
    in_specs = (
        P(None, "gz", "gx", "gy"),
        P(None, "gz", "gx", "gy"),
        P(None, None, "gx", ("gy", "gz")),
        P(),
        P("gx"),
        P(("gy", "gz")),
    )
    out_specs = (
        P(None, "gz", "gx", "gy"),
        P(None, "gz", "gx", "gy"),
        P(None, None, "gx", ("gy", "gz")),
        P(None, None, "gx", ("gy", "gz")),
    )
    return jax.shard_map(body, mesh=mesh, in_specs=in_specs, out_specs=out_specs, check_vma=False)
```

```python
import functools

import jax
import jax.numpy as jnp
from jax import lax
from jax.experimental import pallas as pl
from jax.experimental.pallas import tpu as pltpu
from jax.sharding import PartitionSpec as P

closure_rows = (
    (-24.0 / 17.0, 59.0 / 34.0, -4.0 / 17.0, -3.0 / 34.0, 0.0, 0.0),
    (-0.5, 0.0, 0.5, 0.0, 0.0, 0.0),
    (4.0 / 43.0, -59.0 / 86.0, 0.0, 59.0 / 86.0, -4.0 / 43.0, 0.0),
    (3.0 / 98.0, 0.0, -59.0 / 98.0, 0.0, 32.0 / 49.0, -4.0 / 49.0),
)
inv_norm = 48.0 / 17.0
step_size = 0.25
section_weight = 0.1496590219993
gravity = 0.4
interior_weights = {-2: 1.0 / 12.0, -1: -8.0 / 12.0, 1: 8.0 / 12.0, 2: -1.0 / 12.0}

x_fields = (0, 1, 2, 3, 8, 7)
y_fields = (0, 1, 2, 4, 8, 6)
z_fields = (0, 1, 2, 5, 6, 7)
ocean_x_fields = (1, 0)
ocean_y_fields = (2, 0)
rows, lanes, half = 8, 128, 64
far = 1 << 20


def turn(x, shift, axis):
    shift = shift % x.shape[axis]
    return x if shift == 0 else pltpu.roll(x, shift, axis)


def flag(value, shape=(rows, lanes)):
    return jnp.broadcast_to(value.astype(jnp.int32), shape) == 1


def lane_of(shape=(rows, lanes)):
    return lax.broadcasted_iota(jnp.int32, shape, 1)


def row_of(shape=(rows, lanes)):
    return lax.broadcasted_iota(jnp.int32, shape, 0)


def stencil(position, extent, first, last):
    low = position + far * (1 - first)
    high = extent - 1 - position + far * (1 - last)
    plain = jnp.logical_and(low >= 4, high >= 4)
    weights = {}
    for s in range(-3, 4):
        inside = jnp.logical_and(position + s >= 0, position + s < extent)
        w = jnp.where(jnp.logical_and(inside, plain), interior_weights.get(s, 0.0), 0.0)
        for r in range(4):
            if 0 <= r + s < 6 and closure_rows[r][r + s] != 0.0:
                w = jnp.where(low == r, closure_rows[r][r + s], w)
            if 0 <= r - s < 6 and closure_rows[r][r - s] != 0.0:
                w = jnp.where(high == r, -closure_rows[r][r - s], w)
        weights[s] = w
    return weights


def slope(x, weights, axis):
    total = weights[0] * x
    for s in (-3, -2, -1, 1, 2, 3):
        total = total + weights[s] * turn(x, -s, axis)
    return total


def pack_edges(tiles):
    group = lax.shift_right_logical(lane_of(), 2)
    out = []
    for start in range(0, len(tiles), 32):
        acc = jnp.zeros((rows, lanes), jnp.float32)
        for q, tile in enumerate(tiles[start : start + 32]):
            acc = jnp.where(group == q, turn(tile, 4 * q + 2, 1), acc)
        out.append(acc)
    return out


def edge_terms(left, right, has_left, has_right):
    place = jnp.bitwise_and(lane_of(), 3)
    low = jnp.where(
        place == 2, turn(left, 2, 1) - 8.0 * turn(left, 1, 1), turn(left, 2, 1)
    )
    high = jnp.where(
        place == 0, -turn(right, -2, 1), 8.0 * turn(right, -1, 1) - turn(right, -2, 1)
    )
    low = jnp.where(has_left, low, 0.0)
    high = jnp.where(has_right, high, 0.0)
    return jnp.where(place >= 2, low, high) * (1.0 / 12.0)


def row_terms(pack, from_low):
    even = jnp.bitwise_and(row_of(), 1) == 0
    low = jnp.where(even, pack - 8.0 * turn(pack, -1, 0), pack)
    high = jnp.where(even, -pack, 8.0 * turn(pack, 1, 0) - pack)
    return jnp.where(from_low, low, turn(high, 6, 0)) * (1.0 / 12.0)


def pair_rounds(size):
    first = [(i, i ^ 1) for i in range(size)]
    if size == 2:
        return (first,)
    second = [(i, (i + 1) % size if i % 2 else (i - 1) % size) for i in range(size)]
    return (first, second)


def where_am_i():
    return lax.axis_index("gx"), lax.axis_index("gy"), lax.axis_index("gz")


def paired_level(ocean, field, k, levels):
    a = ocean[field, k]
    b = ocean[field, k + levels // 2]
    return jnp.concatenate([a, b], axis=1)


def row_rims(packs, depth):
    tile = (x_fields.index(2) * depth) // 4
    if len(packs) == 1:
        return jnp.flip(packs[0][tile, :2], 0)
    odd = lax.axis_index("gx") % 2 == 1
    low = jnp.where(odd, packs[0][tile, 1:2], packs[1][tile, 1:2])
    high = jnp.where(odd, packs[1][tile, :1], packs[0][tile, :1])
    return jnp.concatenate([low, high], axis=0)


def rim_tile_of(packs, depth):
    tile = (x_fields.index(2) * depth) // 4
    odd = flag(lax.rem(lax.axis_index("gx"), 2))
    low, high = sides([pack[tile] for pack in packs], odd)
    rim = jnp.where(row_of() == 0, turn(low, -1, 0), turn(high, 1, 0))
    return jnp.where(row_of() < 2, rim, 0.0)


def sides(got, odd):
    if len(got) == 1:
        return got[0], got[0]
    return jnp.where(odd, got[0], got[1]), jnp.where(odd, got[1], got[0])


def one(condition):
    return condition.astype(jnp.int32)


def run_copies(copies):
    for copy in copies:
        copy.start()


def stage_kernel(solid_far, ocean_far, solid, ocean, *refs):
    outs, sems = refs[:-1], refs[-1]
    levels, fine = ocean.shape[1:3]
    depth = solid.shape[1]
    copies = [
        pltpu.make_async_copy(solid_far, solid, sems.at[0]),
        pltpu.make_async_copy(ocean_far, ocean, sems.at[1]),
    ]
    run_copies(copies)
    odd = flag(lax.rem(lax.axis_index("gx"), 2))
    pair = lax.shift_right_logical(row_of(), 1)

    def emit(heads, base):
        for number, out in enumerate(outs):
            acc = None
            for t, (head, tail) in enumerate(heads):
                q = t % 4
                edge = jnp.where(odd, head, tail) if number == 0 else jnp.where(odd, tail, head)
                edge = turn(edge, 2 * q, 0)
                acc = edge if q == 0 else jnp.where(pair == q, edge, acc)
                if q == 3:
                    out[base + t // 4] = acc

    copies[0].wait()
    heads = []
    for field in x_fields:
        for z in range(depth):
            tile = solid[field, z]
            heads.append((tile, turn(tile, 2, 0)))
    emit(heads, 0)
    base = len(heads) // 4
    copies[1].wait()
    heads = []
    for field in ocean_x_fields:
        for k in range(levels // 2):
            tile = paired_level(ocean, field, k, levels)
            heads.append((tile[:rows], turn(tile[fine - rows :], 2, 0)))
    emit(heads, base)


def pack_kernel(
    sizes, solid, ocean, medium, offset_x, offset_y,
    out_y, out_even, out_odd, out_pressure, out_medium, out_blend_x, out_blend_y,
):
    span_x, span_y, span_z = sizes
    levels, fine, width = ocean.shape[1:]
    depth = solid.shape[1]
    x, y, z = where_am_i()
    odd_z = lax.rem(z, 2)
    zero = jnp.zeros((rows, lanes), jnp.float32)
    packed = pack_edges([solid[field, k] for field in y_fields for k in range(depth)])
    outer, inner = [], []
    for field in ocean_y_fields:
        for k in range(levels // 2):
            tile = paired_level(ocean, field, k, levels)
            for r in range(0, fine, rows):
                outer.append(tile[r : r + rows])
                inner.append(turn(tile[r : r + rows], half, 1))
    ends = pack_edges(outer) + pack_edges(inner)
    for i, tile in enumerate(packed + ends + [zero]):
        out_y[i] = tile
    start_even = (1 - odd_z) * (depth - 2)
    start_odd = odd_z * (depth - 2)
    count = 0
    for field in z_fields:
        for k in range(2):
            out_even[count] = solid[field, start_even + k]
            out_odd[count] = solid[field, start_odd + k]
            count += 1
    for tile in ends:
        out_even[count] = tile
        out_odd[count] = tile
        count += 1

    dot = functools.partial(
        jnp.dot, precision=lax.Precision.HIGHEST, preferred_element_type=jnp.float32
    )
    pick_row = (
        lax.shift_right_logical(lane_of((rows, fine)), 1) == row_of((rows, fine))
    ).astype(jnp.float32)
    fine_col, coarse_col = row_of((width, lanes)), lane_of((width, lanes))
    pick_col = jnp.where(
        lax.shift_right_logical(fine_col, 1) + z * (width // 2) == coarse_col, 0.25, 0.0
    )
    pressure = dot(dot(pick_row, ocean[0, levels - 1]), pick_col)
    out_pressure[0] = pressure
    out_even[count] = jnp.where(flag(one(z == 0)), solid[2, 0], pressure)
    out_even[count + 1] = zero

    lower = lane_of() < half
    for m in range(2):
        for k in range(levels // 2):
            out_medium[m, k] = jnp.where(lower, medium[m, k], medium[m, k + levels // 2])

    shape = (2 * rows, fine)
    coarse = lax.shift_right_logical(lane_of(shape), 1)
    target = jnp.clip(coarse + offset_x[...], -(x * rows), (span_x - x) * rows - 1)
    target = jnp.where(target < 0, rows, jnp.where(target >= rows, rows + 1, target))
    out_blend_x[...] = 0.75 * (row_of(shape) == coarse).astype(jnp.float32) + 0.25 * (
        row_of(shape) == target
    ).astype(jnp.float32)
    fine_col, source = lane_of((lanes, lanes)), row_of((lanes, lanes))
    coarse = lax.shift_right_logical(fine_col - half, 1) + z * (width // 2)
    shift_y = jnp.concatenate([offset_y[...], offset_y[...]], axis=1)
    target = jnp.clip(coarse + shift_y, -(y * lanes), (span_y - y) * lanes - 1)
    upper = fine_col >= half
    near_weight = jnp.where(upper, 0.75, 0.0)
    far_weight = jnp.where(upper, 0.25, 0.0)
    out_blend_y[0] = jnp.where(source == coarse, near_weight, 0.0) + jnp.where(
        source == target, far_weight, 0.0
    )
    outside = jnp.logical_or(
        jnp.logical_and(source == lanes - 1, target == -1),
        jnp.logical_and(source == 0, target == lanes),
    )
    out_blend_y[1] = jnp.where(outside, far_weight, 0.0)


def x_scratch(packs, scratch):
    odd = flag(lax.rem(lax.axis_index("gx"), 2))
    yes = jnp.full((rows, lanes), True)

    def fill(tiles):
        for i in tiles:
            low, high = sides([pack[i] for pack in packs], odd)
            if len(packs) == 1:
                scratch[0, i] = row_terms(low, odd)
            else:
                scratch[0, i] = row_terms(low, yes)
                scratch[1, i] = row_terms(high, jnp.logical_not(yes))

    def terms(t, mask_low, mask_high):
        q = t % 4
        tile = turn(scratch[0, t // 4], -2 * q, 0)
        if len(packs) == 1:
            return jnp.where(jnp.logical_or(mask_low, mask_high), tile, 0.0)
        high = turn(scratch[1, t // 4], -2 * q, 0)
        return jnp.where(mask_low, tile, jnp.where(mask_high, high, 0.0))

    return fill, terms


def ocean_kernel(sizes, ocean, medium, *refs):
    packs = refs[:-7]
    ocean_next, ocean_rate, carry, stage_next, stage_rate, scratch, sems = refs[-7:]
    span_x, span_y, span_z = sizes
    levels, fine, width = ocean.shape[1:]
    pairs = levels // 2
    x, y, z = where_am_i()
    x_first, x_last = one(x == 0), one(x == span_x - 1)
    joint_first = one(y == 0) * one(z == 0)
    joint_last = one(y == span_y - 1) * one(z == span_z - 1)
    row = row_of()
    low_rows = jnp.logical_and(row < 2, flag(1 - x_first))
    high_rows = jnp.logical_and(row >= rows - 2, flag(1 - x_last))
    never = jnp.full((rows, lanes), False)
    fill, terms = x_scratch(packs, scratch)
    tiles = len(ocean_x_fields) * pairs // 4
    first_tile = packs[0].shape[0] - tiles
    fill(range(first_tile, first_tile + tiles))

    def x_ends(t):
        t = 4 * first_tile + t
        return jnp.concatenate([terms(t, low_rows, never), terms(t, never, high_rows)], axis=0)

    wide = (fine, lanes)
    lower = lane_of(wide) < half
    weights_x = stencil(row_of(wide), fine, x_first, x_last)
    weights_y = stencil(
        jnp.bitwise_and(lane_of(wide), half - 1), half, joint_first, joint_last
    )
    states = [[paired_level(ocean, m, k, levels) for k in range(pairs)] for m in range(4)]

    def slope_z(m, k):
        def at(i):
            if 0 <= i < pairs:
                return states[m][i]
            return turn(states[m][i % pairs], half, 1)

        total = (at(k - 2) - at(k + 2) + 8.0 * (at(k + 1) - at(k - 1))) * (1.0 / 12.0)
        if k < 4:
            near = sum(w * at(c) for c, w in enumerate(closure_rows[k]) if w != 0.0)
            total = jnp.where(lower, near, total)
        if pairs - 1 - k < 4:
            near = sum(
                -w * at(pairs - 1 - c)
                for c, w in enumerate(closure_rows[pairs - 1 - k])
                if w != 0.0
            )
            total = jnp.where(lower, total, near)
        return total

    copies = []
    chunk = pairs // 2
    for k in range(pairs):
        bulk = jnp.concatenate([medium[0, k]] * 2, axis=0)
        light = jnp.concatenate([medium[1, k]] * 2, axis=0)
        p, u, v, w = (states[m][k] for m in range(4))
        dxu = slope(u, weights_x, 0) + x_ends(k)
        dxp = slope(p, weights_x, 0) + x_ends(pairs + k)
        dyv = slope(v, weights_y, 1)
        dyp = slope(p, weights_y, 1)
        rate_p = -bulk * (2.0 * (dxu + dyv) + slope_z(3, k)) + gravity * w / light
        rate_w = -light * slope_z(0, k)
        if k == pairs - 1:
            rate_p = rate_p + jnp.where(lower, 0.0, inv_norm * bulk * w)
        if k == 0:
            rate_w = rate_w - jnp.where(lower, inv_norm * light * p, 0.0)
        carry[0, k] = rate_p
        carry[1, k] = -2.0 * light * dyp
        carry[2, k] = p
        carry[3, k] = v
        store_pair(stage_rate, stage_next, 0, k, -2.0 * light * dxp, u)
        store_pair(stage_rate, stage_next, 1, k, rate_w, w)
        if (k + 1) % chunk == 0:
            copies += out_copies(
                ((stage_rate, ocean_rate), (stage_next, ocean_next)),
                (1, 3), k + 1 - chunk, chunk, pairs, sems, len(copies),
            )
    for copy in copies:
        copy.wait()


def store_pair(stage_rate, stage_next, slot, k, rate, state):
    pairs = stage_rate.shape[1] // 2
    rate = step_size * rate
    after = state + section_weight * rate
    stage_rate[slot, k] = rate[:, :half]
    stage_next[slot, k] = after[:, :half]
    stage_rate[slot, k + pairs] = turn(rate, half, 1)[:, :half]
    stage_next[slot, k + pairs] = turn(after, half, 1)[:, :half]


def out_copies(routes, fields, start, chunk, pairs, sems, used):
    copies = []
    for stage, out in routes:
        for slot, field in enumerate(fields):
            for base in (start, start + pairs):
                copies.append(
                    pltpu.make_async_copy(
                        stage.at[slot, pl.ds(base, chunk)],
                        out.at[field, pl.ds(base, chunk)],
                        sems.at[used + len(copies)],
                    )
                )
    run_copies(copies)
    return copies


def relay_kernel(count_x, solid, pressure, got_even, got_ya, got_yb, *refs):
    packs, out = refs[:count_x], refs[-1]
    depth = solid.shape[1]
    x, y, z = where_am_i()
    odd_y = flag(lax.rem(y, 2))
    bottom, second = flag(one(z == 0)), flag(one(z == 1))
    lane = lane_of()
    got_y = (got_ya, got_yb)
    edge_tiles = out_edge_tiles(depth)
    ring = 2 * len(z_fields)
    t = y_fields.index(2) * depth
    _, right = sides([g[t // 32] for g in got_y], odd_y)
    right = turn(right, -(4 * (t % 32) + 2), 1)
    _, right_rim = sides([g[edge_tiles + 2] for g in got_y], odd_y)
    first = lane == 0
    plane = jnp.where(first, right, solid[2, 0])
    rim = jnp.where(first, right_rim, rim_tile_of(packs, depth))
    came = got_even[ring + 2]
    out[0] = jnp.where(bottom, plane, jnp.where(second, came, came + pressure[0]))
    out[1] = jnp.where(bottom, rim, got_even[ring + 3])
    for i in range(2):
        low, high = sides([g[edge_tiles + i] for g in got_y], odd_y)
        out[2 + i] = jnp.where(bottom, high, low)


def out_edge_tiles(depth):
    return -(-len(y_fields) * depth // 32)


def solid_kernel(sizes, solid, material, got_even, got_odd, got_ya, got_yb, *refs):
    packs = refs[:-7]
    solid_next, solid_rate, carry, stage_next, stage_rate, scratch, sems = refs[-7:]
    span_x, span_y, span_z = sizes
    depth = solid.shape[1]
    x, y, z = where_am_i()
    x_first, x_last = one(x == 0), one(x == span_x - 1)
    y_first, y_last = one(y == 0), one(y == span_y - 1)
    odd_y, odd_z = flag(lax.rem(y, 2)), flag(lax.rem(z, 2))
    lane, row = lane_of(), row_of()
    low_rows = jnp.logical_and(row < 2, flag(1 - x_first))
    high_rows = jnp.logical_and(row >= rows - 2, flag(1 - x_last))
    fill, x_terms = x_scratch(packs, scratch)
    fill(range(len(x_fields) * depth // 4))
    y_edges = []
    for i in range(out_edge_tiles(depth)):
        low, high = sides([got_ya[i], got_yb[i]], odd_y)
        y_edges.append(edge_terms(low, high, flag(1 - y_first), flag(1 - y_last)))
    end_lanes = jnp.logical_or(lane < 2, lane >= lanes - 2)

    def y_terms(t):
        return jnp.where(end_lanes, turn(y_edges[t // 32], -(4 * (t % 32) + 2), 1), 0.0)

    weights_x = stencil(row, rows, x_first, x_last)
    weights_y = stencil(lane, lanes, y_first, y_last)
    at_first, at_last = flag(one(z == 0)), flag(one(z == span_z - 1))

    def layer(i, k):
        if 0 <= k < depth:
            return solid[z_fields[i], k]
        j = 2 * i + (k + 2 if k < 0 else k - depth)
        low, high = sides([got_even[j], got_odd[j]], odd_z)
        return low if k < 0 else high

    def slope_z(i, k):
        total = (
            layer(i, k - 2) - layer(i, k + 2) + 8.0 * (layer(i, k + 1) - layer(i, k - 1))
        ) * (1.0 / 12.0)
        if k < 4:
            near = sum(w * layer(i, c) for c, w in enumerate(closure_rows[k]) if w != 0.0)
            total = jnp.where(at_first, near, total)
        if depth - 1 - k < 4:
            near = sum(
                -w * layer(i, depth - 1 - c)
                for c, w in enumerate(closure_rows[depth - 1 - k])
                if w != 0.0
            )
            total = jnp.where(at_last, near, total)
        return total

    copies = []
    for k in range(depth):
        dx = {
            m: slope(solid[m, k], weights_x, 0) + x_terms(i * depth + k, low_rows, high_rows)
            for i, m in enumerate(x_fields)
        }
        dy = {
            m: slope(solid[m, k], weights_y, 1) + y_terms(i * depth + k)
            for i, m in enumerate(y_fields)
        }
        metric = material[3, k]
        dz = {m: metric * slope_z(i, k) for i, m in enumerate(z_fields)}
        buoyancy, lame_one, lame_two = material[0, k], material[1, k], material[2, k]
        dilation = lame_one * (dx[0] + dy[1] + dz[2])
        twice = 2.0 * lame_two
        rates = [
            buoyancy * (dx[3] + dy[8] + dz[7]),
            buoyancy * (dx[8] + dy[4] + dz[6]),
            buoyancy * (dx[7] + dy[6] + dz[5]),
            dilation + twice * dx[0],
            dilation + twice * dy[1],
            dilation + twice * dz[2],
            lame_two * (dz[1] + dy[2]),
            lame_two * (dz[0] + dx[2]),
            lame_two * (dy[0] + dx[1]),
        ]
        if k == 0:
            factor = jnp.where(at_first, inv_norm * buoyancy * metric, 0.0)
            rates[0] = rates[0] + factor * solid[7, 0]
            rates[1] = rates[1] + factor * solid[6, 0]
            carry[0] = rates[2] + factor * solid[5, 0]
            carry[1] = factor
        for m, rate in enumerate(rates):
            rate = step_size * rate
            stage_rate[m, k] = rate
            stage_next[m, k] = solid[m, k] + section_weight * rate
        if k == 0:
            spans = ((0, 2, 0, 1), (3, 6, 0, 1))
        else:
            spans = ((0, 9, k, 1),) if k % 2 else ()
            spans = spans if k < 3 else ((0, 9, k - 1, 2),) if k % 2 else ()
        fresh = []
        for first, count, level, thick in spans:
            at = (pl.ds(first, count), pl.ds(level, thick))
            for stage, out in ((stage_rate, solid_rate), (stage_next, solid_next)):
                n = len(copies) + len(fresh)
                fresh.append(pltpu.make_async_copy(stage.at[at], out.at[at], sems.at[n]))
        run_copies(fresh)
        copies += fresh
    for copy in copies:
        copy.wait()


def last_kernel(
    sizes, solid, medium, pressure, blend_x, blend_y, ocean_carry, solid_carry,
    got_even, got_odd, got_far, got_ya, got_yb, *refs,
):
    span_x, span_y, span_z = sizes
    packs = refs[:-13]
    outs = refs[-9:-5]
    solid_next, solid_rate, ocean_next, ocean_rate = outs
    stage_next, stage_rate, vz_next, vz_rate, sems = refs[-5:]
    depth = solid.shape[1]
    pairs, fine = ocean_carry.shape[1:3]
    x, y, z = where_am_i()
    odd_y, odd_z = flag(lax.rem(y, 2)), flag(lax.rem(z, 2))
    bottom, second, top = (flag(one(z == i)) for i in (0, 1, span_z - 1))
    joint_first = one(y == 0) * one(z == 0)
    joint_last = one(y == span_y - 1) * one(z == span_z - 1)
    lane = lane_of()
    ring = 2 * len(z_fields)
    copies = []

    sum_pressure = pressure[0] + got_even[ring + 2] + got_far[0]
    rate = step_size * (solid_carry[0] + solid_carry[1] * sum_pressure)
    vz_rate[0, 0] = rate
    vz_next[0, 0] = solid[2, 0] + section_weight * rate
    at = (pl.ds(2, 1), pl.ds(0, 1))
    for stage, out in ((vz_rate, solid_rate), (vz_next, solid_next)):
        copies.append(pltpu.make_async_copy(stage, out.at[at], sems.at[len(copies)]))
    run_copies(copies)

    lows, highs = [], []
    for i in range(2):
        low, high = sides([got_even[ring + i], got_odd[ring + i]], odd_z)
        lows.append(jnp.where(bottom, got_far[2 + i], low))
        highs.append(jnp.where(top, got_far[2 + i], high))
    has_left, has_right = flag(1 - joint_first), flag(1 - joint_last)
    outer = edge_terms(lows[1], highs[1], has_left, has_right)
    inner = edge_terms(lows[0], highs[0], has_left, has_right)
    end_lanes = jnp.logical_or(lane < 2, lane >= lanes - 2)
    mid_lanes = jnp.logical_and(lane >= half - 2, lane < half + 2)

    def y_ends(t):
        parts = []
        for r in range(fine // rows):
            q = t * (fine // rows) + r
            end = turn(outer, -(4 * q + 2), 1)
            mid = turn(inner, half - (4 * q + 2), 1)
            parts.append(jnp.where(end_lanes, end, jnp.where(mid_lanes, mid, 0.0)))
        return jnp.concatenate(parts, axis=0)

    edge_tiles = out_edge_tiles(depth)
    t = y_fields.index(2) * depth
    left, _ = sides([got_ya[t // 32], got_yb[t // 32]], odd_y)
    left = turn(left, lanes - 1 - (4 * (t % 32) + 1), 1)
    left_rim, _ = sides([got_ya[edge_tiles + 2], got_yb[edge_tiles + 2]], odd_y)
    own_rim = rim_tile_of(packs, depth)
    plane = jnp.where(bottom, solid[2, 0], jnp.where(second, got_even[ring + 2], got_far[0]))
    rim = jnp.where(bottom, own_rim, jnp.where(second, got_even[ring + 3], got_far[1]))
    beside = jnp.where(lane == 0, got_far[0], left)
    beside_rim = jnp.where(lane == 0, got_far[1], left_rim)
    dot = functools.partial(
        lax.dot_general,
        precision=lax.Precision.HIGHEST,
        preferred_element_type=jnp.float32,
    )
    over_rows = (((0,), (0,)), ((), ()))
    plain = (((1,), (0,)), ((), ()))
    blend = blend_x[...]
    inside_rows = dot(blend, jnp.concatenate([plane, rim], axis=0), over_rows)
    beside_rows = dot(blend, jnp.concatenate([beside, beside_rim], axis=0), over_rows)
    bed_speed = dot(inside_rows, blend_y[0], plain) + dot(beside_rows, blend_y[1], plain)

    lower = lane_of((fine, lanes)) < half
    chunk = pairs // 2
    for k in range(pairs):
        bulk = jnp.concatenate([medium[0, k]] * 2, axis=0)
        light = jnp.concatenate([medium[1, k]] * 2, axis=0)
        rate_p = ocean_carry[0, k] - 2.0 * bulk * y_ends(k)
        rate_v = ocean_carry[1, k] - 2.0 * light * y_ends(pairs + k)
        if k == pairs - 1:
            rate_p = rate_p - jnp.where(lower, 0.0, inv_norm * bulk * bed_speed)
        store_pair(stage_rate, stage_next, 0, k, rate_p, ocean_carry[2, k])
        store_pair(stage_rate, stage_next, 1, k, rate_v, ocean_carry[3, k])
        if (k + 1) % chunk == 0:
            copies += out_copies(
                ((stage_rate, ocean_rate), (stage_next, ocean_next)),
                (0, 2), k + 1 - chunk, chunk, pairs, sems, len(copies),
            )
    for copy in copies:
        copy.wait()


def body(solid_state, material, ocean_state, ocean_medium, offset_x, offset_y):
    sizes = tuple(lax.axis_size(axis) for axis in ("gx", "gy", "gz"))
    span_x, span_y, span_z = sizes
    depth = solid_state.shape[1]
    levels, fine, width = ocean_state.shape[1:]
    pairs = levels // 2
    if solid_state.shape[2:] != (rows, lanes) or (fine, width) != (2 * rows, half):
        raise ValueError("tile shape")
    if depth % 4 or levels % 2 or span_z != 4 or span_x % 2 or span_y % 2 or span_y < 4:
        raise ValueError("sizes")
    f32 = jnp.float32
    vmem = pl.BlockSpec(memory_space=pltpu.VMEM)
    smem = pl.BlockSpec(memory_space=pltpu.SMEM)
    hbm = pl.BlockSpec(memory_space=pl.ANY)
    near = lambda x: pltpu.with_memory_space_constraint(x, pltpu.VMEM)
    tiles = lambda *n: pltpu.VMEM((*n, rows, lanes), f32)
    like = lambda a: jax.ShapeDtypeStruct(a.shape, f32)
    dma = pltpu.SemaphoreType.DMA
    material_near = near(material)

    x_rounds = pair_rounds(span_x)
    pack_tiles = (len(x_fields) * depth + len(ocean_x_fields) * pairs) // 4
    solid, ocean, *sent_x = pl.pallas_call(
        stage_kernel,
        out_shape=[pltpu.VMEM(solid_state.shape, f32), pltpu.VMEM(ocean_state.shape, f32)]
        + [tiles(pack_tiles) for _ in x_rounds],
        in_specs=[hbm, hbm],
        out_specs=[vmem] * (2 + len(x_rounds)),
        scratch_shapes=[dma((2,))],
        name="stage",
    )(solid_state, ocean_state)
    solid, ocean = near(solid), near(ocean)
    came_x = [lax.ppermute(m, "gx", p) for m, p in zip(sent_x, x_rounds)]
    got_x = [near(m) for m in came_x]
    count_x = len(got_x)

    edge_tiles = out_edge_tiles(depth)
    layers = 2 * len(z_fields)
    sent_y, sent_even, sent_odd, pressure, medium, blend_x, blend_y = pl.pallas_call(
        functools.partial(pack_kernel, sizes),
        out_shape=[
            tiles(edge_tiles + 3),
            tiles(layers + 4),
            tiles(layers + 2),
            tiles(1),
            tiles(2, pairs),
            pltpu.VMEM((2 * rows, fine), f32),
            pltpu.VMEM((2, lanes, lanes), f32),
        ],
        in_specs=[vmem, vmem, smem, vmem, vmem],
        out_specs=[vmem] * 7,
        name="pack",
    )(solid, ocean, ocean_medium, offset_x.reshape(1, fine), offset_y.reshape(1, width))
    pressure, medium, blend_x, blend_y = map(near, (pressure, medium, blend_x, blend_y))
    ring = ("gy", "gz")
    places = [(y, z) for y in range(span_y) for z in range(span_z)]

    def over_ring(move):
        return [(y * span_z + z, y2 * span_z + z2)
                for y, z in places for y2, z2 in (move(y, z),)]

    even = over_ring(lambda y, z: (y, z ^ 1))
    inner = over_ring(
        lambda y, z: (y ^ 1, z) if z in (0, span_z - 1) else (y, z + 1 if z % 2 else z - 1)
    )
    ends = over_ring(lambda y, z: (y, span_z - 1 - z))
    got_odd = near(lax.ppermute(sent_odd, ring, inner))
    rim = row_rims(came_x, depth)
    sent_y, sent_even = (m.at[m.shape[0] - 1, :2].set(rim) for m in (sent_y, sent_even))
    got_y = [near(lax.ppermute(sent_y, "gy", p)) for p in pair_rounds(span_y)]
    got_even = near(lax.ppermute(sent_even, ring, even))

    ocean_next, ocean_rate, ocean_carry = pl.pallas_call(
        functools.partial(ocean_kernel, sizes),
        out_shape=[like(ocean_state), like(ocean_state), pltpu.VMEM((4, pairs, fine, lanes), f32)],
        in_specs=[vmem] * (2 + count_x),
        out_specs=[hbm, hbm, vmem],
        scratch_shapes=[
            pltpu.VMEM((2, levels, fine, width), f32),
            pltpu.VMEM((2, levels, fine, width), f32),
            pltpu.VMEM((count_x, pack_tiles, rows, lanes), f32),
            dma((16,)),
        ],
        name="ocean",
    )(ocean, medium, *got_x)

    sent_far = pl.pallas_call(
        functools.partial(relay_kernel, count_x),
        out_shape=tiles(4),
        in_specs=[vmem] * (5 + count_x),
        out_specs=vmem,
        name="relay",
    )(solid, pressure, got_even, *got_y, *got_x)
    got_far = near(lax.ppermute(sent_far, ring, ends))

    solid_next, solid_rate, solid_carry = pl.pallas_call(
        functools.partial(solid_kernel, sizes),
        out_shape=[like(solid_state), like(solid_state), tiles(2)],
        in_specs=[vmem] * (6 + count_x),
        out_specs=[hbm, hbm, vmem],
        scratch_shapes=[
            pltpu.VMEM(solid_state.shape, f32),
            pltpu.VMEM(solid_state.shape, f32),
            pltpu.VMEM((count_x, pack_tiles, rows, lanes), f32),
            dma((2 * depth,)),
        ],
        name="solid",
    )(solid, material_near, got_even, got_odd, *got_y, *got_x)

    return pl.pallas_call(
        functools.partial(last_kernel, sizes),
        out_shape=[like(solid_state), like(solid_state), like(ocean_state), like(ocean_state)],
        in_specs=[vmem] * (12 + count_x) + [hbm] * 4,
        out_specs=[hbm] * 4,
        input_output_aliases={12 + count_x + i: i for i in range(4)},
        scratch_shapes=[
            pltpu.VMEM((2, levels, fine, width), f32),
            pltpu.VMEM((2, levels, fine, width), f32),
            tiles(1, 1),
            tiles(1, 1),
            dma((18,)),
        ],
        name="last",
    )(
        solid, medium, pressure, blend_x, blend_y, near(ocean_carry), near(solid_carry),
        got_even, got_odd, got_far, *got_y, *got_x,
        solid_next, solid_rate, ocean_next, ocean_rate,
    )


def solution(mesh):
    in_specs = (
        P(None, "gz", "gx", "gy"),
        P(None, "gz", "gx", "gy"),
        P(None, None, "gx", ("gy", "gz")),
        P(),
        P("gx"),
        P(("gy", "gz")),
    )
    out_specs = (
        P(None, "gz", "gx", "gy"),
        P(None, "gz", "gx", "gy"),
        P(None, None, "gx", ("gy", "gz")),
        P(None, None, "gx", ("gy", "gz")),
    )
    return jax.shard_map(body, mesh=mesh, in_specs=in_specs, out_specs=out_specs, check_vma=False)
```

```python
import functools

import jax
import jax.numpy as jnp
from jax import lax
from jax.experimental import pallas as pl
from jax.experimental.pallas import tpu as pltpu
from jax.sharding import PartitionSpec as P


closure_rows = (
    (-24.0 / 17.0, 59.0 / 34.0, -4.0 / 17.0, -3.0 / 34.0, 0.0, 0.0),
    (-0.5, 0.0, 0.5, 0.0, 0.0, 0.0),
    (4.0 / 43.0, -59.0 / 86.0, 0.0, 59.0 / 86.0, -4.0 / 43.0, 0.0),
    (3.0 / 98.0, 0.0, -59.0 / 98.0, 0.0, 32.0 / 49.0, -4.0 / 49.0),
)
inv_norm = 48.0 / 17.0
step_size = 0.25
section_weight = 0.1496590219993
gravity = 0.4
interior_weights = {-2: 1.0 / 12.0, -1: -8.0 / 12.0, 1: 8.0 / 12.0, 2: -1.0 / 12.0}

x_fields = (0, 1, 2, 3, 8, 7)
y_fields = (0, 1, 2, 4, 8, 6)
z_fields = (0, 1, 2, 5, 6, 7)
ocean_x_fields = (1, 0)
ocean_y_fields = (2, 0)
rows, lanes, half = 8, 128, 64
far = 1 << 20


def turn(x, shift, axis):
    shift = shift % x.shape[axis]
    return x if shift == 0 else pltpu.roll(x, shift, axis)


def flag(value, shape=(rows, lanes)):
    return jnp.broadcast_to(value.astype(jnp.int32), shape) == 1


def lane_of(shape=(rows, lanes)):
    return lax.broadcasted_iota(jnp.int32, shape, 1)


def row_of(shape=(rows, lanes)):
    return lax.broadcasted_iota(jnp.int32, shape, 0)


def stencil(position, extent, first, last):
    low = position + far * (1 - first)
    high = extent - 1 - position + far * (1 - last)
    plain = jnp.logical_and(low >= 4, high >= 4)
    weights = {}
    for s in range(-3, 4):
        inside = jnp.logical_and(position + s >= 0, position + s < extent)
        w = jnp.where(jnp.logical_and(inside, plain), interior_weights.get(s, 0.0), 0.0)
        for r in range(4):
            if 0 <= r + s < 6 and closure_rows[r][r + s] != 0.0:
                w = jnp.where(low == r, closure_rows[r][r + s], w)
            if 0 <= r - s < 6 and closure_rows[r][r - s] != 0.0:
                w = jnp.where(high == r, -closure_rows[r][r - s], w)
        weights[s] = w
    return weights


def slope(x, weights, axis):
    total = weights[0] * x
    for s in (-3, -2, -1, 1, 2, 3):
        total = total + weights[s] * turn(x, -s, axis)
    return total


def pack_edges(tiles):
    group = lax.shift_right_logical(lane_of(), 2)
    out = []
    for start in range(0, len(tiles), 32):
        acc = jnp.zeros((rows, lanes), jnp.float32)
        for q, tile in enumerate(tiles[start : start + 32]):
            acc = jnp.where(group == q, turn(tile, 4 * q + 2, 1), acc)
        out.append(acc)
    return out


def edge_terms(left, right, has_left, has_right):
    place = jnp.bitwise_and(lane_of(), 3)
    low = jnp.where(
        place == 2, turn(left, 2, 1) - 8.0 * turn(left, 1, 1), turn(left, 2, 1)
    )
    high = jnp.where(
        place == 0, -turn(right, -2, 1), 8.0 * turn(right, -1, 1) - turn(right, -2, 1)
    )
    low = jnp.where(has_left, low, 0.0)
    high = jnp.where(has_right, high, 0.0)
    return jnp.where(place >= 2, low, high) * (1.0 / 12.0)


def row_terms(pack, from_low):
    even = jnp.bitwise_and(row_of(), 1) == 0
    low = jnp.where(even, pack - 8.0 * turn(pack, -1, 0), pack)
    high = jnp.where(even, -pack, 8.0 * turn(pack, 1, 0) - pack)
    return jnp.where(from_low, low, turn(high, 6, 0)) * (1.0 / 12.0)


def pair_rounds(size):
    first = [(i, i ^ 1) for i in range(size)]
    if size == 2:
        return (first,)
    second = [(i, (i + 1) % size if i % 2 else (i - 1) % size) for i in range(size)]
    return (first, second)


def where_am_i():
    return lax.axis_index("gx"), lax.axis_index("gy"), lax.axis_index("gz")


def paired_level(ocean, field, k, levels):
    a = ocean[field, k]
    b = ocean[field, k + levels // 2]
    return jnp.concatenate([a, b], axis=1)


def row_rims(planes):
    if len(planes) == 1:
        return jnp.concatenate([planes[0][-1:], planes[0][:1]], axis=0)
    odd = lax.axis_index("gx") % 2 == 1
    low = jnp.where(odd, planes[0][-1:], planes[1][-1:])
    high = jnp.where(odd, planes[1][:1], planes[0][:1])
    return jnp.concatenate([low, high], axis=0)


def rim_tile_of(planes):
    odd = flag(lax.rem(lax.axis_index("gx"), 2))
    low, high = sides([plane[...] for plane in planes], odd)
    rim = jnp.where(row_of() == 0, turn(low, 1, 0), turn(high, 1, 0))
    return jnp.where(row_of() < 2, rim, 0.0)


def sides(got, odd):
    if len(got) == 1:
        return got[0], got[0]
    return jnp.where(odd, got[0], got[1]), jnp.where(odd, got[1], got[0])


def one(condition):
    return condition.astype(jnp.int32)


def run_copies(copies):
    for copy in copies:
        copy.start()


def stage_kernel(sizes, *refs):
    solid_far, ocean_far, medium_far, offset_x_far, offset_y_far = refs[:5]
    solid, ocean, medium, index = refs[5:9]
    small, offset_x, offset_y, sems = refs[9:]
    copies = [
        pltpu.make_async_copy(solid_far, solid, sems.at[0]),
        pltpu.make_async_copy(ocean_far, ocean, sems.at[1]),
        pltpu.make_async_copy(medium_far, small, sems.at[2]),
        pltpu.make_async_copy(offset_x_far, offset_x, sems.at[3]),
        pltpu.make_async_copy(offset_y_far, offset_y, sems.at[4]),
    ]
    run_copies(copies)
    for copy in copies[2:]:
        copy.wait()
    fill_tables(sizes, small, offset_x, offset_y, medium, index)
    for copy in copies[:2]:
        copy.wait()


def pack_x_kernel(solid, ocean, *outs):
    levels, fine = ocean.shape[1:3]
    depth = solid.shape[1]
    odd = flag(lax.rem(lax.axis_index("gx"), 2))
    pair = lax.shift_right_logical(row_of(), 1)

    def emit(heads, base):
        for number, out in enumerate(outs):
            acc = None
            for t, (head, tail) in enumerate(heads):
                q = t % 4
                edge = jnp.where(odd, head, tail) if number == 0 else jnp.where(odd, tail, head)
                edge = turn(edge, 2 * q, 0)
                acc = edge if q == 0 else jnp.where(pair == q, edge, acc)
                if q == 3:
                    out[base + t // 4] = acc

    heads = []
    for field in x_fields:
        for k in range(depth):
            tile = solid[field, k]
            heads.append((tile, turn(tile, 2, 0)))
    emit(heads, 0)
    base = len(heads) // 4
    heads = []
    for field in ocean_x_fields:
        for k in range(levels // 2):
            tile = paired_level(ocean, field, k, levels)
            heads.append((tile[:rows], turn(tile[fine - rows :], 2, 0)))
    emit(heads, base)


def pack_kernel(solid, ocean, out_y, out_small, out_even, out_odd, out_pressure):
    levels, fine, width = ocean.shape[1:]
    depth = solid.shape[1]
    _, _, z = where_am_i()
    odd_z = lax.rem(z, 2)
    zero = jnp.zeros((rows, lanes), jnp.float32)
    packed = pack_edges([solid[field, k] for field in y_fields for k in range(depth)])
    outer, inner = [], []
    for field in ocean_y_fields:
        for k in range(levels // 2):
            tile = paired_level(ocean, field, k, levels)
            for r in range(0, fine, rows):
                outer.append(tile[r : r + rows])
                inner.append(turn(tile[r : r + rows], half, 1))
    ends = pack_edges(outer) + pack_edges(inner)
    for i, tile in enumerate(packed + ends + [zero]):
        out_y[i] = tile
    start_even = (1 - odd_z) * (depth - 2)
    start_odd = odd_z * (depth - 2)
    count = 0
    for field in z_fields:
        for k in range(2):
            out_even[count] = solid[field, start_even + k]
            out_odd[count] = solid[field, start_odd + k]
            count += 1
    for i, tile in enumerate(ends):
        out_small[i] = tile
        out_odd[count + i] = tile

    deepest = ocean[0, levels - 1]
    deepest = jnp.concatenate([deepest, deepest], axis=1)
    source = jnp.bitwise_and(2 * row_of(), rows - 1)
    halves = []
    for r in range(2):
        part = deepest[r * rows : (r + 1) * rows]
        halves.append(pick(part + turn(part, -1, 0), source, 0))
    pressure = jnp.where(row_of() < rows // 2, halves[0], halves[1])
    pressure = 0.25 * (pressure + turn(pressure, -1, 1))
    column = lane_of() - z * (width // 2)
    mine = jnp.logical_and(column >= 0, column < width // 2)
    pressure = pick(pressure, jnp.bitwise_and(2 * column, lanes - 1), 1)
    pressure = jnp.where(mine, pressure, 0.0)
    out_pressure[0] = pressure
    out_small[2] = jnp.where(flag(one(z == 0)), solid[2, 0], pressure)
    out_small[3] = zero


def fill_tables(sizes, medium, offset_x, offset_y, out_medium, out_index):
    span_x, span_y, _ = sizes
    fine, width = offset_x.shape[1], offset_y.shape[1]
    pairs = out_medium.shape[1]
    x, y, z = where_am_i()
    lane, row = lane_of(), row_of()
    lower = lane < half
    for m in range(2):
        for k in range(pairs):
            out_medium[m, k] = jnp.where(lower, medium[m, k], medium[m, k + pairs])

    moves = jnp.concatenate([offset_x[...].astype(jnp.float32)] * (lanes // fine), axis=1)
    moves = jnp.broadcast_to(moves, (rows, lanes))
    for r in range(2):
        place = row + r * rows
        move = jnp.sum(jnp.where(lane == place, moves, 0.0), axis=1, keepdims=True)
        target = lax.shift_right_logical(place, 1) + move.astype(jnp.int32)
        out_index[r] = jnp.clip(target, -(x * rows), (span_x - x) * rows - 1)
    coarse = lax.shift_right_logical(jnp.bitwise_and(lane, half - 1), 1) + z * (width // 2)
    move = jnp.concatenate([offset_y[...], offset_y[...]], axis=1)
    out_index[2] = coarse
    out_index[3] = jnp.clip(
        coarse + jnp.broadcast_to(move, (rows, lanes)), -(y * lanes), (span_y - y) * lanes - 1
    )


def pick(x, index, axis):
    return jnp.take_along_axis(x, index, axis=axis)


def blend_rows(plane, rim, index):
    parts = []
    for r in range(2):
        near = pick(plane, lax.shift_right_logical(row_of() + r * rows, 1), 0)
        target = index[r]
        inside = jnp.logical_and(target >= 0, target < rows)
        beyond = jnp.where(target < 0, rim[0:1], rim[1:2])
        other = jnp.where(inside, pick(plane, jnp.bitwise_and(target, rows - 1), 0), beyond)
        parts.append(0.75 * near + 0.25 * other)
    return parts


def blend_cols(inside, beside, index):
    near, target = index[2], index[3]
    at_home = jnp.logical_and(target >= 0, target < lanes)
    source = jnp.bitwise_and(target, lanes - 1)
    parts = []
    for own, other in zip(inside, beside):
        far_value = jnp.where(at_home, pick(own, source, 1), pick(other, source, 1))
        parts.append(0.75 * pick(own, near, 1) + 0.25 * far_value)
    return jnp.concatenate(parts, axis=0)


def x_scratch(packs, scratch):
    odd = flag(lax.rem(lax.axis_index("gx"), 2))
    yes = jnp.full((rows, lanes), True)

    def fill(tiles):
        for i in tiles:
            low, high = sides([pack[i] for pack in packs], odd)
            if len(packs) == 1:
                scratch[0, i] = row_terms(low, odd)
            else:
                scratch[0, i] = row_terms(low, yes)
                scratch[1, i] = row_terms(high, jnp.logical_not(yes))

    def terms(t, mask_low, mask_high):
        q = t % 4
        tile = turn(scratch[0, t // 4], -2 * q, 0)
        if len(packs) == 1:
            return jnp.where(jnp.logical_or(mask_low, mask_high), tile, 0.0)
        high = turn(scratch[1, t // 4], -2 * q, 0)
        return jnp.where(mask_low, tile, jnp.where(mask_high, high, 0.0))

    return fill, terms


def ocean_kernel(sizes, ocean, medium, *refs):
    packs = refs[:-7]
    ocean_next, ocean_rate, carry, stage_next, stage_rate, scratch, sems = refs[-7:]
    span_x, span_y, span_z = sizes
    levels, fine, _ = ocean.shape[1:]
    pairs = levels // 2
    x, y, z = where_am_i()
    x_first, x_last = one(x == 0), one(x == span_x - 1)
    joint_first = one(y == 0) * one(z == 0)
    joint_last = one(y == span_y - 1) * one(z == span_z - 1)
    row = row_of()
    low_rows = jnp.logical_and(row < 2, flag(1 - x_first))
    high_rows = jnp.logical_and(row >= rows - 2, flag(1 - x_last))
    never = jnp.full((rows, lanes), False)
    fill, terms = x_scratch(packs, scratch)
    tiles = len(ocean_x_fields) * pairs // 4
    first_tile = packs[0].shape[0] - tiles
    fill(range(first_tile, first_tile + tiles))

    def x_ends(t):
        t = 4 * first_tile + t
        return jnp.concatenate([terms(t, low_rows, never), terms(t, never, high_rows)], axis=0)

    wide = (fine, lanes)
    lower = lane_of(wide) < half
    weights_x = stencil(row_of(wide), fine, x_first, x_last)
    weights_y = stencil(
        jnp.bitwise_and(lane_of(wide), half - 1), half, joint_first, joint_last
    )
    states = [[paired_level(ocean, m, k, levels) for k in range(pairs)] for m in range(4)]

    def slope_z(m, k):
        def at(i):
            if 0 <= i < pairs:
                return states[m][i]
            return turn(states[m][i % pairs], half, 1)

        total = (at(k - 2) - at(k + 2) + 8.0 * (at(k + 1) - at(k - 1))) * (1.0 / 12.0)
        if k < 4:
            near = sum(w * at(c) for c, w in enumerate(closure_rows[k]) if w != 0.0)
            total = jnp.where(lower, near, total)
        if pairs - 1 - k < 4:
            near = sum(
                -w * at(pairs - 1 - c)
                for c, w in enumerate(closure_rows[pairs - 1 - k])
                if w != 0.0
            )
            total = jnp.where(lower, total, near)
        return total

    copies = []
    chunk = pairs // 2
    for k in range(pairs):
        bulk = jnp.concatenate([medium[0, k]] * 2, axis=0)
        light = jnp.concatenate([medium[1, k]] * 2, axis=0)
        p, u, v, w = (states[m][k] for m in range(4))
        dxu = slope(u, weights_x, 0) + x_ends(k)
        dxp = slope(p, weights_x, 0) + x_ends(pairs + k)
        dyv = slope(v, weights_y, 1)
        dyp = slope(p, weights_y, 1)
        rate_p = -bulk * (2.0 * (dxu + dyv) + slope_z(3, k)) + gravity * w / light
        rate_w = -light * slope_z(0, k)
        if k == pairs - 1:
            rate_p = rate_p + jnp.where(lower, 0.0, inv_norm * bulk * w)
        if k == 0:
            rate_w = rate_w - jnp.where(lower, inv_norm * light * p, 0.0)
        carry[0, k] = rate_p
        carry[1, k] = -2.0 * light * dyp
        carry[2, k] = p
        carry[3, k] = v
        store_pair(stage_rate, stage_next, 0, k, -2.0 * light * dxp, u)
        store_pair(stage_rate, stage_next, 1, k, rate_w, w)
        if (k + 1) % chunk == 0:
            copies += out_copies(
                ((stage_rate, ocean_rate), (stage_next, ocean_next)),
                (1, 3), k + 1 - chunk, chunk, pairs, sems, len(copies),
            )
    for copy in copies:
        copy.wait()


def store_pair(stage_rate, stage_next, slot, k, rate, state):
    pairs = stage_rate.shape[1] // 2
    rate = step_size * rate
    after = state + section_weight * rate
    stage_rate[slot, k] = rate[:, :half]
    stage_next[slot, k] = after[:, :half]
    stage_rate[slot, k + pairs] = turn(rate, half, 1)[:, :half]
    stage_next[slot, k + pairs] = turn(after, half, 1)[:, :half]


def out_copies(routes, fields, start, chunk, pairs, sems, used):
    copies = []
    for stage, out in routes:
        for slot, field in enumerate(fields):
            for base in (start, start + pairs):
                copies.append(
                    pltpu.make_async_copy(
                        stage.at[slot, pl.ds(base, chunk)],
                        out.at[field, pl.ds(base, chunk)],
                        sems.at[used + len(copies)],
                    )
                )
    run_copies(copies)
    return copies


def relay_kernel(count_x, solid, pressure, got_small, got_ya, got_yb, *refs):
    planes, out = refs[:count_x], refs[-1]
    depth = solid.shape[1]
    _, y, z = where_am_i()
    odd_y = flag(lax.rem(y, 2))
    bottom, second = flag(one(z == 0)), flag(one(z == 1))
    lane = lane_of()
    got_y = (got_ya, got_yb)
    edge_tiles = out_edge_tiles(depth)
    t = y_fields.index(2) * depth
    _, right = sides([g[t // 32] for g in got_y], odd_y)
    right = turn(right, -(4 * (t % 32) + 2), 1)
    _, right_rim = sides([g[edge_tiles + 2] for g in got_y], odd_y)
    first = lane == 0
    plane = jnp.where(first, right, solid[2, 0])
    rim = jnp.where(first, right_rim, rim_tile_of(planes))
    came = got_small[2]
    out[0] = jnp.where(bottom, plane, jnp.where(second, came, came + pressure[0]))
    out[1] = jnp.where(bottom, rim, got_small[3])
    for i in range(2):
        low, high = sides([g[edge_tiles + i] for g in got_y], odd_y)
        out[2 + i] = jnp.where(bottom, high, low)


def out_edge_tiles(depth):
    return -(-len(y_fields) * depth // 32)


def solid_kernel(sizes, solid, material, got_even, got_odd, got_ya, got_yb, *refs):
    packs = refs[:-7]
    solid_next, solid_rate, carry, stage_next, stage_rate, scratch, sems = refs[-7:]
    span_x, span_y, span_z = sizes
    depth = solid.shape[1]
    x, y, z = where_am_i()
    x_first, x_last = one(x == 0), one(x == span_x - 1)
    y_first, y_last = one(y == 0), one(y == span_y - 1)
    odd_y, odd_z = flag(lax.rem(y, 2)), flag(lax.rem(z, 2))
    lane, row = lane_of(), row_of()
    low_rows = jnp.logical_and(row < 2, flag(1 - x_first))
    high_rows = jnp.logical_and(row >= rows - 2, flag(1 - x_last))
    fill, x_terms = x_scratch(packs, scratch)
    fill(range(len(x_fields) * depth // 4))
    y_edges = []
    for i in range(out_edge_tiles(depth)):
        low, high = sides([got_ya[i], got_yb[i]], odd_y)
        y_edges.append(edge_terms(low, high, flag(1 - y_first), flag(1 - y_last)))
    end_lanes = jnp.logical_or(lane < 2, lane >= lanes - 2)

    def y_terms(t):
        return jnp.where(end_lanes, turn(y_edges[t // 32], -(4 * (t % 32) + 2), 1), 0.0)

    weights_x = stencil(row, rows, x_first, x_last)
    weights_y = stencil(lane, lanes, y_first, y_last)
    at_first, at_last = flag(one(z == 0)), flag(one(z == span_z - 1))

    def layer(i, k):
        if 0 <= k < depth:
            return solid[z_fields[i], k]
        j = 2 * i + (k + 2 if k < 0 else k - depth)
        low, high = sides([got_even[j], got_odd[j]], odd_z)
        return low if k < 0 else high

    def slope_z(i, k):
        total = (
            layer(i, k - 2) - layer(i, k + 2) + 8.0 * (layer(i, k + 1) - layer(i, k - 1))
        ) * (1.0 / 12.0)
        if k < 4:
            near = sum(w * layer(i, c) for c, w in enumerate(closure_rows[k]) if w != 0.0)
            total = jnp.where(at_first, near, total)
        if depth - 1 - k < 4:
            near = sum(
                -w * layer(i, depth - 1 - c)
                for c, w in enumerate(closure_rows[depth - 1 - k])
                if w != 0.0
            )
            total = jnp.where(at_last, near, total)
        return total

    copies = []
    for k in range(depth):
        dx = {
            m: slope(solid[m, k], weights_x, 0) + x_terms(i * depth + k, low_rows, high_rows)
            for i, m in enumerate(x_fields)
        }
        dy = {
            m: slope(solid[m, k], weights_y, 1) + y_terms(i * depth + k)
            for i, m in enumerate(y_fields)
        }
        metric = material[3, k]
        dz = {m: metric * slope_z(i, k) for i, m in enumerate(z_fields)}
        buoyancy, lame_one, lame_two = material[0, k], material[1, k], material[2, k]
        dilation = lame_one * (dx[0] + dy[1] + dz[2])
        twice = 2.0 * lame_two
        rates = [
            buoyancy * (dx[3] + dy[8] + dz[7]),
            buoyancy * (dx[8] + dy[4] + dz[6]),
            buoyancy * (dx[7] + dy[6] + dz[5]),
            dilation + twice * dx[0],
            dilation + twice * dy[1],
            dilation + twice * dz[2],
            lame_two * (dz[1] + dy[2]),
            lame_two * (dz[0] + dx[2]),
            lame_two * (dy[0] + dx[1]),
        ]
        if k == 0:
            factor = jnp.where(at_first, inv_norm * buoyancy * metric, 0.0)
            rates[0] = rates[0] + factor * solid[7, 0]
            rates[1] = rates[1] + factor * solid[6, 0]
            carry[0] = rates[2] + factor * solid[5, 0]
            carry[1] = factor
        for m, rate in enumerate(rates):
            rate = step_size * rate
            stage_rate[m, k] = rate
            stage_next[m, k] = solid[m, k] + section_weight * rate
        if k == 0:
            spans = ((0, 2, 0, 1), (3, 6, 0, 1))
        else:
            spans = ((0, 9, k, 1),) if k % 2 else ()
            spans = spans if k < 3 else ((0, 9, k - 1, 2),) if k % 2 else ()
        fresh = []
        for first, count, level, thick in spans:
            at = (pl.ds(first, count), pl.ds(level, thick))
            for stage, out in ((stage_rate, solid_rate), (stage_next, solid_next)):
                n = len(copies) + len(fresh)
                fresh.append(pltpu.make_async_copy(stage.at[at], out.at[at], sems.at[n]))
        run_copies(fresh)
        copies += fresh
    for copy in copies:
        copy.wait()


def last_kernel(
    sizes, solid, medium, pressure, index, ocean_carry, solid_carry,
    got_small, got_odd, got_far, got_ya, got_yb, *refs,
):
    _, span_y, span_z = sizes
    planes = refs[:-13]
    outs = refs[-9:-5]
    solid_next, solid_rate, ocean_next, ocean_rate = outs
    stage_next, stage_rate, vz_next, vz_rate, sems = refs[-5:]
    depth = solid.shape[1]
    pairs, fine = ocean_carry.shape[1:3]
    _, y, z = where_am_i()
    odd_y, odd_z = flag(lax.rem(y, 2)), flag(lax.rem(z, 2))
    bottom, second, top = (flag(one(z == i)) for i in (0, 1, span_z - 1))
    joint_first = one(y == 0) * one(z == 0)
    joint_last = one(y == span_y - 1) * one(z == span_z - 1)
    lane = lane_of()
    ring = 2 * len(z_fields)
    copies = []

    sum_pressure = pressure[0] + got_small[2] + got_far[0]
    rate = step_size * (solid_carry[0] + solid_carry[1] * sum_pressure)
    vz_rate[0, 0] = rate
    vz_next[0, 0] = solid[2, 0] + section_weight * rate
    at = (pl.ds(2, 1), pl.ds(0, 1))
    for stage, out in ((vz_rate, solid_rate), (vz_next, solid_next)):
        copies.append(pltpu.make_async_copy(stage, out.at[at], sems.at[len(copies)]))
    run_copies(copies)

    lows, highs = [], []
    for i in range(2):
        low, high = sides([got_small[i], got_odd[ring + i]], odd_z)
        lows.append(jnp.where(bottom, got_far[2 + i], low))
        highs.append(jnp.where(top, got_far[2 + i], high))
    has_left, has_right = flag(1 - joint_first), flag(1 - joint_last)
    outer = edge_terms(lows[1], highs[1], has_left, has_right)
    inner = edge_terms(lows[0], highs[0], has_left, has_right)
    end_lanes = jnp.logical_or(lane < 2, lane >= lanes - 2)
    mid_lanes = jnp.logical_and(lane >= half - 2, lane < half + 2)

    step = pairs // 2

    def y_ends(t, part):
        parts = []
        for r in range(fine // rows):
            q = t * (fine // rows) + r
            moved = lanes - 4 * (fine // rows) * step * part
            end = pltpu.roll(outer, jnp.bitwise_and(moved - 4 * q - 2, lanes - 1), 1)
            mid = pltpu.roll(inner, jnp.bitwise_and(moved + half - 4 * q - 2, lanes - 1), 1)
            parts.append(jnp.where(end_lanes, end, jnp.where(mid_lanes, mid, 0.0)))
        return jnp.concatenate(parts, axis=0)

    edge_tiles = out_edge_tiles(depth)
    t = y_fields.index(2) * depth
    left, _ = sides([got_ya[t // 32], got_yb[t // 32]], odd_y)
    left = turn(left, lanes - 1 - (4 * (t % 32) + 1), 1)
    left_rim, _ = sides([got_ya[edge_tiles + 2], got_yb[edge_tiles + 2]], odd_y)
    own_rim = rim_tile_of(planes)
    plane = jnp.where(bottom, solid[2, 0], jnp.where(second, got_small[2], got_far[0]))
    rim = jnp.where(bottom, own_rim, jnp.where(second, got_small[3], got_far[1]))
    beside = jnp.where(lane == 0, got_far[0], left)
    beside_rim = jnp.where(lane == 0, got_far[1], left_rim)
    bed_speed = blend_cols(
        blend_rows(plane, rim, index), blend_rows(beside, beside_rim, index), index
    )

    pull = jnp.where(lane_of((fine, lanes)) < half, 0.0, inv_norm * bed_speed)
    pull = pull * jnp.concatenate([medium[0, pairs - 1]] * 2, axis=0)
    routes = [
        (stage, out, slot, field, base)
        for stage, out in ((stage_rate, ocean_rate), (stage_next, ocean_next))
        for slot, field in enumerate((0, 2))
        for base in (0, pairs)
    ]

    def sent(part):
        return [
            pltpu.make_async_copy(
                stage.at[slot, pl.ds(base + part * step, step)],
                out.at[field, pl.ds(base + part * step, step)],
                sems.at[2 + part * len(routes) + i],
            )
            for i, (stage, out, slot, field, base) in enumerate(routes)
        ]

    def half_levels(part, _):
        for j in range(step):
            k = part * step + j
            bulk = jnp.concatenate([medium[0, k]] * 2, axis=0)
            light = jnp.concatenate([medium[1, k]] * 2, axis=0)
            rate_p = ocean_carry[0, k] - 2.0 * bulk * y_ends(j, part)
            if j == step - 1:
                rate_p = rate_p - jnp.where(part == 1, pull, 0.0)
            rate_v = ocean_carry[1, k] - 2.0 * light * y_ends(pairs + j, part)
            store_pair(stage_rate, stage_next, 0, k, rate_p, ocean_carry[2, k])
            store_pair(stage_rate, stage_next, 1, k, rate_v, ocean_carry[3, k])
        run_copies(sent(part))
        return 0

    lax.fori_loop(0, 2, half_levels, 0)
    for copy in copies + sent(0) + sent(1):
        copy.wait()


def compute(solid_state, material, ocean_state, ocean_medium, offset_x, offset_y):
    sizes = tuple(lax.axis_size(axis) for axis in ("gx", "gy", "gz"))
    span_x, span_y, span_z = sizes
    depth = solid_state.shape[1]
    levels, fine, width = ocean_state.shape[1:]
    pairs = levels // 2
    if solid_state.shape[2:] != (rows, lanes) or (fine, width) != (2 * rows, half):
        raise ValueError("tile shape")
    if depth % 4 or levels % 2 or span_z != 4 or span_x % 2 or span_y % 2 or span_y < 4:
        raise ValueError("sizes")
    f32 = jnp.float32
    vmem = pl.BlockSpec(memory_space=pltpu.VMEM)
    smem = pl.BlockSpec(memory_space=pltpu.SMEM)
    hbm = pl.BlockSpec(memory_space=pl.ANY)
    near = lambda x: pltpu.with_memory_space_constraint(x, pltpu.VMEM)
    tiles = lambda *n: pltpu.VMEM((*n, rows, lanes), f32)
    like = lambda a: jax.ShapeDtypeStruct(a.shape, f32)
    dma = pltpu.SemaphoreType.DMA
    material = near(material)
    x_rounds = pair_rounds(span_x)
    count_x = len(x_rounds)
    pack_tiles = (len(x_fields) * depth + len(ocean_x_fields) * pairs) // 4
    edge_tiles = out_edge_tiles(depth)
    layers = 2 * len(z_fields)
    solid, ocean, medium, index = pl.pallas_call(
        functools.partial(stage_kernel, sizes),
        out_shape=[
            pltpu.VMEM(solid_state.shape, f32),
            pltpu.VMEM(ocean_state.shape, f32),
            tiles(2, pairs),
            pltpu.VMEM((4, rows, lanes), jnp.int32),
        ],
        in_specs=[hbm] * 5,
        out_specs=[vmem] * 4,
        scratch_shapes=[
            pltpu.SMEM(ocean_medium.shape, f32),
            pltpu.VMEM((1, fine), jnp.int32),
            pltpu.VMEM((1, width), jnp.int32),
            dma((5,)),
        ],
        name="stage",
    )(
        solid_state,
        ocean_state,
        ocean_medium,
        offset_x.reshape(1, fine),
        offset_y.reshape(1, width),
    )
    solid, ocean = near(solid), near(ocean)
    plane = solid_state[2, 0]
    planes = [lax.ppermute(plane, "gx", p) for p in x_rounds]
    sent_x = pl.pallas_call(
        pack_x_kernel,
        out_shape=[tiles(pack_tiles) for _ in x_rounds],
        in_specs=[vmem] * 2,
        out_specs=[vmem] * count_x,
        name="pack_x",
    )(solid, ocean)
    got_x = [near(lax.ppermute(m, "gx", p)) for m, p in zip(sent_x, x_rounds)]
    sent_y, sent_small, sent_even, sent_odd, pressure = pl.pallas_call(
        pack_kernel,
        out_shape=[tiles(edge_tiles + 3), tiles(4), tiles(layers), tiles(layers + 2), tiles(1)],
        in_specs=[vmem] * 2,
        out_specs=[vmem] * 5,
        name="pack",
    )(solid, ocean)
    pressure, medium, index = map(near, (pressure, medium, index))
    ring = ("gy", "gz")
    places = [(y, z) for y in range(span_y) for z in range(span_z)]

    def over_ring(move):
        return [(y * span_z + z, y2 * span_z + z2)
                for y, z in places for y2, z2 in (move(y, z),)]

    even = over_ring(lambda y, z: (y, z ^ 1))
    inner = over_ring(
        lambda y, z: (y ^ 1, z) if z in (0, span_z - 1) else (y, z + 1 if z % 2 else z - 1)
    )
    ends = over_ring(lambda y, z: (y, span_z - 1 - z))
    rim = row_rims(planes)
    planes = [near(plane) for plane in planes]
    sent_y, sent_small = (m.at[m.shape[0] - 1, :2].set(rim) for m in (sent_y, sent_small))
    rounds_y = pair_rounds(span_y)
    got_ya = near(lax.ppermute(sent_y, "gy", rounds_y[0]))
    got_yb = near(lax.ppermute(sent_y, "gy", rounds_y[1]))
    got_y = (got_ya, got_yb)
    got_small = near(lax.ppermute(sent_small, ring, even))
    got_even = near(lax.ppermute(sent_even, ring, even))
    got_odd = near(lax.ppermute(sent_odd, ring, inner))

    ocean_next, ocean_rate, ocean_carry = pl.pallas_call(
        functools.partial(ocean_kernel, sizes),
        out_shape=[like(ocean_state), like(ocean_state), pltpu.VMEM((4, pairs, fine, lanes), f32)],
        in_specs=[vmem] * (2 + count_x),
        out_specs=[hbm, hbm, vmem],
        scratch_shapes=[
            pltpu.VMEM((2, levels, fine, width), f32),
            pltpu.VMEM((2, levels, fine, width), f32),
            pltpu.VMEM((count_x, pack_tiles, rows, lanes), f32),
            dma((16,)),
        ],
        name="ocean",
    )(ocean, medium, *got_x)

    sent_far = pl.pallas_call(
        functools.partial(relay_kernel, count_x),
        out_shape=tiles(4),
        in_specs=[vmem] * (5 + count_x),
        out_specs=vmem,
        name="relay",
    )(solid, pressure, got_small, *got_y, *planes)
    got_far = near(lax.ppermute(sent_far, ring, ends))

    solid_next, solid_rate, solid_carry = pl.pallas_call(
        functools.partial(solid_kernel, sizes),
        out_shape=[like(solid_state), like(solid_state), tiles(2)],
        in_specs=[vmem] * (6 + count_x),
        out_specs=[hbm, hbm, vmem],
        scratch_shapes=[
            pltpu.VMEM(solid_state.shape, f32),
            pltpu.VMEM(solid_state.shape, f32),
            pltpu.VMEM((count_x, pack_tiles, rows, lanes), f32),
            dma((2 * depth,)),
        ],
        name="solid",
    )(solid, material, got_even, got_odd, *got_y, *got_x)

    return pl.pallas_call(
        functools.partial(last_kernel, sizes),
        out_shape=[like(solid_state), like(solid_state), like(ocean_state), like(ocean_state)],
        in_specs=[vmem] * (11 + count_x) + [hbm] * 4,
        out_specs=[hbm] * 4,
        input_output_aliases={11 + count_x + i: i for i in range(4)},
        scratch_shapes=[
            pltpu.VMEM((2, levels, fine, width), f32),
            pltpu.VMEM((2, levels, fine, width), f32),
            tiles(1, 1),
            tiles(1, 1),
            dma((18,)),
        ],
        name="last",
    )(
        solid, medium, pressure, index, near(ocean_carry), near(solid_carry),
        got_small, got_odd, got_far, *got_y, *planes,
        solid_next, solid_rate, ocean_next, ocean_rate,
    )


def solution(mesh):
    in_specs = (
        P(None, "gz", "gx", "gy"),
        P(None, "gz", "gx", "gy"),
        P(None, None, "gx", ("gy", "gz")),
        P(),
        P("gx"),
        P(("gy", "gz")),
    )
    out_specs = (
        P(None, "gz", "gx", "gy"),
        P(None, "gz", "gx", "gy"),
        P(None, None, "gx", ("gy", "gz")),
        P(None, None, "gx", ("gy", "gz")),
    )
    return jax.shard_map(compute, mesh=mesh, in_specs=in_specs, out_specs=out_specs, check_vma=False)
```

```python
import functools

import jax
import jax.numpy as jnp
from jax import lax
from jax.experimental import pallas as pl
from jax.experimental.pallas import tpu as pltpu
from jax.sharding import PartitionSpec as P


closure_rows = (
    (-24.0 / 17.0, 59.0 / 34.0, -4.0 / 17.0, -3.0 / 34.0, 0.0, 0.0),
    (-0.5, 0.0, 0.5, 0.0, 0.0, 0.0),
    (4.0 / 43.0, -59.0 / 86.0, 0.0, 59.0 / 86.0, -4.0 / 43.0, 0.0),
    (3.0 / 98.0, 0.0, -59.0 / 98.0, 0.0, 32.0 / 49.0, -4.0 / 49.0),
)
inv_norm = 48.0 / 17.0
step_size = 0.25
section_weight = 0.1496590219993
gravity = 0.4
interior_weights = {-2: 1.0 / 12.0, -1: -8.0 / 12.0, 1: 8.0 / 12.0, 2: -1.0 / 12.0}

x_fields = (0, 1, 2, 3, 8, 7)
y_fields = (0, 1, 2, 4, 8, 6)
z_fields = (0, 1, 2, 5, 6, 7)
ocean_x_fields = (1, 0)
ocean_y_fields = (2, 0)
rows, lanes, half = 8, 128, 64
far = 1 << 20


def turn(x, shift, axis):
    shift = shift % x.shape[axis]
    return x if shift == 0 else pltpu.roll(x, shift, axis)


def flag(value, shape=(rows, lanes)):
    return jnp.broadcast_to(value.astype(jnp.int32), shape) == 1


def lane_of(shape=(rows, lanes)):
    return lax.broadcasted_iota(jnp.int32, shape, 1)


def row_of(shape=(rows, lanes)):
    return lax.broadcasted_iota(jnp.int32, shape, 0)


def stencil(position, extent, first, last):
    low = position + far * (1 - first)
    high = extent - 1 - position + far * (1 - last)
    plain = jnp.logical_and(low >= 4, high >= 4)
    weights = {}
    for s in range(-3, 4):
        inside = jnp.logical_and(position + s >= 0, position + s < extent)
        w = jnp.where(jnp.logical_and(inside, plain), interior_weights.get(s, 0.0), 0.0)
        for r in range(4):
            if 0 <= r + s < 6 and closure_rows[r][r + s] != 0.0:
                w = jnp.where(low == r, closure_rows[r][r + s], w)
            if 0 <= r - s < 6 and closure_rows[r][r - s] != 0.0:
                w = jnp.where(high == r, -closure_rows[r][r - s], w)
        weights[s] = w
    return weights


def slope(x, weights, axis):
    total = weights[0] * x
    for s in (-3, -2, -1, 1, 2, 3):
        total = total + weights[s] * turn(x, -s, axis)
    return total


def pack_edges(tiles, offset=2):
    group = lax.shift_right_logical(lane_of(), 2)
    out = []
    for start in range(0, len(tiles), 32):
        acc = jnp.zeros((rows, lanes), jnp.float32)
        for q, tile in enumerate(tiles[start : start + 32]):
            acc = jnp.where(group == q, turn(tile, 4 * q + offset, 1), acc)
        out.append(acc)
    return out


def edge_terms(left, right, has_left, has_right):
    place = jnp.bitwise_and(lane_of(), 3)
    low = jnp.where(
        place == 2, turn(left, 2, 1) - 8.0 * turn(left, 1, 1), turn(left, 2, 1)
    )
    high = jnp.where(
        place == 0, -turn(right, -2, 1), 8.0 * turn(right, -1, 1) - turn(right, -2, 1)
    )
    low = jnp.where(has_left, low, 0.0)
    high = jnp.where(has_right, high, 0.0)
    return jnp.where(place >= 2, low, high) * (1.0 / 12.0)


def row_terms(pack, from_low):
    even = jnp.bitwise_and(row_of(), 1) == 0
    low = jnp.where(even, pack - 8.0 * turn(pack, -1, 0), pack)
    high = jnp.where(even, -pack, 8.0 * turn(pack, 1, 0) - pack)
    return jnp.where(from_low, low, turn(high, 6, 0)) * (1.0 / 12.0)


def pair_rounds(size):
    first = [(i, i ^ 1) for i in range(size)]
    if size == 2:
        return (first,)
    second = [(i, (i + 1) % size if i % 2 else (i - 1) % size) for i in range(size)]
    return (first, second)


def where_am_i():
    return lax.axis_index("gx"), lax.axis_index("gy"), lax.axis_index("gz")


def paired_level(ocean, field, k, levels):
    a = ocean[field, k]
    b = ocean[field, k + levels // 2]
    return jnp.concatenate([a, b], axis=1)


def row_rims(planes):
    if len(planes) == 1:
        return jnp.concatenate([planes[0][-1:], planes[0][:1]], axis=0)
    odd = lax.axis_index("gx") % 2 == 1
    low = jnp.where(odd, planes[0][-1:], planes[1][-1:])
    high = jnp.where(odd, planes[1][:1], planes[0][:1])
    return jnp.concatenate([low, high], axis=0)


def rim_tile_of(planes):
    odd = flag(lax.rem(lax.axis_index("gx"), 2))
    low, high = sides([plane[...] for plane in planes], odd)
    rim = jnp.where(row_of() == 0, turn(low, 1, 0), turn(high, 1, 0))
    return jnp.where(row_of() < 2, rim, 0.0)


def sides(got, odd):
    if len(got) == 1:
        return got[0], got[0]
    return jnp.where(odd, got[0], got[1]), jnp.where(odd, got[1], got[0])


def one(condition):
    return condition.astype(jnp.int32)


def run_copies(copies):
    for copy in copies:
        copy.start()


def stage_kernel(*refs):
    solid_far, ocean_far, medium_far, offset_x_far, offset_y_far = refs[:5]
    solid, ocean, small, offset_x, offset_y, sems = refs[5:]
    copies = [
        pltpu.make_async_copy(solid_far, solid, sems.at[0]),
        pltpu.make_async_copy(ocean_far, ocean, sems.at[1]),
        pltpu.make_async_copy(medium_far, small, sems.at[2]),
        pltpu.make_async_copy(offset_x_far, offset_x, sems.at[3]),
        pltpu.make_async_copy(offset_y_far, offset_y, sems.at[4]),
    ]
    run_copies(copies)
    for copy in copies:
        copy.wait()


def pack_x_kernel(solid, ocean, *outs):
    levels, fine = ocean.shape[1:3]
    depth = solid.shape[1]
    odd = flag(lax.rem(lax.axis_index("gx"), 2))
    pair = lax.shift_right_logical(row_of(), 1)

    def emit(heads, base):
        for number, out in enumerate(outs):
            acc = None
            for t, (head, tail) in enumerate(heads):
                q = t % 4
                edge = jnp.where(odd, head, tail) if number == 0 else jnp.where(odd, tail, head)
                edge = turn(edge, 2 * q, 0)
                acc = edge if q == 0 else jnp.where(pair == q, edge, acc)
                if q == 3:
                    out[base + t // 4] = acc

    heads = []
    for field in x_fields:
        for k in range(depth):
            tile = solid[field, k]
            heads.append((tile, turn(tile, 2, 0)))
    emit(heads, 0)
    base = len(heads) // 4
    heads = []
    for field in ocean_x_fields:
        for k in range(levels // 2):
            tile = paired_level(ocean, field, k, levels)
            heads.append((tile[:rows], turn(tile[fine - rows :], 2, 0)))
    emit(heads, base)


def pack_kernel(solid, ocean, out_y, out_small, out_pressure):
    levels, fine, width = ocean.shape[1:]
    depth = solid.shape[1]
    _, _, z = where_am_i()
    zero = jnp.zeros((rows, lanes), jnp.float32)
    packed = pack_edges([solid[field, k] for field in y_fields for k in range(depth)])
    tiles = []
    for field in ocean_y_fields:
        for k in range(levels // 2):
            tile = paired_level(ocean, field, k, levels)
            tiles += [tile[r : r + rows] for r in range(0, fine, rows)]
    ends = pack_edges(tiles) + pack_edges(tiles, half + 2)
    for i, tile in enumerate(packed + ends + [zero]):
        out_y[i] = tile
    for i, tile in enumerate(ends):
        out_small[i] = tile
    deepest = ocean[0, levels - 1]
    deepest = jnp.concatenate([deepest, deepest], axis=1)
    source = jnp.bitwise_and(2 * row_of(), rows - 1)
    halves = []
    for r in range(2):
        part = deepest[r * rows : (r + 1) * rows]
        halves.append(pick(part + turn(part, -1, 0), source, 0))
    pressure = jnp.where(row_of() < rows // 2, halves[0], halves[1])
    pressure = 0.25 * (pressure + turn(pressure, -1, 1))
    column = lane_of() - z * (width // 2)
    mine = jnp.logical_and(column >= 0, column < width // 2)
    pressure = pick(pressure, jnp.bitwise_and(2 * column, lanes - 1), 1)
    pressure = jnp.where(mine, pressure, 0.0)
    out_pressure[0] = pressure
    out_small[2] = jnp.where(flag(one(z == 0)), solid[2, 0], pressure)
    out_small[3] = zero


def pack_z_kernel(
    sizes, solid, sent_small, medium, offset_x, offset_y, out_even, out_odd, out_medium, out_index
):
    fill_tables(sizes, medium, offset_x, offset_y, out_medium, out_index)
    odd_z = lax.rem(lax.axis_index("gz"), 2)
    depth = solid.shape[1]
    start_even = (1 - odd_z) * (depth - 2)
    start_odd = odd_z * (depth - 2)
    for i, field in enumerate(z_fields):
        for k in range(2):
            out_even[2 * i + k] = solid[field, start_even + k]
            out_odd[2 * i + k] = solid[field, start_odd + k]
    for i in range(2):
        out_odd[2 * len(z_fields) + i] = sent_small[i]


def fill_tables(sizes, medium, offset_x, offset_y, out_medium, out_index):
    span_x, span_y, _ = sizes
    fine, width = offset_x.shape[1], offset_y.shape[1]
    pairs = out_medium.shape[1]
    x, y, z = where_am_i()
    lane, row = lane_of(), row_of()
    lower = lane < half
    for m in range(2):
        values = jnp.concatenate([medium[m : m + 1, :]] * (lanes // (2 * pairs)), axis=1)
        values = jnp.broadcast_to(values, (rows, lanes))
        for k in range(pairs):
            out_medium[m, k] = pick(values, jnp.where(lower, k, k + pairs), 1)

    moves = jnp.concatenate([offset_x[...].astype(jnp.float32)] * (lanes // fine), axis=1)
    moves = jnp.broadcast_to(moves, (rows, lanes))
    for r in range(2):
        place = row + r * rows
        move = jnp.sum(jnp.where(lane == place, moves, 0.0), axis=1, keepdims=True)
        target = lax.shift_right_logical(place, 1) + move.astype(jnp.int32)
        out_index[r] = jnp.clip(target, -(x * rows), (span_x - x) * rows - 1)
    coarse = lax.shift_right_logical(jnp.bitwise_and(lane, half - 1), 1) + z * (width // 2)
    move = jnp.concatenate([offset_y[...], offset_y[...]], axis=1)
    out_index[2] = coarse
    out_index[3] = jnp.clip(
        coarse + jnp.broadcast_to(move, (rows, lanes)), -(y * lanes), (span_y - y) * lanes - 1
    )


def pick(x, index, axis):
    return jnp.take_along_axis(x, index, axis=axis)


def blend_rows(plane, rim, index):
    parts = []
    for r in range(2):
        near = pick(plane, lax.shift_right_logical(row_of() + r * rows, 1), 0)
        target = index[r]
        inside = jnp.logical_and(target >= 0, target < rows)
        beyond = jnp.where(target < 0, rim[0:1], rim[1:2])
        other = jnp.where(inside, pick(plane, jnp.bitwise_and(target, rows - 1), 0), beyond)
        parts.append(0.75 * near + 0.25 * other)
    return parts


def blend_cols(inside, beside, index):
    near, target = index[2], index[3]
    at_home = jnp.logical_and(target >= 0, target < lanes)
    source = jnp.bitwise_and(target, lanes - 1)
    parts = []
    for own, other in zip(inside, beside):
        far_value = jnp.where(at_home, pick(own, source, 1), pick(other, source, 1))
        parts.append(0.75 * pick(own, near, 1) + 0.25 * far_value)
    return jnp.concatenate(parts, axis=0)


def x_scratch(packs, scratch):
    odd = flag(lax.rem(lax.axis_index("gx"), 2))
    yes = jnp.full((rows, lanes), True)

    def fill(tiles):
        for i in tiles:
            low, high = sides([pack[i] for pack in packs], odd)
            if len(packs) == 1:
                scratch[0, i] = row_terms(low, odd)
            else:
                scratch[0, i] = row_terms(low, yes)
                scratch[1, i] = row_terms(high, jnp.logical_not(yes))

    def terms(t, mask_low, mask_high):
        q = t % 4
        tile = turn(scratch[0, t // 4], -2 * q, 0)
        if len(packs) == 1:
            return jnp.where(jnp.logical_or(mask_low, mask_high), tile, 0.0)
        high = turn(scratch[1, t // 4], -2 * q, 0)
        return jnp.where(mask_low, tile, jnp.where(mask_high, high, 0.0))

    return fill, terms


def ocean_kernel(sizes, ocean, medium, *refs):
    packs = refs[:-7]
    ocean_next, ocean_rate, carry, stage_next, stage_rate, scratch, sems = refs[-7:]
    span_x, span_y, span_z = sizes
    levels, fine, _ = ocean.shape[1:]
    pairs = levels // 2
    x, y, z = where_am_i()
    x_first, x_last = one(x == 0), one(x == span_x - 1)
    joint_first = one(y == 0) * one(z == 0)
    joint_last = one(y == span_y - 1) * one(z == span_z - 1)
    row = row_of()
    low_rows = jnp.logical_and(row < 2, flag(1 - x_first))
    high_rows = jnp.logical_and(row >= rows - 2, flag(1 - x_last))
    never = jnp.full((rows, lanes), False)
    fill, terms = x_scratch(packs, scratch)
    tiles = len(ocean_x_fields) * pairs // 4
    first_tile = packs[0].shape[0] - tiles
    fill(range(first_tile, first_tile + tiles))

    def x_ends(t):
        t = 4 * first_tile + t
        return jnp.concatenate([terms(t, low_rows, never), terms(t, never, high_rows)], axis=0)

    wide = (fine, lanes)
    lower = lane_of(wide) < half
    weights_x = stencil(row_of(wide), fine, x_first, x_last)
    weights_y = stencil(
        jnp.bitwise_and(lane_of(wide), half - 1), half, joint_first, joint_last
    )
    states = [[paired_level(ocean, m, k, levels) for k in range(pairs)] for m in range(4)]

    def slope_z(m, k):
        def at(i):
            if 0 <= i < pairs:
                return states[m][i]
            return turn(states[m][i % pairs], half, 1)

        total = (at(k - 2) - at(k + 2) + 8.0 * (at(k + 1) - at(k - 1))) * (1.0 / 12.0)
        if k < 4:
            near = sum(w * at(c) for c, w in enumerate(closure_rows[k]) if w != 0.0)
            total = jnp.where(lower, near, total)
        if pairs - 1 - k < 4:
            near = sum(
                -w * at(pairs - 1 - c)
                for c, w in enumerate(closure_rows[pairs - 1 - k])
                if w != 0.0
            )
            total = jnp.where(lower, total, near)
        return total

    copies = []
    chunk = pairs // 2
    for k in range(pairs):
        bulk = jnp.concatenate([medium[0, k]] * 2, axis=0)
        light = jnp.concatenate([medium[1, k]] * 2, axis=0)
        p, u, v, w = (states[m][k] for m in range(4))
        dxu = slope(u, weights_x, 0) + x_ends(k)
        dxp = slope(p, weights_x, 0) + x_ends(pairs + k)
        dyv = slope(v, weights_y, 1)
        dyp = slope(p, weights_y, 1)
        rate_p = -bulk * (2.0 * (dxu + dyv) + slope_z(3, k)) + gravity * w / light
        rate_w = -light * slope_z(0, k)
        if k == pairs - 1:
            rate_p = rate_p + jnp.where(lower, 0.0, inv_norm * bulk * w)
        if k == 0:
            rate_w = rate_w - jnp.where(lower, inv_norm * light * p, 0.0)
        carry[0, k] = rate_p
        carry[1, k] = -2.0 * light * dyp
        carry[2, k] = p
        carry[3, k] = v
        store_pair(stage_rate, stage_next, 0, k, -2.0 * light * dxp, u)
        store_pair(stage_rate, stage_next, 1, k, rate_w, w)
        if (k + 1) % chunk == 0:
            copies += out_copies(
                ((stage_rate, ocean_rate), (stage_next, ocean_next)),
                (1, 3), k + 1 - chunk, chunk, pairs, sems, len(copies),
            )
    for copy in copies:
        copy.wait()


def store_pair(stage_rate, stage_next, slot, k, rate, state):
    pairs = stage_rate.shape[1] // 2
    rate = step_size * rate
    after = state + section_weight * rate
    stage_rate[slot, k] = rate[:, :half]
    stage_next[slot, k] = after[:, :half]
    stage_rate[slot, k + pairs] = turn(rate, half, 1)[:, :half]
    stage_next[slot, k + pairs] = turn(after, half, 1)[:, :half]


def out_copies(routes, fields, start, chunk, pairs, sems, used):
    copies = []
    for stage, out in routes:
        for slot, field in enumerate(fields):
            for base in (start, start + pairs):
                copies.append(
                    pltpu.make_async_copy(
                        stage.at[slot, pl.ds(base, chunk)],
                        out.at[field, pl.ds(base, chunk)],
                        sems.at[used + len(copies)],
                    )
                )
    run_copies(copies)
    return copies


def relay_kernel(count_x, solid, pressure, got_small, got_ya, got_yb, *refs):
    planes, out = refs[:count_x], refs[-1]
    depth = solid.shape[1]
    _, y, z = where_am_i()
    odd_y = flag(lax.rem(y, 2))
    bottom, second = flag(one(z == 0)), flag(one(z == 1))
    lane = lane_of()
    got_y = (got_ya, got_yb)
    edge_tiles = out_edge_tiles(depth)
    t = y_fields.index(2) * depth
    _, right = sides([g[t // 32] for g in got_y], odd_y)
    right = turn(right, -(4 * (t % 32) + 2), 1)
    _, right_rim = sides([g[edge_tiles + 2] for g in got_y], odd_y)
    first = lane == 0
    plane = jnp.where(first, right, solid[2, 0])
    rim = jnp.where(first, right_rim, rim_tile_of(planes))
    came = got_small[2]
    out[0] = jnp.where(bottom, plane, jnp.where(second, came, came + pressure[0]))
    out[1] = jnp.where(bottom, rim, got_small[3])
    for i in range(2):
        low, high = sides([g[edge_tiles + i] for g in got_y], odd_y)
        out[2 + i] = jnp.where(bottom, high, low)


def out_edge_tiles(depth):
    return -(-len(y_fields) * depth // 32)


def solid_kernel(sizes, solid, material, got_even, got_odd, got_ya, got_yb, *refs):
    packs = refs[:-7]
    solid_next, solid_rate, carry, stage_next, stage_rate, scratch, sems = refs[-7:]
    span_x, span_y, span_z = sizes
    depth = solid.shape[1]
    x, y, z = where_am_i()
    x_first, x_last = one(x == 0), one(x == span_x - 1)
    y_first, y_last = one(y == 0), one(y == span_y - 1)
    odd_y, odd_z = flag(lax.rem(y, 2)), flag(lax.rem(z, 2))
    lane, row = lane_of(), row_of()
    low_rows = jnp.logical_and(row < 2, flag(1 - x_first))
    high_rows = jnp.logical_and(row >= rows - 2, flag(1 - x_last))
    fill, x_terms = x_scratch(packs, scratch)
    fill(range(len(x_fields) * depth // 4))
    y_edges = []
    for i in range(out_edge_tiles(depth)):
        low, high = sides([got_ya[i], got_yb[i]], odd_y)
        y_edges.append(edge_terms(low, high, flag(1 - y_first), flag(1 - y_last)))
    end_lanes = jnp.logical_or(lane < 2, lane >= lanes - 2)

    def y_terms(t):
        return jnp.where(end_lanes, turn(y_edges[t // 32], -(4 * (t % 32) + 2), 1), 0.0)

    weights_x = stencil(row, rows, x_first, x_last)
    weights_y = stencil(lane, lanes, y_first, y_last)
    at_first, at_last = flag(one(z == 0)), flag(one(z == span_z - 1))

    def layer(i, k):
        if 0 <= k < depth:
            return solid[z_fields[i], k]
        j = 2 * i + (k + 2 if k < 0 else k - depth)
        low, high = sides([got_even[j], got_odd[j]], odd_z)
        return low if k < 0 else high

    def slope_z(i, k):
        total = (
            layer(i, k - 2) - layer(i, k + 2) + 8.0 * (layer(i, k + 1) - layer(i, k - 1))
        ) * (1.0 / 12.0)
        if k < 4:
            near = sum(w * layer(i, c) for c, w in enumerate(closure_rows[k]) if w != 0.0)
            total = jnp.where(at_first, near, total)
        if depth - 1 - k < 4:
            near = sum(
                -w * layer(i, depth - 1 - c)
                for c, w in enumerate(closure_rows[depth - 1 - k])
                if w != 0.0
            )
            total = jnp.where(at_last, near, total)
        return total

    copies = []
    for k in range(depth):
        dx = {
            m: slope(solid[m, k], weights_x, 0) + x_terms(i * depth + k, low_rows, high_rows)
            for i, m in enumerate(x_fields)
        }
        dy = {
            m: slope(solid[m, k], weights_y, 1) + y_terms(i * depth + k)
            for i, m in enumerate(y_fields)
        }
        metric = material[3, k]
        dz = {m: metric * slope_z(i, k) for i, m in enumerate(z_fields)}
        buoyancy, lame_one, lame_two = material[0, k], material[1, k], material[2, k]
        dilation = lame_one * (dx[0] + dy[1] + dz[2])
        twice = 2.0 * lame_two
        rates = [
            buoyancy * (dx[3] + dy[8] + dz[7]),
            buoyancy * (dx[8] + dy[4] + dz[6]),
            buoyancy * (dx[7] + dy[6] + dz[5]),
            dilation + twice * dx[0],
            dilation + twice * dy[1],
            dilation + twice * dz[2],
            lame_two * (dz[1] + dy[2]),
            lame_two * (dz[0] + dx[2]),
            lame_two * (dy[0] + dx[1]),
        ]
        if k == 0:
            factor = jnp.where(at_first, inv_norm * buoyancy * metric, 0.0)
            rates[0] = rates[0] + factor * solid[7, 0]
            rates[1] = rates[1] + factor * solid[6, 0]
            carry[0] = rates[2] + factor * solid[5, 0]
            carry[1] = factor
        for m, rate in enumerate(rates):
            rate = step_size * rate
            stage_rate[m, k] = rate
            stage_next[m, k] = solid[m, k] + section_weight * rate
        if k == 0:
            spans = ((0, 2, 0, 1), (3, 6, 0, 1))
        else:
            spans = ((0, 9, k, 1),) if k % 2 else ()
            spans = spans if k < 3 else ((0, 9, k - 1, 2),) if k % 2 else ()
        fresh = []
        for first, count, level, thick in spans:
            at = (pl.ds(first, count), pl.ds(level, thick))
            for stage, out in ((stage_rate, solid_rate), (stage_next, solid_next)):
                n = len(copies) + len(fresh)
                fresh.append(pltpu.make_async_copy(stage.at[at], out.at[at], sems.at[n]))
        run_copies(fresh)
        copies += fresh
    for copy in copies:
        copy.wait()


def last_kernel(
    sizes, solid, medium, pressure, index, ocean_carry, solid_carry,
    got_small, got_odd, got_far, got_ya, got_yb, *refs,
):
    _, span_y, span_z = sizes
    planes = refs[:-13]
    outs = refs[-9:-5]
    solid_next, solid_rate, ocean_next, ocean_rate = outs
    stage_next, stage_rate, vz_next, vz_rate, sems = refs[-5:]
    depth = solid.shape[1]
    pairs, fine = ocean_carry.shape[1:3]
    _, y, z = where_am_i()
    odd_y, odd_z = flag(lax.rem(y, 2)), flag(lax.rem(z, 2))
    bottom, second, top = (flag(one(z == i)) for i in (0, 1, span_z - 1))
    joint_first = one(y == 0) * one(z == 0)
    joint_last = one(y == span_y - 1) * one(z == span_z - 1)
    lane = lane_of()
    ring = 2 * len(z_fields)
    copies = []

    sum_pressure = pressure[0] + got_small[2] + got_far[0]
    rate = step_size * (solid_carry[0] + solid_carry[1] * sum_pressure)
    vz_rate[0, 0] = rate
    vz_next[0, 0] = solid[2, 0] + section_weight * rate
    at = (pl.ds(2, 1), pl.ds(0, 1))
    for stage, out in ((vz_rate, solid_rate), (vz_next, solid_next)):
        copies.append(pltpu.make_async_copy(stage, out.at[at], sems.at[len(copies)]))
    run_copies(copies)

    lows, highs = [], []
    for i in range(2):
        low, high = sides([got_small[i], got_odd[ring + i]], odd_z)
        lows.append(jnp.where(bottom, got_far[2 + i], low))
        highs.append(jnp.where(top, got_far[2 + i], high))
    has_left, has_right = flag(1 - joint_first), flag(1 - joint_last)
    outer = edge_terms(lows[1], highs[1], has_left, has_right)
    inner = edge_terms(lows[0], highs[0], has_left, has_right)
    end_lanes = jnp.logical_or(lane < 2, lane >= lanes - 2)
    mid_lanes = jnp.logical_and(lane >= half - 2, lane < half + 2)

    def y_ends(t):
        parts = []
        for r in range(fine // rows):
            q = t * (fine // rows) + r
            end = turn(outer, -4 * q - 2, 1)
            mid = turn(inner, half - 4 * q - 2, 1)
            parts.append(jnp.where(end_lanes, end, jnp.where(mid_lanes, mid, 0.0)))
        return jnp.concatenate(parts, axis=0)

    edge_tiles = out_edge_tiles(depth)
    t = y_fields.index(2) * depth
    left, _ = sides([got_ya[t // 32], got_yb[t // 32]], odd_y)
    left = turn(left, lanes - 1 - (4 * (t % 32) + 1), 1)
    left_rim, _ = sides([got_ya[edge_tiles + 2], got_yb[edge_tiles + 2]], odd_y)
    own_rim = rim_tile_of(planes)
    plane = jnp.where(bottom, solid[2, 0], jnp.where(second, got_small[2], got_far[0]))
    rim = jnp.where(bottom, own_rim, jnp.where(second, got_small[3], got_far[1]))
    beside = jnp.where(lane == 0, got_far[0], left)
    beside_rim = jnp.where(lane == 0, got_far[1], left_rim)
    bed_speed = blend_cols(
        blend_rows(plane, rim, index), blend_rows(beside, beside_rim, index), index
    )

    pull = jnp.where(lane_of((fine, lanes)) < half, 0.0, inv_norm * bed_speed)
    pull = pull * jnp.concatenate([medium[0, pairs - 1]] * 2, axis=0)
    for slot, field in ((1, 2), (0, 0)):
        for k in range(pairs):
            scale = jnp.concatenate([medium[slot, k]] * 2, axis=0)
            ends = y_ends((pairs if slot else 0) + k)
            rate = ocean_carry[slot, k] - 2.0 * scale * ends
            if slot == 0 and k == pairs - 1:
                rate = rate - pull
            store_pair(stage_rate, stage_next, slot, k, rate, ocean_carry[2 + slot, k])
        fresh = [
            pltpu.make_async_copy(stage.at[slot], out.at[field], sems.at[len(copies) + i])
            for i, (stage, out) in enumerate(
                ((stage_rate, ocean_rate), (stage_next, ocean_next))
            )
        ]
        run_copies(fresh)
        copies += fresh
    for copy in copies:
        copy.wait()


def compute(solid_state, material, ocean_state, ocean_medium, offset_x, offset_y):
    sizes = tuple(lax.axis_size(axis) for axis in ("gx", "gy", "gz"))
    span_x, span_y, span_z = sizes
    depth = solid_state.shape[1]
    levels, fine, width = ocean_state.shape[1:]
    pairs = levels // 2
    if solid_state.shape[2:] != (rows, lanes) or (fine, width) != (2 * rows, half):
        raise ValueError("tile shape")
    if depth % 4 or levels % 2 or span_z != 4 or span_x % 2 or span_y % 2 or span_y < 4:
        raise ValueError("sizes")
    f32 = jnp.float32
    vmem = pl.BlockSpec(memory_space=pltpu.VMEM)
    smem = pl.BlockSpec(memory_space=pltpu.SMEM)
    hbm = pl.BlockSpec(memory_space=pl.ANY)
    near = lambda x: pltpu.with_memory_space_constraint(x, pltpu.VMEM)
    tiles = lambda *n: pltpu.VMEM((*n, rows, lanes), f32)
    like = lambda a: jax.ShapeDtypeStruct(a.shape, f32)
    dma = pltpu.SemaphoreType.DMA
    material = near(material)
    x_rounds = pair_rounds(span_x)
    count_x = len(x_rounds)
    pack_tiles = (len(x_fields) * depth + len(ocean_x_fields) * pairs) // 4
    edge_tiles = out_edge_tiles(depth)
    layers = 2 * len(z_fields)
    solid, ocean, small, move_x, move_y = pl.pallas_call(
        stage_kernel,
        out_shape=[
            pltpu.VMEM(solid_state.shape, f32),
            pltpu.VMEM(ocean_state.shape, f32),
            pltpu.VMEM(ocean_medium.shape, f32),
            pltpu.VMEM((1, fine), jnp.int32),
            pltpu.VMEM((1, width), jnp.int32),
        ],
        in_specs=[hbm] * 5,
        out_specs=[vmem] * 5,
        scratch_shapes=[dma((5,))],
        name="stage",
    )(
        solid_state,
        ocean_state,
        ocean_medium,
        offset_x.reshape(1, fine),
        offset_y.reshape(1, width),
    )
    solid, ocean = near(solid), near(ocean)
    plane = solid_state[2, 0]
    planes = [lax.ppermute(plane, "gx", p) for p in x_rounds]
    sent_x = pl.pallas_call(
        pack_x_kernel,
        out_shape=[tiles(pack_tiles) for _ in x_rounds],
        in_specs=[vmem] * 2,
        out_specs=[vmem] * count_x,
        name="pack_x",
    )(solid, ocean)
    got_x = [near(lax.ppermute(m, "gx", p)) for m, p in zip(sent_x, x_rounds)]
    sent_y, sent_small, pressure = pl.pallas_call(
        pack_kernel,
        out_shape=[tiles(edge_tiles + 3), tiles(4), tiles(1)],
        in_specs=[vmem] * 2,
        out_specs=[vmem] * 3,
        name="pack",
    )(solid, ocean)
    pressure = near(pressure)
    ring = ("gy", "gz")
    places = [(y, z) for y in range(span_y) for z in range(span_z)]

    def over_ring(move):
        return [(y * span_z + z, y2 * span_z + z2)
                for y, z in places for y2, z2 in (move(y, z),)]

    even = over_ring(lambda y, z: (y, z ^ 1))
    inner = over_ring(
        lambda y, z: (y ^ 1, z) if z in (0, span_z - 1) else (y, z + 1 if z % 2 else z - 1)
    )
    ends = over_ring(lambda y, z: (y, span_z - 1 - z))
    rim = row_rims(planes)
    planes = [near(plane) for plane in planes]
    sent_y, sent_small = (m.at[m.shape[0] - 1, :2].set(rim) for m in (sent_y, sent_small))
    sent_even, sent_odd, medium, index = pl.pallas_call(
        functools.partial(pack_z_kernel, sizes),
        out_shape=[
            tiles(layers),
            tiles(layers + 2),
            tiles(2, pairs),
            pltpu.VMEM((4, rows, lanes), jnp.int32),
        ],
        in_specs=[vmem] * 5,
        out_specs=[vmem] * 4,
        name="pack_z",
    )(solid, near(sent_small), near(small), near(move_x), near(move_y))
    medium, index = near(medium), near(index)
    rounds_y = pair_rounds(span_y)
    got_ya = near(lax.ppermute(sent_y, "gy", rounds_y[0]))
    got_yb = near(lax.ppermute(sent_y, "gy", rounds_y[1]))
    got_y = (got_ya, got_yb)
    got_small = near(lax.ppermute(sent_small, ring, even))
    got_even = near(lax.ppermute(sent_even, ring, even))
    got_odd = near(lax.ppermute(sent_odd, ring, inner))

    ocean_next, ocean_rate, ocean_carry = pl.pallas_call(
        functools.partial(ocean_kernel, sizes),
        out_shape=[like(ocean_state), like(ocean_state), pltpu.VMEM((4, pairs, fine, lanes), f32)],
        in_specs=[vmem] * (2 + count_x),
        out_specs=[hbm, hbm, vmem],
        scratch_shapes=[
            pltpu.VMEM((2, levels, fine, width), f32),
            pltpu.VMEM((2, levels, fine, width), f32),
            pltpu.VMEM((count_x, pack_tiles, rows, lanes), f32),
            dma((16,)),
        ],
        name="ocean",
    )(ocean, medium, *got_x)

    sent_far = pl.pallas_call(
        functools.partial(relay_kernel, count_x),
        out_shape=tiles(4),
        in_specs=[vmem] * (5 + count_x),
        out_specs=vmem,
        name="relay",
    )(solid, pressure, got_small, *got_y, *planes)
    got_far = near(lax.ppermute(sent_far, ring, ends))

    solid_next, solid_rate, solid_carry = pl.pallas_call(
        functools.partial(solid_kernel, sizes),
        out_shape=[like(solid_state), like(solid_state), tiles(2)],
        in_specs=[vmem] * (6 + count_x),
        out_specs=[hbm, hbm, vmem],
        scratch_shapes=[
            pltpu.VMEM(solid_state.shape, f32),
            pltpu.VMEM(solid_state.shape, f32),
            pltpu.VMEM((count_x, pack_tiles, rows, lanes), f32),
            dma((2 * depth,)),
        ],
        name="solid",
    )(solid, material, got_even, got_odd, *got_y, *got_x)

    return pl.pallas_call(
        functools.partial(last_kernel, sizes),
        out_shape=[like(solid_state), like(solid_state), like(ocean_state), like(ocean_state)],
        in_specs=[vmem] * (11 + count_x) + [hbm] * 4,
        out_specs=[hbm] * 4,
        input_output_aliases={11 + count_x + i: i for i in range(4)},
        scratch_shapes=[
            pltpu.VMEM((2, levels, fine, width), f32),
            pltpu.VMEM((2, levels, fine, width), f32),
            tiles(1, 1),
            tiles(1, 1),
            dma((6,)),
        ],
        name="last",
    )(
        solid, medium, pressure, index, near(ocean_carry), near(solid_carry),
        got_small, got_odd, got_far, *got_y, *planes,
        solid_next, solid_rate, ocean_next, ocean_rate,
    )


def solution(mesh):
    in_specs = (
        P(None, "gz", "gx", "gy"),
        P(None, "gz", "gx", "gy"),
        P(None, None, "gx", ("gy", "gz")),
        P(),
        P("gx"),
        P(("gy", "gz")),
    )
    out_specs = (
        P(None, "gz", "gx", "gy"),
        P(None, "gz", "gx", "gy"),
        P(None, None, "gx", ("gy", "gz")),
        P(None, None, "gx", ("gy", "gz")),
    )
    return jax.shard_map(compute, mesh=mesh, in_specs=in_specs, out_specs=out_specs, check_vma=False)
```

```python
import functools

import jax
import jax.numpy as jnp
from jax import lax
from jax.experimental import pallas as pl
from jax.experimental.pallas import tpu as pltpu
from jax.sharding import PartitionSpec as P


closure_rows = (
    (-24.0 / 17.0, 59.0 / 34.0, -4.0 / 17.0, -3.0 / 34.0, 0.0, 0.0),
    (-0.5, 0.0, 0.5, 0.0, 0.0, 0.0),
    (4.0 / 43.0, -59.0 / 86.0, 0.0, 59.0 / 86.0, -4.0 / 43.0, 0.0),
    (3.0 / 98.0, 0.0, -59.0 / 98.0, 0.0, 32.0 / 49.0, -4.0 / 49.0),
)
inv_norm = 48.0 / 17.0
step_size = 0.25
section_weight = 0.1496590219993
gravity = 0.4
interior_weights = {-2: 1.0 / 12.0, -1: -8.0 / 12.0, 1: 8.0 / 12.0, 2: -1.0 / 12.0}

x_fields = (0, 1, 2, 3, 8, 7)
y_fields = (0, 1, 2, 4, 8, 6)
z_fields = (0, 1, 2, 5, 6, 7)
ocean_x_fields = (1, 0)
ocean_y_fields = (2, 0)
rows, lanes, half = 8, 128, 64
far = 1 << 20


def turn(x, shift, axis):
    shift = shift % x.shape[axis]
    return x if shift == 0 else pltpu.roll(x, shift, axis)


def flag(value, shape=(rows, lanes)):
    return jnp.broadcast_to(value.astype(jnp.int32), shape) == 1


def lane_of(shape=(rows, lanes)):
    return lax.broadcasted_iota(jnp.int32, shape, 1)


def row_of(shape=(rows, lanes)):
    return lax.broadcasted_iota(jnp.int32, shape, 0)


def stencil(position, extent, first, last):
    low = position + far * (1 - first)
    high = extent - 1 - position + far * (1 - last)
    plain = jnp.logical_and(low >= 4, high >= 4)
    weights = {}
    for s in range(-3, 4):
        inside = jnp.logical_and(position + s >= 0, position + s < extent)
        w = jnp.where(jnp.logical_and(inside, plain), interior_weights.get(s, 0.0), 0.0)
        for r in range(4):
            if 0 <= r + s < 6 and closure_rows[r][r + s] != 0.0:
                w = jnp.where(low == r, closure_rows[r][r + s], w)
            if 0 <= r - s < 6 and closure_rows[r][r - s] != 0.0:
                w = jnp.where(high == r, -closure_rows[r][r - s], w)
        weights[s] = w
    return weights


def slope(x, weights, axis):
    total = weights[0] * x
    for s in (-3, -2, -1, 1, 2, 3):
        total = total + weights[s] * turn(x, -s, axis)
    return total


def pack_edges(tiles, offset=2):
    group = lax.shift_right_logical(lane_of(), 2)
    out = []
    for start in range(0, len(tiles), 32):
        acc = jnp.zeros((rows, lanes), jnp.float32)
        for q, tile in enumerate(tiles[start : start + 32]):
            acc = jnp.where(group == q, turn(tile, 4 * q + offset, 1), acc)
        out.append(acc)
    return out


def edge_terms(left, right, has_left, has_right):
    place = jnp.bitwise_and(lane_of(), 3)
    low = jnp.where(
        place == 2, turn(left, 2, 1) - 8.0 * turn(left, 1, 1), turn(left, 2, 1)
    )
    high = jnp.where(
        place == 0, -turn(right, -2, 1), 8.0 * turn(right, -1, 1) - turn(right, -2, 1)
    )
    low = jnp.where(has_left, low, 0.0)
    high = jnp.where(has_right, high, 0.0)
    return jnp.where(place >= 2, low, high) * (1.0 / 12.0)


def row_terms(pack, from_low):
    even = jnp.bitwise_and(row_of(), 1) == 0
    low = jnp.where(even, pack - 8.0 * turn(pack, -1, 0), pack)
    high = jnp.where(even, -pack, 8.0 * turn(pack, 1, 0) - pack)
    return jnp.where(from_low, low, turn(high, 6, 0)) * (1.0 / 12.0)


def pair_rounds(size):
    first = [(i, i ^ 1) for i in range(size)]
    if size == 2:
        return (first,)
    second = [(i, (i + 1) % size if i % 2 else (i - 1) % size) for i in range(size)]
    return (first, second)


def where_am_i():
    return lax.axis_index("gx"), lax.axis_index("gy"), lax.axis_index("gz")


def paired_level(ocean, field, k, levels):
    a = ocean[field, k]
    b = ocean[field, k + levels // 2]
    return jnp.concatenate([a, b], axis=1)


def row_rims(planes):
    if len(planes) == 1:
        return jnp.concatenate([planes[0][-1:], planes[0][:1]], axis=0)
    odd = lax.axis_index("gx") % 2 == 1
    low = jnp.where(odd, planes[0][-1:], planes[1][-1:])
    high = jnp.where(odd, planes[1][:1], planes[0][:1])
    return jnp.concatenate([low, high], axis=0)


def rim_tile_of(planes):
    odd = flag(lax.rem(lax.axis_index("gx"), 2))
    low, high = sides([plane[...] for plane in planes], odd)
    rim = jnp.where(row_of() == 0, turn(low, 1, 0), turn(high, 1, 0))
    return jnp.where(row_of() < 2, rim, 0.0)


def sides(got, odd):
    if len(got) == 1:
        return got[0], got[0]
    return jnp.where(odd, got[0], got[1]), jnp.where(odd, got[1], got[0])


def one(condition):
    return condition.astype(jnp.int32)


def run_copies(copies):
    for copy in copies:
        copy.start()


def stage_kernel(*refs):
    solid_far, ocean_far, medium_far, offset_x_far, offset_y_far = refs[:5]
    solid, ocean, small, offset_x, offset_y, sems = refs[5:]
    copies = [
        pltpu.make_async_copy(solid_far, solid, sems.at[0]),
        pltpu.make_async_copy(ocean_far.at[pl.ds(0, 3)], ocean, sems.at[1]),
        pltpu.make_async_copy(medium_far, small, sems.at[2]),
        pltpu.make_async_copy(offset_x_far, offset_x, sems.at[3]),
        pltpu.make_async_copy(offset_y_far, offset_y, sems.at[4]),
    ]
    run_copies(copies)
    for copy in copies:
        copy.wait()


def pack_x_kernel(solid, ocean, *outs):
    levels, fine = ocean.shape[1:3]
    depth = solid.shape[1]
    odd = flag(lax.rem(lax.axis_index("gx"), 2))
    pair = lax.shift_right_logical(row_of(), 1)

    def emit(heads, base):
        for number, out in enumerate(outs):
            acc = None
            for t, (head, tail) in enumerate(heads):
                q = t % 4
                edge = jnp.where(odd, head, tail) if number == 0 else jnp.where(odd, tail, head)
                edge = turn(edge, 2 * q, 0)
                acc = edge if q == 0 else jnp.where(pair == q, edge, acc)
                if q == 3:
                    out[base + t // 4] = acc

    heads = []
    for field in x_fields:
        for k in range(depth):
            tile = solid[field, k]
            heads.append((tile, turn(tile, 2, 0)))
    emit(heads, 0)
    base = len(heads) // 4
    heads = []
    for field in ocean_x_fields:
        for k in range(levels // 2):
            tile = paired_level(ocean, field, k, levels)
            heads.append((tile[:rows], turn(tile[fine - rows :], 2, 0)))
    emit(heads, base)


def pack_kernel(solid, ocean, out_y, out_small, out_pressure):
    levels, fine, width = ocean.shape[1:]
    depth = solid.shape[1]
    _, _, z = where_am_i()
    zero = jnp.zeros((rows, lanes), jnp.float32)
    packed = pack_edges([solid[field, k] for field in y_fields for k in range(depth)])
    tiles = []
    for field in ocean_y_fields:
        for k in range(levels // 2):
            tile = paired_level(ocean, field, k, levels)
            tiles += [tile[r : r + rows] for r in range(0, fine, rows)]
    ends = pack_edges(tiles) + pack_edges(tiles, half + 2)
    for i, tile in enumerate(packed + ends + [zero]):
        out_y[i] = tile
    for i, tile in enumerate(ends):
        out_small[i] = tile
    deepest = ocean[0, levels - 1]
    deepest = jnp.concatenate([deepest, deepest], axis=1)
    source = jnp.bitwise_and(2 * row_of(), rows - 1)
    halves = []
    for r in range(2):
        part = deepest[r * rows : (r + 1) * rows]
        halves.append(pick(part + turn(part, -1, 0), source, 0))
    pressure = jnp.where(row_of() < rows // 2, halves[0], halves[1])
    pressure = 0.25 * (pressure + turn(pressure, -1, 1))
    column = lane_of() - z * (width // 2)
    mine = jnp.logical_and(column >= 0, column < width // 2)
    pressure = pick(pressure, jnp.bitwise_and(2 * column, lanes - 1), 1)
    pressure = jnp.where(mine, pressure, 0.0)
    out_pressure[0] = pressure
    out_small[2] = jnp.where(flag(one(z == 0)), solid[2, 0], pressure)
    out_small[3] = zero


def pack_z_kernel(
    sizes, solid, sent_small, medium, offset_x, offset_y, out_even, out_odd, out_medium, out_index
):
    fill_tables(sizes, medium, offset_x, offset_y, out_medium, out_index)
    odd_z = lax.rem(lax.axis_index("gz"), 2)
    depth = solid.shape[1]
    start_even = (1 - odd_z) * (depth - 2)
    start_odd = odd_z * (depth - 2)
    for i, field in enumerate(z_fields):
        for k in range(2):
            out_even[2 * i + k] = solid[field, start_even + k]
            out_odd[2 * i + k] = solid[field, start_odd + k]
    for i in range(2):
        out_odd[2 * len(z_fields) + i] = sent_small[i]


def fill_tables(sizes, medium, offset_x, offset_y, out_medium, out_index):
    span_x, span_y, _ = sizes
    fine, width = offset_x.shape[1], offset_y.shape[1]
    pairs = out_medium.shape[1]
    x, y, z = where_am_i()
    lane, row = lane_of(), row_of()
    lower = lane < half
    for m in range(2):
        values = jnp.concatenate([medium[m : m + 1, :]] * (lanes // (2 * pairs)), axis=1)
        values = jnp.broadcast_to(values, (rows, lanes))
        for k in range(pairs):
            out_medium[m, k] = pick(values, jnp.where(lower, k, k + pairs), 1)

    moves = jnp.concatenate([offset_x[...].astype(jnp.float32)] * (lanes // fine), axis=1)
    moves = jnp.broadcast_to(moves, (rows, lanes))
    for r in range(2):
        place = row + r * rows
        move = jnp.sum(jnp.where(lane == place, moves, 0.0), axis=1, keepdims=True)
        target = lax.shift_right_logical(place, 1) + move.astype(jnp.int32)
        out_index[r] = jnp.clip(target, -(x * rows), (span_x - x) * rows - 1)
    coarse = lax.shift_right_logical(jnp.bitwise_and(lane, half - 1), 1) + z * (width // 2)
    move = jnp.concatenate([offset_y[...], offset_y[...]], axis=1)
    out_index[2] = coarse
    out_index[3] = jnp.clip(
        coarse + jnp.broadcast_to(move, (rows, lanes)), -(y * lanes), (span_y - y) * lanes - 1
    )


def pick(x, index, axis):
    return jnp.take_along_axis(x, index, axis=axis)


def blend_rows(plane, rim, index):
    parts = []
    for r in range(2):
        near = pick(plane, lax.shift_right_logical(row_of() + r * rows, 1), 0)
        target = index[r]
        inside = jnp.logical_and(target >= 0, target < rows)
        beyond = jnp.where(target < 0, rim[0:1], rim[1:2])
        other = jnp.where(inside, pick(plane, jnp.bitwise_and(target, rows - 1), 0), beyond)
        parts.append(0.75 * near + 0.25 * other)
    return parts


def blend_cols(inside, beside, index):
    near, target = index[2], index[3]
    at_home = jnp.logical_and(target >= 0, target < lanes)
    source = jnp.bitwise_and(target, lanes - 1)
    parts = []
    for own, other in zip(inside, beside):
        far_value = jnp.where(at_home, pick(own, source, 1), pick(other, source, 1))
        parts.append(0.75 * pick(own, near, 1) + 0.25 * far_value)
    return jnp.concatenate(parts, axis=0)


def x_scratch(packs, scratch):
    odd = flag(lax.rem(lax.axis_index("gx"), 2))
    yes = jnp.full((rows, lanes), True)

    def fill(tiles):
        for i in tiles:
            low, high = sides([pack[i] for pack in packs], odd)
            if len(packs) == 1:
                scratch[0, i] = row_terms(low, odd)
            else:
                scratch[0, i] = row_terms(low, yes)
                scratch[1, i] = row_terms(high, jnp.logical_not(yes))

    def terms(t, mask_low, mask_high):
        q = t % 4
        tile = turn(scratch[0, t // 4], -2 * q, 0)
        if len(packs) == 1:
            return jnp.where(jnp.logical_or(mask_low, mask_high), tile, 0.0)
        high = turn(scratch[1, t // 4], -2 * q, 0)
        return jnp.where(mask_low, tile, jnp.where(mask_high, high, 0.0))

    return fill, terms


def ocean_kernel(sizes, ocean, medium, *refs):
    packs = refs[:-7]
    ocean_next, ocean_rate, carry, stage_next, stage_rate, scratch, sems = refs[-7:]
    span_x, span_y, span_z = sizes
    levels, fine, _ = ocean.shape[1:]
    pairs = levels // 2
    x, y, z = where_am_i()
    x_first, x_last = one(x == 0), one(x == span_x - 1)
    joint_first = one(y == 0) * one(z == 0)
    joint_last = one(y == span_y - 1) * one(z == span_z - 1)
    row = row_of()
    low_rows = jnp.logical_and(row < 2, flag(1 - x_first))
    high_rows = jnp.logical_and(row >= rows - 2, flag(1 - x_last))
    never = jnp.full((rows, lanes), False)
    fill, terms = x_scratch(packs, scratch)
    tiles = len(ocean_x_fields) * pairs // 4
    first_tile = packs[0].shape[0] - tiles
    fill(range(first_tile, first_tile + tiles))

    def x_ends(t):
        t = 4 * first_tile + t
        return jnp.concatenate([terms(t, low_rows, never), terms(t, never, high_rows)], axis=0)

    wide = (fine, lanes)
    lower = lane_of(wide) < half
    weights_x = stencil(row_of(wide), fine, x_first, x_last)
    weights_y = stencil(
        jnp.bitwise_and(lane_of(wide), half - 1), half, joint_first, joint_last
    )
    states = [[paired_level(ocean, m, k, levels) for k in range(pairs)] for m in range(4)]

    def slope_z(m, k):
        def at(i):
            if 0 <= i < pairs:
                return states[m][i]
            return turn(states[m][i % pairs], half, 1)

        total = (at(k - 2) - at(k + 2) + 8.0 * (at(k + 1) - at(k - 1))) * (1.0 / 12.0)
        if k < 4:
            near = sum(w * at(c) for c, w in enumerate(closure_rows[k]) if w != 0.0)
            total = jnp.where(lower, near, total)
        if pairs - 1 - k < 4:
            near = sum(
                -w * at(pairs - 1 - c)
                for c, w in enumerate(closure_rows[pairs - 1 - k])
                if w != 0.0
            )
            total = jnp.where(lower, total, near)
        return total

    copies = []
    chunk = pairs // 2
    for k in range(pairs):
        bulk = jnp.concatenate([medium[0, k]] * 2, axis=0)
        light = jnp.concatenate([medium[1, k]] * 2, axis=0)
        p, u, v, w = (states[m][k] for m in range(4))
        dxu = slope(u, weights_x, 0) + x_ends(k)
        dxp = slope(p, weights_x, 0) + x_ends(pairs + k)
        dyv = slope(v, weights_y, 1)
        dyp = slope(p, weights_y, 1)
        rate_p = -bulk * (2.0 * (dxu + dyv) + slope_z(3, k)) + gravity * w / light
        rate_w = -light * slope_z(0, k)
        if k == pairs - 1:
            rate_p = rate_p + jnp.where(lower, 0.0, inv_norm * bulk * w)
        if k == 0:
            rate_w = rate_w - jnp.where(lower, inv_norm * light * p, 0.0)
        carry[0, k] = rate_p
        carry[1, k] = -2.0 * light * dyp
        carry[2, k] = p
        carry[3, k] = v
        store_pair(stage_rate, stage_next, 0, k, -2.0 * light * dxp, u)
        store_pair(stage_rate, stage_next, 1, k, rate_w, w)
        if (k + 1) % chunk == 0:
            copies += out_copies(
                ((stage_rate, ocean_rate), (stage_next, ocean_next)),
                (1, 3), k + 1 - chunk, chunk, pairs, sems, len(copies),
            )
    for copy in copies:
        copy.wait()


def store_pair(stage_rate, stage_next, slot, k, rate, state):
    pairs = stage_rate.shape[1] // 2
    rate = step_size * rate
    after = state + section_weight * rate
    stage_rate[slot, k] = rate[:, :half]
    stage_next[slot, k] = after[:, :half]
    stage_rate[slot, k + pairs] = turn(rate, half, 1)[:, :half]
    stage_next[slot, k + pairs] = turn(after, half, 1)[:, :half]


def out_copies(routes, fields, start, chunk, pairs, sems, used):
    copies = []
    for stage, out in routes:
        for slot, field in enumerate(fields):
            for base in (start, start + pairs):
                copies.append(
                    pltpu.make_async_copy(
                        stage.at[slot, pl.ds(base, chunk)],
                        out.at[field, pl.ds(base, chunk)],
                        sems.at[used + len(copies)],
                    )
                )
    run_copies(copies)
    return copies


def relay_kernel(count_x, solid, pressure, got_small, got_ya, got_yb, *refs):
    planes, out = refs[:count_x], refs[-1]
    depth = solid.shape[1]
    _, y, z = where_am_i()
    odd_y = flag(lax.rem(y, 2))
    bottom, second = flag(one(z == 0)), flag(one(z == 1))
    lane = lane_of()
    got_y = (got_ya, got_yb)
    edge_tiles = out_edge_tiles(depth)
    t = y_fields.index(2) * depth
    _, right = sides([g[t // 32] for g in got_y], odd_y)
    right = turn(right, -(4 * (t % 32) + 2), 1)
    _, right_rim = sides([g[edge_tiles + 2] for g in got_y], odd_y)
    first = lane == 0
    plane = jnp.where(first, right, solid[2, 0])
    rim = jnp.where(first, right_rim, rim_tile_of(planes))
    came = got_small[2]
    out[0] = jnp.where(bottom, plane, jnp.where(second, came, came + pressure[0]))
    out[1] = jnp.where(bottom, rim, got_small[3])
    for i in range(2):
        low, high = sides([g[edge_tiles + i] for g in got_y], odd_y)
        out[2 + i] = jnp.where(bottom, high, low)


def out_edge_tiles(depth):
    return -(-len(y_fields) * depth // 32)


def solid_kernel(sizes, solid, material, got_even, got_odd, got_ya, got_yb, *refs):
    packs = refs[:-7]
    solid_next, solid_rate, carry, stage_next, stage_rate, scratch, sems = refs[-7:]
    span_x, span_y, span_z = sizes
    depth = solid.shape[1]
    x, y, z = where_am_i()
    x_first, x_last = one(x == 0), one(x == span_x - 1)
    y_first, y_last = one(y == 0), one(y == span_y - 1)
    odd_y, odd_z = flag(lax.rem(y, 2)), flag(lax.rem(z, 2))
    lane, row = lane_of(), row_of()
    low_rows = jnp.logical_and(row < 2, flag(1 - x_first))
    high_rows = jnp.logical_and(row >= rows - 2, flag(1 - x_last))
    fill, x_terms = x_scratch(packs, scratch)
    fill(range(len(x_fields) * depth // 4))
    y_edges = []
    for i in range(out_edge_tiles(depth)):
        low, high = sides([got_ya[i], got_yb[i]], odd_y)
        y_edges.append(edge_terms(low, high, flag(1 - y_first), flag(1 - y_last)))
    end_lanes = jnp.logical_or(lane < 2, lane >= lanes - 2)

    def y_terms(t):
        return jnp.where(end_lanes, turn(y_edges[t // 32], -(4 * (t % 32) + 2), 1), 0.0)

    weights_x = stencil(row, rows, x_first, x_last)
    weights_y = stencil(lane, lanes, y_first, y_last)
    at_first, at_last = flag(one(z == 0)), flag(one(z == span_z - 1))

    def layer(i, k):
        if 0 <= k < depth:
            return solid[z_fields[i], k]
        j = 2 * i + (k + 2 if k < 0 else k - depth)
        low, high = sides([got_even[j], got_odd[j]], odd_z)
        return low if k < 0 else high

    def slope_z(i, k):
        total = (
            layer(i, k - 2) - layer(i, k + 2) + 8.0 * (layer(i, k + 1) - layer(i, k - 1))
        ) * (1.0 / 12.0)
        if k < 4:
            near = sum(w * layer(i, c) for c, w in enumerate(closure_rows[k]) if w != 0.0)
            total = jnp.where(at_first, near, total)
        if depth - 1 - k < 4:
            near = sum(
                -w * layer(i, depth - 1 - c)
                for c, w in enumerate(closure_rows[depth - 1 - k])
                if w != 0.0
            )
            total = jnp.where(at_last, near, total)
        return total

    copies = []
    for k in range(depth):
        dx = {
            m: slope(solid[m, k], weights_x, 0) + x_terms(i * depth + k, low_rows, high_rows)
            for i, m in enumerate(x_fields)
        }
        dy = {
            m: slope(solid[m, k], weights_y, 1) + y_terms(i * depth + k)
            for i, m in enumerate(y_fields)
        }
        metric = material[3, k]
        dz = {m: metric * slope_z(i, k) for i, m in enumerate(z_fields)}
        buoyancy, lame_one, lame_two = material[0, k], material[1, k], material[2, k]
        dilation = lame_one * (dx[0] + dy[1] + dz[2])
        twice = 2.0 * lame_two
        rates = [
            buoyancy * (dx[3] + dy[8] + dz[7]),
            buoyancy * (dx[8] + dy[4] + dz[6]),
            buoyancy * (dx[7] + dy[6] + dz[5]),
            dilation + twice * dx[0],
            dilation + twice * dy[1],
            dilation + twice * dz[2],
            lame_two * (dz[1] + dy[2]),
            lame_two * (dz[0] + dx[2]),
            lame_two * (dy[0] + dx[1]),
        ]
        if k == 0:
            factor = jnp.where(at_first, inv_norm * buoyancy * metric, 0.0)
            rates[0] = rates[0] + factor * solid[7, 0]
            rates[1] = rates[1] + factor * solid[6, 0]
            carry[0] = rates[2] + factor * solid[5, 0]
            carry[1] = factor
        for m, rate in enumerate(rates):
            rate = step_size * rate
            stage_rate[m, k] = rate
            stage_next[m, k] = solid[m, k] + section_weight * rate
        if k == 0:
            spans = ((0, 2, 0, 1), (3, 6, 0, 1))
        else:
            spans = ((0, 9, k, 1),) if k % 2 else ()
            spans = spans if k < 3 else ((0, 9, k - 1, 2),) if k % 2 else ()
        fresh = []
        for first, count, level, thick in spans:
            at = (pl.ds(first, count), pl.ds(level, thick))
            for stage, out in ((stage_rate, solid_rate), (stage_next, solid_next)):
                n = len(copies) + len(fresh)
                fresh.append(pltpu.make_async_copy(stage.at[at], out.at[at], sems.at[n]))
        run_copies(fresh)
        copies += fresh
    for copy in copies:
        copy.wait()


def last_kernel(
    sizes, solid, medium, pressure, index, ocean_carry, solid_carry,
    got_small, got_odd, got_far, got_ya, got_yb, *refs,
):
    _, span_y, span_z = sizes
    planes = refs[:-13]
    outs = refs[-9:-5]
    solid_next, solid_rate, ocean_next, ocean_rate = outs
    stage_next, stage_rate, vz_next, vz_rate, sems = refs[-5:]
    depth = solid.shape[1]
    pairs, fine = ocean_carry.shape[1:3]
    _, y, z = where_am_i()
    odd_y, odd_z = flag(lax.rem(y, 2)), flag(lax.rem(z, 2))
    bottom, second, top = (flag(one(z == i)) for i in (0, 1, span_z - 1))
    joint_first = one(y == 0) * one(z == 0)
    joint_last = one(y == span_y - 1) * one(z == span_z - 1)
    lane = lane_of()
    ring = 2 * len(z_fields)
    copies = []

    sum_pressure = pressure[0] + got_small[2] + got_far[0]
    rate = step_size * (solid_carry[0] + solid_carry[1] * sum_pressure)
    vz_rate[0, 0] = rate
    vz_next[0, 0] = solid[2, 0] + section_weight * rate
    at = (pl.ds(2, 1), pl.ds(0, 1))
    for stage, out in ((vz_rate, solid_rate), (vz_next, solid_next)):
        copies.append(pltpu.make_async_copy(stage, out.at[at], sems.at[len(copies)]))
    run_copies(copies)

    lows, highs = [], []
    for i in range(2):
        low, high = sides([got_small[i], got_odd[ring + i]], odd_z)
        lows.append(jnp.where(bottom, got_far[2 + i], low))
        highs.append(jnp.where(top, got_far[2 + i], high))
    has_left, has_right = flag(1 - joint_first), flag(1 - joint_last)
    outer = edge_terms(lows[1], highs[1], has_left, has_right)
    inner = edge_terms(lows[0], highs[0], has_left, has_right)
    end_lanes = jnp.logical_or(lane < 2, lane >= lanes - 2)
    mid_lanes = jnp.logical_and(lane >= half - 2, lane < half + 2)

    def y_ends(t):
        parts = []
        for r in range(fine // rows):
            q = t * (fine // rows) + r
            end = turn(outer, -4 * q - 2, 1)
            mid = turn(inner, half - 4 * q - 2, 1)
            parts.append(jnp.where(end_lanes, end, jnp.where(mid_lanes, mid, 0.0)))
        return jnp.concatenate(parts, axis=0)

    edge_tiles = out_edge_tiles(depth)
    t = y_fields.index(2) * depth
    left, _ = sides([got_ya[t // 32], got_yb[t // 32]], odd_y)
    left = turn(left, lanes - 1 - (4 * (t % 32) + 1), 1)
    left_rim, _ = sides([got_ya[edge_tiles + 2], got_yb[edge_tiles + 2]], odd_y)
    own_rim = rim_tile_of(planes)
    plane = jnp.where(bottom, solid[2, 0], jnp.where(second, got_small[2], got_far[0]))
    rim = jnp.where(bottom, own_rim, jnp.where(second, got_small[3], got_far[1]))
    beside = jnp.where(lane == 0, got_far[0], left)
    beside_rim = jnp.where(lane == 0, got_far[1], left_rim)
    bed_speed = blend_cols(
        blend_rows(plane, rim, index), blend_rows(beside, beside_rim, index), index
    )

    pull = jnp.where(lane_of((fine, lanes)) < half, 0.0, inv_norm * bed_speed)
    pull = pull * jnp.concatenate([medium[0, pairs - 1]] * 2, axis=0)
    for slot, field in ((1, 2), (0, 0)):
        for k in range(pairs):
            scale = jnp.concatenate([medium[slot, k]] * 2, axis=0)
            ends = y_ends((pairs if slot else 0) + k)
            rate = ocean_carry[slot, k] - 2.0 * scale * ends
            if slot == 0 and k == pairs - 1:
                rate = rate - pull
            store_pair(stage_rate, stage_next, slot, k, rate, ocean_carry[2 + slot, k])
        fresh = [
            pltpu.make_async_copy(stage.at[slot], out.at[field], sems.at[len(copies) + i])
            for i, (stage, out) in enumerate(
                ((stage_rate, ocean_rate), (stage_next, ocean_next))
            )
        ]
        run_copies(fresh)
        copies += fresh
    for copy in copies:
        copy.wait()


def compute(solid_state, material, ocean_state, ocean_medium, offset_x, offset_y):
    sizes = tuple(lax.axis_size(axis) for axis in ("gx", "gy", "gz"))
    span_x, span_y, span_z = sizes
    depth = solid_state.shape[1]
    levels, fine, width = ocean_state.shape[1:]
    pairs = levels // 2
    if solid_state.shape[2:] != (rows, lanes) or (fine, width) != (2 * rows, half):
        raise ValueError("tile shape")
    if depth % 4 or levels % 2 or span_z != 4 or span_x % 2 or span_y % 2 or span_y < 4:
        raise ValueError("sizes")
    f32 = jnp.float32
    vmem = pl.BlockSpec(memory_space=pltpu.VMEM)
    smem = pl.BlockSpec(memory_space=pltpu.SMEM)
    hbm = pl.BlockSpec(memory_space=pl.ANY)
    near = lambda x: pltpu.with_memory_space_constraint(x, pltpu.VMEM)
    tiles = lambda *n: pltpu.VMEM((*n, rows, lanes), f32)
    like = lambda a: jax.ShapeDtypeStruct(a.shape, f32)
    dma = pltpu.SemaphoreType.DMA
    material = near(material)
    x_rounds = pair_rounds(span_x)
    count_x = len(x_rounds)
    pack_tiles = (len(x_fields) * depth + len(ocean_x_fields) * pairs) // 4
    edge_tiles = out_edge_tiles(depth)
    layers = 2 * len(z_fields)
    solid, ocean, small, move_x, move_y = pl.pallas_call(
        stage_kernel,
        out_shape=[
            pltpu.VMEM(solid_state.shape, f32),
            pltpu.VMEM((3, *ocean_state.shape[1:]), f32),
            pltpu.VMEM(ocean_medium.shape, f32),
            pltpu.VMEM((1, fine), jnp.int32),
            pltpu.VMEM((1, width), jnp.int32),
        ],
        in_specs=[hbm] * 5,
        out_specs=[vmem] * 5,
        scratch_shapes=[dma((5,))],
        name="stage",
    )(
        solid_state,
        ocean_state,
        ocean_medium,
        offset_x.reshape(1, fine),
        offset_y.reshape(1, width),
    )
    solid, ocean = near(solid), near(ocean)
    plane = solid_state[2, 0]
    planes = [lax.ppermute(plane, "gx", p) for p in x_rounds]
    sent_x = pl.pallas_call(
        pack_x_kernel,
        out_shape=[tiles(pack_tiles) for _ in x_rounds],
        in_specs=[vmem] * 2,
        out_specs=[vmem] * count_x,
        name="pack_x",
    )(solid, ocean)
    got_x = [near(lax.ppermute(m, "gx", p)) for m, p in zip(sent_x, x_rounds)]
    sent_y, sent_small, pressure = pl.pallas_call(
        pack_kernel,
        out_shape=[tiles(edge_tiles + 3), tiles(4), tiles(1)],
        in_specs=[vmem] * 2,
        out_specs=[vmem] * 3,
        name="pack",
    )(solid, ocean)
    pressure = near(pressure)
    ring = ("gy", "gz")
    places = [(y, z) for y in range(span_y) for z in range(span_z)]

    def over_ring(move):
        return [(y * span_z + z, y2 * span_z + z2)
                for y, z in places for y2, z2 in (move(y, z),)]

    even = over_ring(lambda y, z: (y, z ^ 1))
    inner = over_ring(
        lambda y, z: (y ^ 1, z) if z in (0, span_z - 1) else (y, z + 1 if z % 2 else z - 1)
    )
    ends = over_ring(lambda y, z: (y, span_z - 1 - z))
    rim = row_rims(planes)
    planes = [near(plane) for plane in planes]
    sent_y, sent_small = (m.at[m.shape[0] - 1, :2].set(rim) for m in (sent_y, sent_small))
    sent_even, sent_odd, medium, index = pl.pallas_call(
        functools.partial(pack_z_kernel, sizes),
        out_shape=[
            tiles(layers),
            tiles(layers + 2),
            tiles(2, pairs),
            pltpu.VMEM((4, rows, lanes), jnp.int32),
        ],
        in_specs=[vmem] * 5,
        out_specs=[vmem] * 4,
        name="pack_z",
    )(solid, near(sent_small), near(small), near(move_x), near(move_y))
    medium, index = near(medium), near(index)
    rounds_y = pair_rounds(span_y)
    got_ya = near(lax.ppermute(sent_y, "gy", rounds_y[0]))
    got_yb = near(lax.ppermute(sent_y, "gy", rounds_y[1]))
    got_y = (got_ya, got_yb)
    got_small = near(lax.ppermute(sent_small, ring, even))
    got_even = near(lax.ppermute(sent_even, ring, even))
    got_odd = near(lax.ppermute(sent_odd, ring, inner))

    ocean_next, ocean_rate, ocean_carry = pl.pallas_call(
        functools.partial(ocean_kernel, sizes),
        out_shape=[like(ocean_state), like(ocean_state), pltpu.VMEM((4, pairs, fine, lanes), f32)],
        in_specs=[vmem] * (2 + count_x),
        out_specs=[hbm, hbm, vmem],
        scratch_shapes=[
            pltpu.VMEM((2, levels, fine, width), f32),
            pltpu.VMEM((2, levels, fine, width), f32),
            pltpu.VMEM((count_x, pack_tiles, rows, lanes), f32),
            dma((16,)),
        ],
        name="ocean",
    )(near(ocean_state), medium, *got_x)

    sent_far = pl.pallas_call(
        functools.partial(relay_kernel, count_x),
        out_shape=tiles(4),
        in_specs=[vmem] * (5 + count_x),
        out_specs=vmem,
        name="relay",
    )(solid, pressure, got_small, *got_y, *planes)
    got_far = near(lax.ppermute(sent_far, ring, ends))

    solid_next, solid_rate, solid_carry = pl.pallas_call(
        functools.partial(solid_kernel, sizes),
        out_shape=[like(solid_state), like(solid_state), tiles(2)],
        in_specs=[vmem] * (6 + count_x),
        out_specs=[hbm, hbm, vmem],
        scratch_shapes=[
            pltpu.VMEM(solid_state.shape, f32),
            pltpu.VMEM(solid_state.shape, f32),
            pltpu.VMEM((count_x, pack_tiles, rows, lanes), f32),
            dma((2 * depth,)),
        ],
        name="solid",
    )(solid, material, got_even, got_odd, *got_y, *got_x)

    return pl.pallas_call(
        functools.partial(last_kernel, sizes),
        out_shape=[like(solid_state), like(solid_state), like(ocean_state), like(ocean_state)],
        in_specs=[vmem] * (11 + count_x) + [hbm] * 4,
        out_specs=[hbm] * 4,
        input_output_aliases={11 + count_x + i: i for i in range(4)},
        scratch_shapes=[
            pltpu.VMEM((2, levels, fine, width), f32),
            pltpu.VMEM((2, levels, fine, width), f32),
            tiles(1, 1),
            tiles(1, 1),
            dma((6,)),
        ],
        name="last",
    )(
        solid, medium, pressure, index, near(ocean_carry), near(solid_carry),
        got_small, got_odd, got_far, *got_y, *planes,
        solid_next, solid_rate, ocean_next, ocean_rate,
    )


def solution(mesh):
    in_specs = (
        P(None, "gz", "gx", "gy"),
        P(None, "gz", "gx", "gy"),
        P(None, None, "gx", ("gy", "gz")),
        P(),
        P("gx"),
        P(("gy", "gz")),
    )
    out_specs = (
        P(None, "gz", "gx", "gy"),
        P(None, "gz", "gx", "gy"),
        P(None, None, "gx", ("gy", "gz")),
        P(None, None, "gx", ("gy", "gz")),
    )
    return jax.shard_map(compute, mesh=mesh, in_specs=in_specs, out_specs=out_specs, check_vma=False)
```

```python
import functools

import jax
import jax.numpy as jnp
from jax import lax
from jax.experimental import pallas as pl
from jax.experimental.pallas import tpu as pltpu
from jax.sharding import PartitionSpec as P


closure_rows = (
    (-24.0 / 17.0, 59.0 / 34.0, -4.0 / 17.0, -3.0 / 34.0, 0.0, 0.0),
    (-0.5, 0.0, 0.5, 0.0, 0.0, 0.0),
    (4.0 / 43.0, -59.0 / 86.0, 0.0, 59.0 / 86.0, -4.0 / 43.0, 0.0),
    (3.0 / 98.0, 0.0, -59.0 / 98.0, 0.0, 32.0 / 49.0, -4.0 / 49.0),
)
inv_norm = 48.0 / 17.0
step_size = 0.25
section_weight = 0.1496590219993
gravity = 0.4
interior_weights = {-2: 1.0 / 12.0, -1: -8.0 / 12.0, 1: 8.0 / 12.0, 2: -1.0 / 12.0}

x_fields = (0, 1, 2, 3, 8, 7)
y_fields = (0, 1, 2, 4, 8, 6)
z_fields = (0, 1, 2, 5, 6, 7)
ocean_x_fields = (1, 0)
ocean_y_fields = (2, 0)
rows, lanes, half = 8, 128, 64
far = 1 << 20


def turn(x, shift, axis):
    shift = shift % x.shape[axis]
    return x if shift == 0 else pltpu.roll(x, shift, axis)


def flag(value, shape=(rows, lanes)):
    return jnp.broadcast_to(value.astype(jnp.int32), shape) == 1


def lane_of(shape=(rows, lanes)):
    return lax.broadcasted_iota(jnp.int32, shape, 1)


def row_of(shape=(rows, lanes)):
    return lax.broadcasted_iota(jnp.int32, shape, 0)


def stencil(position, extent, first, last):
    low = position + far * (1 - first)
    high = extent - 1 - position + far * (1 - last)
    plain = jnp.logical_and(low >= 4, high >= 4)
    weights = {}
    for s in range(-3, 4):
        inside = jnp.logical_and(position + s >= 0, position + s < extent)
        w = jnp.where(jnp.logical_and(inside, plain), interior_weights.get(s, 0.0), 0.0)
        for r in range(4):
            if 0 <= r + s < 6 and closure_rows[r][r + s] != 0.0:
                w = jnp.where(low == r, closure_rows[r][r + s], w)
            if 0 <= r - s < 6 and closure_rows[r][r - s] != 0.0:
                w = jnp.where(high == r, -closure_rows[r][r - s], w)
        weights[s] = w
    return weights


def slope(x, weights, axis):
    total = weights[0] * x
    for s in (-3, -2, -1, 1, 2, 3):
        total = total + weights[s] * turn(x, -s, axis)
    return total


def pack_edges(tiles, offset=2):
    group = lax.shift_right_logical(lane_of(), 2)
    out = []
    for start in range(0, len(tiles), 32):
        acc = jnp.zeros((rows, lanes), jnp.float32)
        for q, tile in enumerate(tiles[start : start + 32]):
            acc = jnp.where(group == q, turn(tile, 4 * q + offset, 1), acc)
        out.append(acc)
    return out


def edge_terms(left, right, has_left, has_right):
    place = jnp.bitwise_and(lane_of(), 3)
    low = jnp.where(
        place == 2, turn(left, 2, 1) - 8.0 * turn(left, 1, 1), turn(left, 2, 1)
    )
    high = jnp.where(
        place == 0, -turn(right, -2, 1), 8.0 * turn(right, -1, 1) - turn(right, -2, 1)
    )
    low = jnp.where(has_left, low, 0.0)
    high = jnp.where(has_right, high, 0.0)
    return jnp.where(place >= 2, low, high) * (1.0 / 12.0)


def row_terms(pack, from_low):
    even = jnp.bitwise_and(row_of(), 1) == 0
    low = jnp.where(even, pack - 8.0 * turn(pack, -1, 0), pack)
    high = jnp.where(even, -pack, 8.0 * turn(pack, 1, 0) - pack)
    return jnp.where(from_low, low, turn(high, 6, 0)) * (1.0 / 12.0)


def pair_rounds(size):
    first = [(i, i ^ 1) for i in range(size)]
    if size == 2:
        return (first,)
    second = [(i, (i + 1) % size if i % 2 else (i - 1) % size) for i in range(size)]
    return (first, second)


def where_am_i():
    return lax.axis_index("gx"), lax.axis_index("gy"), lax.axis_index("gz")


def paired_level(ocean, field, k, levels):
    a = ocean[field, k]
    b = ocean[field, k + levels // 2]
    return jnp.concatenate([a, b], axis=1)


def row_rims(planes):
    if len(planes) == 1:
        return jnp.concatenate([planes[0][-1:], planes[0][:1]], axis=0)
    odd = lax.axis_index("gx") % 2 == 1
    low = jnp.where(odd, planes[0][-1:], planes[1][-1:])
    high = jnp.where(odd, planes[1][:1], planes[0][:1])
    return jnp.concatenate([low, high], axis=0)


def rim_tile_of(planes):
    odd = flag(lax.rem(lax.axis_index("gx"), 2))
    low, high = sides([plane[...] for plane in planes], odd)
    rim = jnp.where(row_of() == 0, turn(low, 1, 0), turn(high, 1, 0))
    return jnp.where(row_of() < 2, rim, 0.0)


def sides(got, odd):
    if len(got) == 1:
        return got[0], got[0]
    return jnp.where(odd, got[0], got[1]), jnp.where(odd, got[1], got[0])


def one(condition):
    return condition.astype(jnp.int32)


def run_copies(copies):
    for copy in copies:
        copy.start()


def stage_kernel(*refs):
    solid_far, ocean_far, medium_far, offset_x_far, offset_y_far = refs[:5]
    solid, ocean, small, offset_x, offset_y, sems = refs[5:]
    copies = [
        pltpu.make_async_copy(solid_far, solid, sems.at[0]),
        pltpu.make_async_copy(ocean_far, ocean, sems.at[1]),
        pltpu.make_async_copy(medium_far, small, sems.at[2]),
        pltpu.make_async_copy(offset_x_far, offset_x, sems.at[3]),
        pltpu.make_async_copy(offset_y_far, offset_y, sems.at[4]),
    ]
    run_copies(copies)
    for copy in copies:
        copy.wait()


def pack_x_kernel(solid, ocean, *outs):
    levels, fine = ocean.shape[1:3]
    depth = solid.shape[1]
    odd = flag(lax.rem(lax.axis_index("gx"), 2))
    pair = lax.shift_right_logical(row_of(), 1)

    def emit(heads, base):
        for number, out in enumerate(outs):
            acc = None
            for t, (head, tail) in enumerate(heads):
                q = t % 4
                edge = jnp.where(odd, head, tail) if number == 0 else jnp.where(odd, tail, head)
                edge = turn(edge, 2 * q, 0)
                acc = edge if q == 0 else jnp.where(pair == q, edge, acc)
                if q == 3:
                    out[base + t // 4] = acc

    heads = []
    for field in x_fields:
        for k in range(depth):
            tile = solid[field, k]
            heads.append((tile, turn(tile, 2, 0)))
    emit(heads, 0)
    base = len(heads) // 4
    heads = []
    for field in ocean_x_fields:
        for k in range(levels // 2):
            tile = paired_level(ocean, field, k, levels)
            heads.append((tile[:rows], turn(tile[fine - rows :], 2, 0)))
    emit(heads, base)


def pack_kernel(solid, ocean, out_y, out_small, out_pressure):
    levels, fine, width = ocean.shape[1:]
    depth = solid.shape[1]
    _, _, z = where_am_i()
    zero = jnp.zeros((rows, lanes), jnp.float32)
    packed = pack_edges([solid[field, k] for field in y_fields for k in range(depth)])
    tiles = []
    for field in ocean_y_fields:
        for k in range(levels // 2):
            tile = paired_level(ocean, field, k, levels)
            tiles += [tile[r : r + rows] for r in range(0, fine, rows)]
    ends = pack_edges(tiles) + pack_edges(tiles, half + 2)
    for i, tile in enumerate(packed + ends + [zero]):
        out_y[i] = tile
    for i, tile in enumerate(ends):
        out_small[i] = tile
    deepest = ocean[0, levels - 1]
    deepest = jnp.concatenate([deepest, deepest], axis=1)
    source = jnp.bitwise_and(2 * row_of(), rows - 1)
    halves = []
    for r in range(2):
        part = deepest[r * rows : (r + 1) * rows]
        halves.append(pick(part + turn(part, -1, 0), source, 0))
    pressure = jnp.where(row_of() < rows // 2, halves[0], halves[1])
    pressure = 0.25 * (pressure + turn(pressure, -1, 1))
    column = lane_of() - z * (width // 2)
    mine = jnp.logical_and(column >= 0, column < width // 2)
    pressure = pick(pressure, jnp.bitwise_and(2 * column, lanes - 1), 1)
    pressure = jnp.where(mine, pressure, 0.0)
    out_pressure[0] = pressure
    out_small[2] = jnp.where(flag(one(z == 0)), solid[2, 0], pressure)
    out_small[3] = zero


def pack_z_kernel(
    sizes, solid, sent_small, medium, offset_x, offset_y, out_even, out_odd, out_medium, out_index
):
    fill_tables(sizes, medium, offset_x, offset_y, out_medium, out_index)
    odd_z = lax.rem(lax.axis_index("gz"), 2)
    depth = solid.shape[1]
    start_even = (1 - odd_z) * (depth - 2)
    start_odd = odd_z * (depth - 2)
    for i, field in enumerate(z_fields):
        for k in range(2):
            out_even[2 * i + k] = solid[field, start_even + k]
            out_odd[2 * i + k] = solid[field, start_odd + k]
    for i in range(2):
        out_odd[2 * len(z_fields) + i] = sent_small[i]


def fill_tables(sizes, medium, offset_x, offset_y, out_medium, out_index):
    span_x, span_y, _ = sizes
    fine, width = offset_x.shape[1], offset_y.shape[1]
    pairs = out_medium.shape[1]
    x, y, z = where_am_i()
    lane, row = lane_of(), row_of()
    lower = lane < half
    for m in range(2):
        values = jnp.concatenate([medium[m : m + 1, :]] * (lanes // (2 * pairs)), axis=1)
        values = jnp.broadcast_to(values, (rows, lanes))
        for k in range(pairs):
            out_medium[m, k] = pick(values, jnp.where(lower, k, k + pairs), 1)

    moves = jnp.concatenate([offset_x[...].astype(jnp.float32)] * (lanes // fine), axis=1)
    moves = jnp.broadcast_to(moves, (rows, lanes))
    for r in range(2):
        place = row + r * rows
        move = jnp.sum(jnp.where(lane == place, moves, 0.0), axis=1, keepdims=True)
        target = lax.shift_right_logical(place, 1) + move.astype(jnp.int32)
        out_index[r] = jnp.clip(target, -(x * rows), (span_x - x) * rows - 1)
    coarse = lax.shift_right_logical(jnp.bitwise_and(lane, half - 1), 1) + z * (width // 2)
    move = jnp.concatenate([offset_y[...], offset_y[...]], axis=1)
    out_index[2] = coarse
    out_index[3] = jnp.clip(
        coarse + jnp.broadcast_to(move, (rows, lanes)), -(y * lanes), (span_y - y) * lanes - 1
    )


def pick(x, index, axis):
    return jnp.take_along_axis(x, index, axis=axis)


def blend_rows(plane, rim, index):
    parts = []
    for r in range(2):
        near = pick(plane, lax.shift_right_logical(row_of() + r * rows, 1), 0)
        target = index[r]
        inside = jnp.logical_and(target >= 0, target < rows)
        beyond = jnp.where(target < 0, rim[0:1], rim[1:2])
        other = jnp.where(inside, pick(plane, jnp.bitwise_and(target, rows - 1), 0), beyond)
        parts.append(0.75 * near + 0.25 * other)
    return parts


def blend_cols(inside, beside, index):
    near, target = index[2], index[3]
    at_home = jnp.logical_and(target >= 0, target < lanes)
    source = jnp.bitwise_and(target, lanes - 1)
    parts = []
    for own, other in zip(inside, beside):
        far_value = jnp.where(at_home, pick(own, source, 1), pick(other, source, 1))
        parts.append(0.75 * pick(own, near, 1) + 0.25 * far_value)
    return jnp.concatenate(parts, axis=0)


def x_scratch(packs, scratch):
    odd = flag(lax.rem(lax.axis_index("gx"), 2))
    yes = jnp.full((rows, lanes), True)

    def fill(tiles):
        for i in tiles:
            low, high = sides([pack[i] for pack in packs], odd)
            if len(packs) == 1:
                scratch[0, i] = row_terms(low, odd)
            else:
                scratch[0, i] = row_terms(low, yes)
                scratch[1, i] = row_terms(high, jnp.logical_not(yes))

    def terms(t, mask_low, mask_high):
        q = t % 4
        tile = turn(scratch[0, t // 4], -2 * q, 0)
        if len(packs) == 1:
            return jnp.where(jnp.logical_or(mask_low, mask_high), tile, 0.0)
        high = turn(scratch[1, t // 4], -2 * q, 0)
        return jnp.where(mask_low, tile, jnp.where(mask_high, high, 0.0))

    return fill, terms


def ocean_kernel(sizes, ocean, medium, *refs):
    packs = refs[:-7]
    ocean_next, ocean_rate, carry, stage_next, stage_rate, scratch, sems = refs[-7:]
    span_x, span_y, span_z = sizes
    levels, fine, _ = ocean.shape[1:]
    pairs = levels // 2
    x, y, z = where_am_i()
    x_first, x_last = one(x == 0), one(x == span_x - 1)
    joint_first = one(y == 0) * one(z == 0)
    joint_last = one(y == span_y - 1) * one(z == span_z - 1)
    row = row_of()
    low_rows = jnp.logical_and(row < 2, flag(1 - x_first))
    high_rows = jnp.logical_and(row >= rows - 2, flag(1 - x_last))
    never = jnp.full((rows, lanes), False)
    fill, terms = x_scratch(packs, scratch)
    tiles = len(ocean_x_fields) * pairs // 4
    first_tile = packs[0].shape[0] - tiles
    fill(range(first_tile, first_tile + tiles))

    def x_ends(t):
        t = 4 * first_tile + t
        return jnp.concatenate([terms(t, low_rows, never), terms(t, never, high_rows)], axis=0)

    wide = (fine, lanes)
    lower = lane_of(wide) < half
    weights_x = stencil(row_of(wide), fine, x_first, x_last)
    weights_y = stencil(
        jnp.bitwise_and(lane_of(wide), half - 1), half, joint_first, joint_last
    )
    states = [[paired_level(ocean, m, k, levels) for k in range(pairs)] for m in range(4)]

    def slope_z(m, k):
        def at(i):
            if 0 <= i < pairs:
                return states[m][i]
            return turn(states[m][i % pairs], half, 1)

        total = (at(k - 2) - at(k + 2) + 8.0 * (at(k + 1) - at(k - 1))) * (1.0 / 12.0)
        if k < 4:
            near = sum(w * at(c) for c, w in enumerate(closure_rows[k]) if w != 0.0)
            total = jnp.where(lower, near, total)
        if pairs - 1 - k < 4:
            near = sum(
                -w * at(pairs - 1 - c)
                for c, w in enumerate(closure_rows[pairs - 1 - k])
                if w != 0.0
            )
            total = jnp.where(lower, total, near)
        return total

    copies = []
    chunk = pairs // 2
    for k in range(pairs):
        bulk = jnp.concatenate([medium[0, k]] * 2, axis=0)
        light = jnp.concatenate([medium[1, k]] * 2, axis=0)
        p, u, v, w = (states[m][k] for m in range(4))
        dxu = slope(u, weights_x, 0) + x_ends(k)
        dxp = slope(p, weights_x, 0) + x_ends(pairs + k)
        dyv = slope(v, weights_y, 1)
        dyp = slope(p, weights_y, 1)
        rate_p = -bulk * (2.0 * (dxu + dyv) + slope_z(3, k)) + gravity * w / light
        rate_w = -light * slope_z(0, k)
        if k == pairs - 1:
            rate_p = rate_p + jnp.where(lower, 0.0, inv_norm * bulk * w)
        if k == 0:
            rate_w = rate_w - jnp.where(lower, inv_norm * light * p, 0.0)
        carry[0, k] = rate_p
        carry[1, k] = -2.0 * light * dyp
        store_pair(stage_rate, stage_next, 0, k, -2.0 * light * dxp, u)
        store_pair(stage_rate, stage_next, 1, k, rate_w, w)
        if (k + 1) % chunk == 0:
            copies += out_copies(
                ((stage_rate, ocean_rate), (stage_next, ocean_next)),
                (1, 3), k + 1 - chunk, chunk, pairs, sems, len(copies),
            )
    for copy in copies:
        copy.wait()


def store_pair(stage_rate, stage_next, slot, k, rate, state):
    pairs = stage_rate.shape[1] // 2
    rate = step_size * rate
    after = state + section_weight * rate
    stage_rate[slot, k] = rate[:, :half]
    stage_next[slot, k] = after[:, :half]
    stage_rate[slot, k + pairs] = turn(rate, half, 1)[:, :half]
    stage_next[slot, k + pairs] = turn(after, half, 1)[:, :half]


def out_copies(routes, fields, start, chunk, pairs, sems, used):
    copies = []
    for stage, out in routes:
        for slot, field in enumerate(fields):
            for base in (start, start + pairs):
                copies.append(
                    pltpu.make_async_copy(
                        stage.at[slot, pl.ds(base, chunk)],
                        out.at[field, pl.ds(base, chunk)],
                        sems.at[used + len(copies)],
                    )
                )
    run_copies(copies)
    return copies


def relay_kernel(count_x, solid, pressure, got_small, got_ya, got_yb, *refs):
    planes, out = refs[:count_x], refs[-1]
    depth = solid.shape[1]
    _, y, z = where_am_i()
    odd_y = flag(lax.rem(y, 2))
    bottom, second = flag(one(z == 0)), flag(one(z == 1))
    lane = lane_of()
    got_y = (got_ya, got_yb)
    edge_tiles = out_edge_tiles(depth)
    t = y_fields.index(2) * depth
    _, right = sides([g[t // 32] for g in got_y], odd_y)
    right = turn(right, -(4 * (t % 32) + 2), 1)
    _, right_rim = sides([g[edge_tiles + 2] for g in got_y], odd_y)
    first = lane == 0
    plane = jnp.where(first, right, solid[2, 0])
    rim = jnp.where(first, right_rim, rim_tile_of(planes))
    came = got_small[2]
    out[0] = jnp.where(bottom, plane, jnp.where(second, came, came + pressure[0]))
    out[1] = jnp.where(bottom, rim, got_small[3])
    for i in range(2):
        low, high = sides([g[edge_tiles + i] for g in got_y], odd_y)
        out[2 + i] = jnp.where(bottom, high, low)


def out_edge_tiles(depth):
    return -(-len(y_fields) * depth // 32)


def solid_kernel(sizes, solid, material, got_even, got_odd, got_ya, got_yb, *refs):
    packs = refs[:-7]
    solid_next, solid_rate, carry, stage_next, stage_rate, scratch, sems = refs[-7:]
    span_x, span_y, span_z = sizes
    depth = solid.shape[1]
    x, y, z = where_am_i()
    x_first, x_last = one(x == 0), one(x == span_x - 1)
    y_first, y_last = one(y == 0), one(y == span_y - 1)
    odd_y, odd_z = flag(lax.rem(y, 2)), flag(lax.rem(z, 2))
    lane, row = lane_of(), row_of()
    low_rows = jnp.logical_and(row < 2, flag(1 - x_first))
    high_rows = jnp.logical_and(row >= rows - 2, flag(1 - x_last))
    fill, x_terms = x_scratch(packs, scratch)
    fill(range(len(x_fields) * depth // 4))
    y_edges = []
    for i in range(out_edge_tiles(depth)):
        low, high = sides([got_ya[i], got_yb[i]], odd_y)
        y_edges.append(edge_terms(low, high, flag(1 - y_first), flag(1 - y_last)))
    end_lanes = jnp.logical_or(lane < 2, lane >= lanes - 2)

    def y_terms(t):
        return jnp.where(end_lanes, turn(y_edges[t // 32], -(4 * (t % 32) + 2), 1), 0.0)

    weights_x = stencil(row, rows, x_first, x_last)
    weights_y = stencil(lane, lanes, y_first, y_last)
    at_first, at_last = flag(one(z == 0)), flag(one(z == span_z - 1))

    def layer(i, k):
        if 0 <= k < depth:
            return solid[z_fields[i], k]
        j = 2 * i + (k + 2 if k < 0 else k - depth)
        low, high = sides([got_even[j], got_odd[j]], odd_z)
        return low if k < 0 else high

    def slope_z(i, k):
        total = (
            layer(i, k - 2) - layer(i, k + 2) + 8.0 * (layer(i, k + 1) - layer(i, k - 1))
        ) * (1.0 / 12.0)
        if k < 4:
            near = sum(w * layer(i, c) for c, w in enumerate(closure_rows[k]) if w != 0.0)
            total = jnp.where(at_first, near, total)
        if depth - 1 - k < 4:
            near = sum(
                -w * layer(i, depth - 1 - c)
                for c, w in enumerate(closure_rows[depth - 1 - k])
                if w != 0.0
            )
            total = jnp.where(at_last, near, total)
        return total

    copies = []
    for k in range(depth):
        dx = {
            m: slope(solid[m, k], weights_x, 0) + x_terms(i * depth + k, low_rows, high_rows)
            for i, m in enumerate(x_fields)
        }
        dy = {
            m: slope(solid[m, k], weights_y, 1) + y_terms(i * depth + k)
            for i, m in enumerate(y_fields)
        }
        metric = material[3, k]
        dz = {m: metric * slope_z(i, k) for i, m in enumerate(z_fields)}
        buoyancy, lame_one, lame_two = material[0, k], material[1, k], material[2, k]
        dilation = lame_one * (dx[0] + dy[1] + dz[2])
        twice = 2.0 * lame_two
        rates = [
            buoyancy * (dx[3] + dy[8] + dz[7]),
            buoyancy * (dx[8] + dy[4] + dz[6]),
            buoyancy * (dx[7] + dy[6] + dz[5]),
            dilation + twice * dx[0],
            dilation + twice * dy[1],
            dilation + twice * dz[2],
            lame_two * (dz[1] + dy[2]),
            lame_two * (dz[0] + dx[2]),
            lame_two * (dy[0] + dx[1]),
        ]
        if k == 0:
            factor = jnp.where(at_first, inv_norm * buoyancy * metric, 0.0)
            rates[0] = rates[0] + factor * solid[7, 0]
            rates[1] = rates[1] + factor * solid[6, 0]
            carry[0] = rates[2] + factor * solid[5, 0]
            carry[1] = factor
        for m, rate in enumerate(rates):
            rate = step_size * rate
            stage_rate[m, k] = rate
            stage_next[m, k] = solid[m, k] + section_weight * rate
        if k == 0:
            spans = ((0, 2, 0, 1), (3, 6, 0, 1))
        else:
            spans = ((0, 9, k, 1),) if k % 2 else ()
            spans = spans if k < 3 else ((0, 9, k - 1, 2),) if k % 2 else ()
        fresh = []
        for first, count, level, thick in spans:
            at = (pl.ds(first, count), pl.ds(level, thick))
            for stage, out in ((stage_rate, solid_rate), (stage_next, solid_next)):
                n = len(copies) + len(fresh)
                fresh.append(pltpu.make_async_copy(stage.at[at], out.at[at], sems.at[n]))
        run_copies(fresh)
        copies += fresh
    for copy in copies:
        copy.wait()


def last_kernel(
    sizes, solid, ocean, medium, pressure, index, ocean_carry, solid_carry,
    got_small, got_odd, got_far, got_ya, got_yb, *refs,
):
    _, span_y, span_z = sizes
    planes = refs[:-13]
    outs = refs[-9:-5]
    solid_next, solid_rate, ocean_next, ocean_rate = outs
    stage_next, stage_rate, vz_next, vz_rate, sems = refs[-5:]
    depth = solid.shape[1]
    pairs, fine = ocean_carry.shape[1:3]
    _, y, z = where_am_i()
    odd_y, odd_z = flag(lax.rem(y, 2)), flag(lax.rem(z, 2))
    bottom, second, top = (flag(one(z == i)) for i in (0, 1, span_z - 1))
    joint_first = one(y == 0) * one(z == 0)
    joint_last = one(y == span_y - 1) * one(z == span_z - 1)
    lane = lane_of()
    ring = 2 * len(z_fields)
    copies = []

    sum_pressure = pressure[0] + got_small[2] + got_far[0]
    rate = step_size * (solid_carry[0] + solid_carry[1] * sum_pressure)
    vz_rate[0, 0] = rate
    vz_next[0, 0] = solid[2, 0] + section_weight * rate
    at = (pl.ds(2, 1), pl.ds(0, 1))
    for stage, out in ((vz_rate, solid_rate), (vz_next, solid_next)):
        copies.append(pltpu.make_async_copy(stage, out.at[at], sems.at[len(copies)]))
    run_copies(copies)

    lows, highs = [], []
    for i in range(2):
        low, high = sides([got_small[i], got_odd[ring + i]], odd_z)
        lows.append(jnp.where(bottom, got_far[2 + i], low))
        highs.append(jnp.where(top, got_far[2 + i], high))
    has_left, has_right = flag(1 - joint_first), flag(1 - joint_last)
    outer = edge_terms(lows[1], highs[1], has_left, has_right)
    inner = edge_terms(lows[0], highs[0], has_left, has_right)
    end_lanes = jnp.logical_or(lane < 2, lane >= lanes - 2)
    mid_lanes = jnp.logical_and(lane >= half - 2, lane < half + 2)

    def y_ends(t):
        parts = []
        for r in range(fine // rows):
            q = t * (fine // rows) + r
            end = turn(outer, -4 * q - 2, 1)
            mid = turn(inner, half - 4 * q - 2, 1)
            parts.append(jnp.where(end_lanes, end, jnp.where(mid_lanes, mid, 0.0)))
        return jnp.concatenate(parts, axis=0)

    edge_tiles = out_edge_tiles(depth)
    t = y_fields.index(2) * depth
    left, _ = sides([got_ya[t // 32], got_yb[t // 32]], odd_y)
    left = turn(left, lanes - 1 - (4 * (t % 32) + 1), 1)
    left_rim, _ = sides([got_ya[edge_tiles + 2], got_yb[edge_tiles + 2]], odd_y)
    own_rim = rim_tile_of(planes)
    plane = jnp.where(bottom, solid[2, 0], jnp.where(second, got_small[2], got_far[0]))
    rim = jnp.where(bottom, own_rim, jnp.where(second, got_small[3], got_far[1]))
    beside = jnp.where(lane == 0, got_far[0], left)
    beside_rim = jnp.where(lane == 0, got_far[1], left_rim)
    bed_speed = blend_cols(
        blend_rows(plane, rim, index), blend_rows(beside, beside_rim, index), index
    )

    pull = jnp.where(lane_of((fine, lanes)) < half, 0.0, inv_norm * bed_speed)
    pull = pull * jnp.concatenate([medium[0, pairs - 1]] * 2, axis=0)
    for slot, field in ((1, 2), (0, 0)):
        for k in range(pairs):
            scale = jnp.concatenate([medium[slot, k]] * 2, axis=0)
            ends = y_ends((pairs if slot else 0) + k)
            rate = ocean_carry[slot, k] - 2.0 * scale * ends
            if slot == 0 and k == pairs - 1:
                rate = rate - pull
            rate = step_size * rate
            for level, part in ((k, rate), (k + pairs, turn(rate, half, 1))):
                stage_rate[slot, level] = part[:, :half]
                stage_next[slot, level] = (
                    ocean[field, level] + section_weight * part[:, :half]
                )
        fresh = [
            pltpu.make_async_copy(stage.at[slot], out.at[field], sems.at[len(copies) + i])
            for i, (stage, out) in enumerate(
                ((stage_rate, ocean_rate), (stage_next, ocean_next))
            )
        ]
        run_copies(fresh)
        copies += fresh
    for copy in copies:
        copy.wait()


def compute(solid_state, material, ocean_state, ocean_medium, offset_x, offset_y):
    sizes = tuple(lax.axis_size(axis) for axis in ("gx", "gy", "gz"))
    span_x, span_y, span_z = sizes
    depth = solid_state.shape[1]
    levels, fine, width = ocean_state.shape[1:]
    pairs = levels // 2
    if solid_state.shape[2:] != (rows, lanes) or (fine, width) != (2 * rows, half):
        raise ValueError("tile shape")
    if depth % 4 or levels % 2 or span_z != 4 or span_x % 2 or span_y % 2 or span_y < 4:
        raise ValueError("sizes")
    f32 = jnp.float32
    vmem = pl.BlockSpec(memory_space=pltpu.VMEM)
    smem = pl.BlockSpec(memory_space=pltpu.SMEM)
    hbm = pl.BlockSpec(memory_space=pl.ANY)
    near = lambda x: pltpu.with_memory_space_constraint(x, pltpu.VMEM)
    tiles = lambda *n: pltpu.VMEM((*n, rows, lanes), f32)
    like = lambda a: jax.ShapeDtypeStruct(a.shape, f32)
    dma = pltpu.SemaphoreType.DMA
    material = near(material)
    x_rounds = pair_rounds(span_x)
    count_x = len(x_rounds)
    pack_tiles = (len(x_fields) * depth + len(ocean_x_fields) * pairs) // 4
    edge_tiles = out_edge_tiles(depth)
    layers = 2 * len(z_fields)
    solid, ocean, small, move_x, move_y = pl.pallas_call(
        stage_kernel,
        out_shape=[
            pltpu.VMEM(solid_state.shape, f32),
            pltpu.VMEM(ocean_state.shape, f32),
            pltpu.VMEM(ocean_medium.shape, f32),
            pltpu.VMEM((1, fine), jnp.int32),
            pltpu.VMEM((1, width), jnp.int32),
        ],
        in_specs=[hbm] * 5,
        out_specs=[vmem] * 5,
        scratch_shapes=[dma((5,))],
        name="stage",
    )(
        solid_state,
        ocean_state,
        ocean_medium,
        offset_x.reshape(1, fine),
        offset_y.reshape(1, width),
    )
    solid, ocean = near(solid), near(ocean)
    plane = solid_state[2, 0]
    planes = [lax.ppermute(plane, "gx", p) for p in x_rounds]
    sent_x = pl.pallas_call(
        pack_x_kernel,
        out_shape=[tiles(pack_tiles) for _ in x_rounds],
        in_specs=[vmem] * 2,
        out_specs=[vmem] * count_x,
        name="pack_x",
    )(solid, ocean)
    got_x = [near(lax.ppermute(m, "gx", p)) for m, p in zip(sent_x, x_rounds)]
    sent_y, sent_small, pressure = pl.pallas_call(
        pack_kernel,
        out_shape=[tiles(edge_tiles + 3), tiles(4), tiles(1)],
        in_specs=[vmem] * 2,
        out_specs=[vmem] * 3,
        name="pack",
    )(solid, ocean)
    pressure = near(pressure)
    ring = ("gy", "gz")
    places = [(y, z) for y in range(span_y) for z in range(span_z)]

    def over_ring(move):
        return [(y * span_z + z, y2 * span_z + z2)
                for y, z in places for y2, z2 in (move(y, z),)]

    even = over_ring(lambda y, z: (y, z ^ 1))
    inner = over_ring(
        lambda y, z: (y ^ 1, z) if z in (0, span_z - 1) else (y, z + 1 if z % 2 else z - 1)
    )
    ends = over_ring(lambda y, z: (y, span_z - 1 - z))
    rim = row_rims(planes)
    planes = [near(plane) for plane in planes]
    sent_y, sent_small = (m.at[m.shape[0] - 1, :2].set(rim) for m in (sent_y, sent_small))
    sent_even, sent_odd, medium, index = pl.pallas_call(
        functools.partial(pack_z_kernel, sizes),
        out_shape=[
            tiles(layers),
            tiles(layers + 2),
            tiles(2, pairs),
            pltpu.VMEM((4, rows, lanes), jnp.int32),
        ],
        in_specs=[vmem] * 5,
        out_specs=[vmem] * 4,
        name="pack_z",
    )(solid, near(sent_small), near(small), near(move_x), near(move_y))
    medium, index = near(medium), near(index)
    rounds_y = pair_rounds(span_y)
    got_ya = near(lax.ppermute(sent_y, "gy", rounds_y[0]))
    got_yb = near(lax.ppermute(sent_y, "gy", rounds_y[1]))
    got_y = (got_ya, got_yb)
    got_small = near(lax.ppermute(sent_small, ring, even))
    got_even = near(lax.ppermute(sent_even, ring, even))
    got_odd = near(lax.ppermute(sent_odd, ring, inner))

    ocean_next, ocean_rate, ocean_carry = pl.pallas_call(
        functools.partial(ocean_kernel, sizes),
        out_shape=[like(ocean_state), like(ocean_state), pltpu.VMEM((2, pairs, fine, lanes), f32)],
        in_specs=[vmem] * (2 + count_x),
        out_specs=[hbm, hbm, vmem],
        scratch_shapes=[
            pltpu.VMEM((2, levels, fine, width), f32),
            pltpu.VMEM((2, levels, fine, width), f32),
            pltpu.VMEM((count_x, pack_tiles, rows, lanes), f32),
            dma((16,)),
        ],
        name="ocean",
    )(ocean, medium, *got_x)

    sent_far = pl.pallas_call(
        functools.partial(relay_kernel, count_x),
        out_shape=tiles(4),
        in_specs=[vmem] * (5 + count_x),
        out_specs=vmem,
        name="relay",
    )(solid, pressure, got_small, *got_y, *planes)
    got_far = near(lax.ppermute(sent_far, ring, ends))

    solid_next, solid_rate, solid_carry = pl.pallas_call(
        functools.partial(solid_kernel, sizes),
        out_shape=[like(solid_state), like(solid_state), tiles(2)],
        in_specs=[vmem] * (6 + count_x),
        out_specs=[hbm, hbm, vmem],
        scratch_shapes=[
            pltpu.VMEM(solid_state.shape, f32),
            pltpu.VMEM(solid_state.shape, f32),
            pltpu.VMEM((count_x, pack_tiles, rows, lanes), f32),
            dma((2 * depth,)),
        ],
        name="solid",
    )(solid, material, got_even, got_odd, *got_y, *got_x)

    return pl.pallas_call(
        functools.partial(last_kernel, sizes),
        out_shape=[like(solid_state), like(solid_state), like(ocean_state), like(ocean_state)],
        in_specs=[vmem] * (12 + count_x) + [hbm] * 4,
        out_specs=[hbm] * 4,
        input_output_aliases={12 + count_x + i: i for i in range(4)},
        scratch_shapes=[
            pltpu.VMEM((2, levels, fine, width), f32),
            pltpu.VMEM((2, levels, fine, width), f32),
            tiles(1, 1),
            tiles(1, 1),
            dma((6,)),
        ],
        name="last",
    )(
        solid, ocean, medium, pressure, index, near(ocean_carry), near(solid_carry),
        got_small, got_odd, got_far, *got_y, *planes,
        solid_next, solid_rate, ocean_next, ocean_rate,
    )


def solution(mesh):
    in_specs = (
        P(None, "gz", "gx", "gy"),
        P(None, "gz", "gx", "gy"),
        P(None, None, "gx", ("gy", "gz")),
        P(),
        P("gx"),
        P(("gy", "gz")),
    )
    out_specs = (
        P(None, "gz", "gx", "gy"),
        P(None, "gz", "gx", "gy"),
        P(None, None, "gx", ("gy", "gz")),
        P(None, None, "gx", ("gy", "gz")),
    )
    return jax.shard_map(compute, mesh=mesh, in_specs=in_specs, out_specs=out_specs, check_vma=False)
```
